32 devices in a mesh: bal: 8 (over z, x), seq: 4 (over y, core).
Axes of the slice: x: 2, y: 2, z: 4, core: 2. Of those that a mesh axis runs over, the one named last changes fastest.
Arguments:
- tokens: bfloat16 [128, 64, 5120], P('bal', 'seq'), may hold values from -6 to 6
- w_qkv: bfloat16 [5120, 24, 384], P('bal', 'seq')
- q_gain: float32 [24, 128], P('seq')
- k_gain: float32 [24, 128], P('seq')
- modulation: float32 [8, 4, 2, 5120], P('bal'), may hold values from -3 to 3
- tile_owner: int32 [128], P('bal'), may hold values from 0 to 7, as said below
- clip_dims: int32 [8, 4, 3], P('bal'), may hold values from 0 to 4, as said below
Outputs:
- attn_out: bfloat16 [128, 64, 3072], P('bal', 'seq')
The draws below stay inside these ranges and needn't reach their ends.
Inputs may be any that keep to these rules, and one draw needn't show every extreme that they name: `tile_owner`: each owner is named by exactly 16 tiles. The 16 tiles of one bal index name any owner at most 2 times, and in every draw some owner exactly 2 times. `clip_dims`: for each owner the clips' products f h w add up to 16; entries after its last clip are 0; a clip spans at most 2 tile frames, 3 tile rows and 4 tile columns and has 4 tiles or more.
All inputs are finite; a program needn't handle non-finite values.
Results may differ from the reference program's by a relative error of at most 0.006.
Values may be sent and summed in bfloat16 or wider, within the bound.
No kernel may reach another device: no remote copies, remote signals or barrier semaphores. Data moves between devices by JAX's collectives and lax.ppermute only.
A program may use at most 128 MiB of HBM per device.

```python
import jax
import jax.numpy as jnp
import numpy as np
from jax import lax

D = 5120
HEADS = 24
HD = 128
TILE = 64
TILES_OWN = 16
MAXCLIPS = 4
TILES = 128
N_BAL = 8


def draw_w_qkv(key, part):
    key_query, key_key, key_value = jax.random.split(jax.random.fold_in(key, 13), 3)
    head_frac = jnp.arange(HEADS, dtype=jnp.float32) / max(HEADS - 1, 1)
    base_scale = D ** (-0.5)
    spread = (3.0 ** head_frac)[None, :, None] * base_scale
    query_part = jax.random.normal(key_query, (D, HEADS, HD), jnp.float32) * spread
    key_part = jax.random.normal(key_key, (D, HEADS, HD), jnp.float32) * spread
    value_part = jax.random.normal(key_value, (D, HEADS, HD), jnp.float32) * base_scale
    return jnp.concatenate([query_part, key_part, value_part], axis=2).astype(jnp.bfloat16)


def gain_table(key, salt):
    gain_key = jax.random.fold_in(key, salt)
    return jax.random.uniform(gain_key, (HEADS, HD), jnp.float32, 0.6, 1.6)


def draw_q_gain(key, part):
    return gain_table(key, 11)


def draw_k_gain(key, part):
    return gain_table(key, 12)


def draw_tile_owner(key, part):
    key_offset, key_source, key_owner, key_shuffle = jax.random.split(jax.random.fold_in(key, 21), 4)
    offsets_perm = jax.random.permutation(key_offset, N_BAL)
    source_perm = jax.random.permutation(key_source, N_BAL)
    owner_perm = jax.random.permutation(key_owner, N_BAL)
    distinct = min(N_BAL, TILES_OWN)
    offsets = offsets_perm[jnp.arange(TILES_OWN) % distinct]
    owners = owner_perm[(source_perm[:, None] + offsets[None, :]) % N_BAL]
    row_keys = jax.random.split(key_shuffle, N_BAL)
    owners = jax.vmap(lambda row_key, row_vals: jax.random.permutation(row_key, row_vals))(row_keys, owners)
    return owners.reshape(-1).astype(jnp.int32)


def draw_clip_dims(key, part):
    table = np.array([[[2, 2, 4], [0, 0, 0], [0, 0, 0], [0, 0, 0]], [[2, 2, 2], [2, 2, 2], [0, 0, 0], [0, 0, 0]], [[1, 3, 4], [1, 2, 2], [0, 0, 0], [0, 0, 0]], [[1, 2, 2], [1, 2, 2], [1, 2, 2], [1, 2, 2]]], dtype=np.int32)
    picks = jax.random.randint(jax.random.fold_in(key, 31), (N_BAL,), 0, 4)
    return jnp.asarray(table)[picks].astype(jnp.int32)


def levels(rng, extent, cuts, least, high):
    loudness, own = 1.0, jax.random.fold_in(rng, 6)
    for position, blocks in cuts:
        heights = jnp.exp(jax.random.uniform(jax.random.fold_in(own, position), (blocks,), jnp.float32, least / len(cuts), high / len(cuts)))
        loudness = loudness * jnp.repeat(heights, extent[position] // blocks).reshape([-1 if axis == position else 1 for axis in range(len(extent))])
    return loudness


def centred(own_key, dims, deviation, most, shards=(), kind=jnp.bfloat16):
    values = deviation * jax.random.normal(own_key, dims, jnp.float32)
    if shards:
        values = values * levels(own_key, dims, shards, -0.22, 0.18)
    return jnp.clip(values, -most, most).astype(kind)


def setup_inputs(seed: int = 0) -> dict:
    arg_keys = jax.random.split(jax.random.key(seed), 8)
    tokens = centred(arg_keys[0], (TILES, TILE, D), 1.0, 6.0, ((0, 8), (1, 4)))
    w_qkv = draw_w_qkv(jax.random.fold_in(arg_keys[7], 71), 0)
    q_gain = draw_q_gain(jax.random.fold_in(arg_keys[7], 71), 0)
    k_gain = draw_k_gain(jax.random.fold_in(arg_keys[7], 71), 0)
    modulation = centred(arg_keys[4], (N_BAL, MAXCLIPS, 2, D), 0.5, 3.0, ((0, 8),), jnp.float32)
    tile_owner = draw_tile_owner(jax.random.fold_in(arg_keys[7], 71), 0)
    clip_dims = draw_clip_dims(jax.random.fold_in(arg_keys[7], 71), 0)
    return dict(tokens=tokens, w_qkv=w_qkv, q_gain=q_gain, k_gain=k_gain, modulation=modulation, tile_owner=tile_owner, clip_dims=clip_dims)


eps_norm = 1e-06
score_fill = -1e+30

def tile_layout(clip_shape):
    frames_of = clip_shape[:, 0]
    rows_of = clip_shape[:, 1]
    cols_of = clip_shape[:, 2]
    clip_sizes = (frames_of * rows_of * cols_of).astype(jnp.int32)
    clip_ends = jnp.cumsum(clip_sizes).astype(jnp.int32)
    clip_starts = clip_ends - clip_sizes
    local_index = jnp.arange(TILES_OWN, dtype=jnp.int32)
    member = lax.optimization_barrier(jnp.sum((local_index[:, None] >= clip_ends[None, :]).astype(jnp.int32), axis=1)).astype(jnp.int32)
    onehot = member[:, None] == jnp.arange(clip_shape.shape[0], dtype=jnp.int32)[None, :]

    def select_clip(values):
        return lax.optimization_barrier(jnp.sum(jnp.where(onehot, values[None, :], 0), axis=1)).astype(jnp.int32)
    offset = local_index - select_clip(clip_starts)
    height = jnp.maximum(select_clip(rows_of), 1)
    width_tiles = jnp.maximum(select_clip(cols_of), 1)
    frame_index = offset // (height * width_tiles)
    row_index = offset // width_tiles % height
    column = offset % width_tiles

    def within_one(coords):
        return jnp.abs(coords[:, None] - coords[None, :]) <= 1
    tile_mask = (member[:, None] == member[None, :]) & within_one(frame_index) & within_one(row_index) & within_one(column)
    return (onehot, tile_mask)

def clip_rows(onehot, mod_table):
    picked = lax.optimization_barrier(jnp.sum(jnp.where(onehot[:, :, None, None], mod_table[None], 0.0), axis=1))
    return (picked[:, 0], picked[:, 1])

def modulate(pieces, shift_rows, scale_rows):
    values = pieces.astype(jnp.float32)
    center = lax.optimization_barrier(jnp.mean(values, axis=-1, keepdims=True))
    spread = lax.optimization_barrier(jnp.mean(jnp.square(values - center), axis=-1, keepdims=True))
    normal = (values - center) * lax.rsqrt(spread + eps_norm)
    return (normal * (1.0 + scale_rows[:, None, :]) + shift_rows[:, None, :]).astype(jnp.bfloat16)

def attend(q_block, key_rows, values, block_mask):
    scores = jnp.einsum('qhd,khd->hqk', q_block.astype(jnp.float32), key_rows.astype(jnp.float32)) * key_rows.shape[2] ** (-0.5)
    scores = jnp.where(block_mask[None], scores, score_fill)
    largest = lax.optimization_barrier(jnp.max(scores, axis=-1, keepdims=True))
    exp_scores = jnp.exp(scores - largest)
    totals = lax.optimization_barrier(jnp.sum(exp_scores, axis=-1, keepdims=True))
    weights = (exp_scores / totals).astype(jnp.bfloat16)
    return jnp.einsum('hqk,khd->qhd', weights.astype(jnp.float32), values.astype(jnp.float32))

def reference(tokens, w_qkv, q_gain, k_gain, modulation, tile_owner, clip_dims):
    owner_order = jnp.argsort(tile_owner, stable=True).astype(jnp.int32).reshape(N_BAL, TILES_OWN)
    flat_weight = w_qkv.reshape(D, -1)
    token_count = TILES_OWN * TILE

    def one_owner(inputs):
        indices, mod_table, clip_shape = inputs
        pieces = jnp.take(tokens, indices, axis=0)
        onehot, tile_mask = tile_layout(clip_shape)
        shift_rows, scale_rows = clip_rows(onehot, mod_table)
        normed = modulate(pieces, shift_rows, scale_rows).reshape(token_count, D)
        projected = jnp.dot(normed, flat_weight, preferred_element_type=jnp.float32).reshape(token_count, HEADS, 3, HD)
        query = projected[:, :, 0]
        keyed = projected[:, :, 1]
        valued = projected[:, :, 2].astype(jnp.bfloat16)
        features = HEADS * HD
        q_scale = lax.rsqrt(lax.optimization_barrier(jnp.sum(jnp.square(query), axis=(1, 2))) / features + eps_norm)
        k_scale = lax.rsqrt(lax.optimization_barrier(jnp.sum(jnp.square(keyed), axis=(1, 2))) / features + eps_norm)
        q_normed = (query * q_scale[:, None, None] * q_gain[None]).astype(jnp.bfloat16)
        k_normed = (keyed * k_scale[:, None, None] * k_gain[None]).astype(jnp.bfloat16)
        token_mask = jnp.repeat(jnp.repeat(tile_mask, TILE, axis=0), TILE, axis=1)
        block_rows = min(512, token_count)
        outputs = []
        for block_start in range(0, token_count, block_rows):
            outputs.append(attend(q_normed[block_start:block_start + block_rows], k_normed, valued, token_mask[block_start:block_start + block_rows]))
        attended = jnp.concatenate(outputs, axis=0).astype(jnp.bfloat16)
        return attended.reshape(TILES_OWN, TILE, HEADS * HD)
    owner_tiles = lax.map(one_owner, (owner_order, modulation, clip_dims))
    result = jnp.zeros((TILES, TILE, HEADS * HD), jnp.bfloat16)
    return result.at[owner_order.reshape(-1)].set(owner_tiles.reshape(TILES, TILE, HEADS * HD))
```

```python
import functools

import jax
import jax.numpy as jnp
from jax import lax
from jax.experimental import pallas as pl
from jax.experimental.pallas import tpu as pltpu
from jax.sharding import PartitionSpec as P

TILES_OWN = 16
AXES = ("bal", "seq")

eps_norm = 1e-06
score_fill = -1e30


def tile_layout(clip_shape):
    frames_of = clip_shape[:, 0]
    rows_of = clip_shape[:, 1]
    cols_of = clip_shape[:, 2]
    clip_sizes = frames_of * rows_of * cols_of
    clip_ends = jnp.cumsum(clip_sizes)
    clip_starts = clip_ends - clip_sizes
    local_index = jnp.arange(TILES_OWN, dtype=jnp.int32)
    member = jnp.sum((local_index[:, None] >= clip_ends[None, :]).astype(jnp.int32), axis=1)
    onehot = member[:, None] == jnp.arange(clip_shape.shape[0], dtype=jnp.int32)[None, :]

    def select_clip(values):
        return jnp.sum(jnp.where(onehot, values[None, :], 0), axis=1)

    offset = local_index - select_clip(clip_starts)
    height = jnp.maximum(select_clip(rows_of), 1)
    width_tiles = jnp.maximum(select_clip(cols_of), 1)
    frame_index = offset // (height * width_tiles)
    row_index = offset // width_tiles % height
    column = offset % width_tiles

    def within_one(coords):
        return jnp.abs(coords[:, None] - coords[None, :]) <= 1

    tile_mask = (
        (member[:, None] == member[None, :])
        & within_one(frame_index)
        & within_one(row_index)
        & within_one(column)
    )
    return (member.astype(jnp.int32), tile_mask)


def smem():
    return pl.BlockSpec(memory_space=pltpu.SMEM)


def vmem():
    return pl.BlockSpec(memory_space=pltpu.VMEM)


def pick_tiles(tokens, tile_owner, ids, groups, capacity):
    count = tokens.shape[0]

    def body(own_ref, ids_ref, tok_ref, *rest):
        outs, seen, index = rest[:groups], rest[groups], rest[groups + 1]
        for k in range(groups):
            seen[k] = 0
        for k in range(groups * capacity):
            index[k] = 0
        for i in range(count):
            k = lax.rem(own_ref[i] - ids_ref[0] + groups, groups)
            r = seen[k]
            seen[k] = r + 1
            index[k * capacity + r] = i
        for k in range(groups):
            for j in range(capacity):
                outs[k][j] = tok_ref[index[k * capacity + j]]

    shape = jax.ShapeDtypeStruct((capacity,) + tokens.shape[1:], tokens.dtype)
    return pl.pallas_call(
        body,
        out_shape=[shape] * groups,
        in_specs=[smem(), smem(), vmem()],
        out_specs=[vmem()] * groups,
        scratch_shapes=[
            pltpu.SMEM((groups,), jnp.int32),
            pltpu.SMEM((groups * capacity,), jnp.int32),
        ],
        name="pick_tiles",
    )(tile_owner, ids, tokens)


def norm_tiles(pieces, table, member, place, ids, groups):
    capacity, piece, width = pieces[0].shape
    tiles = TILES_OWN
    depth = width // groups

    def body(member_ref, place_ref, ids_ref, table_ref, *rest):
        ins, out_ref, held = rest[:groups], rest[groups], rest[groups + 1]
        for k in range(groups):
            source = lax.rem(ids_ref[1] - k + groups, groups)
            for j in range(capacity):
                held[place_ref[source * capacity + j]] = ins[k][j]

        def one(r, carry):
            values = held[r].astype(jnp.float32)
            center = jnp.mean(values, axis=-1, keepdims=True)
            values = values - center
            spread = jnp.mean(jnp.square(values), axis=-1, keepdims=True)
            values = values * lax.rsqrt(spread + eps_norm)
            rows = table_ref[member_ref[r]]
            done = (values * (1.0 + rows[1:2]) + rows[0:1]).astype(out_ref.dtype)
            at = pl.multiple_of(r * piece, piece)
            for g in range(groups):
                out_ref[g, pl.ds(at, piece), :] = done[:, g * depth : (g + 1) * depth]
            return carry

        lax.fori_loop(0, tiles, one, 0)

    return pl.pallas_call(
        body,
        out_shape=jax.ShapeDtypeStruct((groups, tiles * piece, depth), pieces[0].dtype),
        in_specs=[smem(), smem(), smem(), vmem()] + [vmem()] * groups,
        out_specs=vmem(),
        scratch_shapes=[pltpu.VMEM((tiles + 1, piece, width), pieces[0].dtype)],
        cost_estimate=pl.CostEstimate(
            flops=12 * tiles * piece * width,
            bytes_accessed=4 * tiles * piece * width,
            transcendentals=0,
        ),
        name="norm_tiles",
    )(member, place, ids, table, *pieces)


def project(xs, w_own, w_par, at, acc, sums):
    heads, depth, cols = w_own.shape
    n, (_, rows, _) = len(xs), xs[0].shape
    total = n * rows

    def body(at_ref, *refs):
        x_own, x_par = refs[:n], refs[n : 2 * n]
        wo, wp = refs[2 * n], refs[2 * n + 1]
        rest = refs[2 * n + 2 :]
        if acc is not None:
            acc_ref, rest = rest[0], rest[1:]
        out_ref = rest[0]
        for j in range(n):
            part = jnp.dot(x_own[j][0], wo[0], preferred_element_type=jnp.float32)
            part += jnp.dot(x_par[j][0], wp[0], preferred_element_type=jnp.float32)
            here = slice(j * rows, (j + 1) * rows)
            if acc is not None:
                part += acc_ref[0, here]
            out_ref[0, here] = part
            if sums:
                lane = lax.broadcasted_iota(jnp.int32, (8, cols), 1)
                row = lax.broadcasted_iota(jnp.int32, (8, cols), 0)
                picker = (lane // (cols // 2) == row).astype(jnp.float32)
                squares = lax.dot_general(
                    picker,
                    jnp.square(part),
                    (((1,), (1,)), ((), ())),
                    precision=lax.Precision.HIGHEST,
                    preferred_element_type=jnp.float32,
                )
                sums_ref = rest[1]

                @pl.when(pl.program_id(0) == 0)
                def _():
                    sums_ref[:, here] = squares

                @pl.when(pl.program_id(0) > 0)
                def _():
                    sums_ref[:, here] += squares

    x_block = (1, rows, depth)
    specs = [pl.BlockSpec(x_block, lambda h, a: (a[0], 0, 0))] * n
    specs += [pl.BlockSpec(x_block, lambda h, a: (a[1], 0, 0))] * n
    specs += [pl.BlockSpec((1, depth, cols), lambda h, a: (h, 0, 0))] * 2
    args = [*xs, *xs, w_own, w_par]
    acc_spec = pl.BlockSpec((1, total, cols), lambda h, a: (h, 0, 0))
    aliases = {}
    if acc is not None:
        aliases = {1 + len(args): 0}
        specs.append(acc_spec)
        args.append(acc)
    out_shape = [jax.ShapeDtypeStruct((heads, total, cols), jnp.float32)]
    out_specs = [acc_spec]
    if sums:
        out_shape.append(jax.ShapeDtypeStruct((8, total), jnp.float32))
        out_specs.append(pl.BlockSpec((8, total), lambda h, a: (0, 0)))
    return pl.pallas_call(
        body,
        out_shape=out_shape,
        grid_spec=pltpu.PrefetchScalarGridSpec(
            num_scalar_prefetch=1, grid=(heads,), in_specs=specs, out_specs=out_specs
        ),
        input_output_aliases=aliases,
        cost_estimate=pl.CostEstimate(
            flops=4 * total * depth * cols * heads,
            bytes_accessed=4 * (total + cols * heads) * depth + 8 * total * cols * heads,
            transcendentals=0,
        ),
        name="project",
    )(at, *args)


def soft_weights(qk, partial_sums, gains, mask, features):
    heads, total, cols = qk.shape
    dim = cols // 2
    rows = mask.shape[0]
    n = len(partial_sums)

    def body(*refs):
        q_ref, k_ref = refs[0], refs[1]
        sum_refs = refs[2 : 2 + n]
        qg_ref, kg_ref, mask_ref, out_ref, scales, keys = refs[2 + n :]
        head, block = pl.program_id(0), pl.program_id(1)

        @pl.when((head == 0) & (block == 0))
        def _():
            for p in range(n):
                whole = None
                for q in range(n):
                    there = (p // 2 - q // 2) % (n // 2) * 2 + (p % 2 ^ q % 2)
                    part = sum_refs[q][:, there * rows : (there + 1) * rows]
                    whole = part if whole is None else whole + part
                scales[p * rows : (p + 1) * rows] = jnp.transpose(lax.rsqrt(whole / features + eps_norm))

        @pl.when(block == 0)
        def _():
            keys[...] = (k_ref[0] * scales[:, 1:2] * kg_ref[pl.ds(head, 1), :]).astype(keys.dtype)

        at = pl.multiple_of(block * rows, rows)
        query = q_ref[0] * scales[pl.ds(at, rows), 0:1] * qg_ref[pl.ds(head, 1), :]
        scores = lax.dot_general(
            query.astype(keys.dtype),
            keys[...],
            (((1,), (1,)), ((), ())),
            preferred_element_type=jnp.float32,
        ) * dim ** (-0.5)
        scores = jnp.where(mask_ref[...] > 0.5, scores, score_fill)
        largest = jnp.max(scores, axis=-1, keepdims=True)
        powers = jnp.exp(scores - largest)
        share = 1.0 / jnp.sum(powers, axis=-1, keepdims=True)
        out_ref[0] = (powers * share).astype(out_ref.dtype)

    whole_sum = pl.BlockSpec((8, total), lambda h, b: (0, 0))
    gain = pl.BlockSpec((heads, dim), lambda h, b: (0, 0))
    return pl.pallas_call(
        body,
        out_shape=jax.ShapeDtypeStruct((heads, total, total), jnp.bfloat16),
        grid=(heads, total // rows),
        in_specs=[
            pl.BlockSpec((1, rows, dim), lambda h, b: (h, b, 0)),
            pl.BlockSpec((1, total, dim), lambda h, b: (h, 0, 1)),
        ]
        + [whole_sum] * n
        + [gain, gain, pl.BlockSpec(mask.shape, lambda h, b: (0, 0))],
        out_specs=pl.BlockSpec((1, rows, total), lambda h, b: (h, b, 0)),
        scratch_shapes=[pltpu.VMEM((total, 8), jnp.float32), pltpu.VMEM((total, dim), jnp.bfloat16)],
        cost_estimate=pl.CostEstimate(
            flops=(2 * dim + 8) * heads * total * total,
            bytes_accessed=heads * total * (2 * total + 4 * cols),
            transcendentals=heads * total * total,
        ),
        name="soft_weights",
    )(qk, qk, *partial_sums, *gains, mask)


def mix_values(weights, values, order, place, groups, capacity, piece):
    heads, total, dim = values.shape
    n = order.shape[0]
    rows = total // n

    full = groups * capacity == TILES_OWN

    def body(order_ref, place_ref, w_ref, v_ref, out_ref, held, *staged):
        @pl.when(pl.program_id(1) == 0)
        def _():
            held[...] = v_ref[0].astype(held.dtype)

        mixed = jnp.dot(w_ref[0], held[...], preferred_element_type=jnp.float32)
        if full:
            out_ref[:, 0] = mixed.astype(out_ref.dtype).reshape(groups, capacity * piece, dim)
            return
        staged[0][...] = mixed
        for slot in range(groups * capacity):
            tile = jnp.minimum(place_ref[slot], TILES_OWN - 1)
            rows_of = staged[0][pl.ds(pl.multiple_of(tile * piece, piece), piece), :]
            at = slot % capacity * piece
            out_ref[slot // capacity, 0, at : at + piece] = rows_of.astype(out_ref.dtype)

    return pl.pallas_call(
        body,
        out_shape=jax.ShapeDtypeStruct((groups, n, capacity * piece, heads * dim), jnp.bfloat16),
        grid_spec=pltpu.PrefetchScalarGridSpec(
            num_scalar_prefetch=2,
            grid=(heads, n),
            in_specs=[
                pl.BlockSpec((1, rows, total), lambda h, p, o, s: (h, p, 0)),
                pl.BlockSpec((1, total, dim), lambda h, p, o, s: (h, 0, 0)),
            ],
            out_specs=pl.BlockSpec((groups, 1, capacity * piece, dim), lambda h, p, o, s: (0, o[p], 0, h)),
            scratch_shapes=[pltpu.VMEM((total, dim), jnp.bfloat16)]
            + [pltpu.VMEM((rows, dim), jnp.float32)] * (not full),
        ),
        cost_estimate=pl.CostEstimate(
            flops=2 * heads * total * total * dim,
            bytes_accessed=heads * total * (2 * total + 6 * dim),
            transcendentals=0,
        ),
        name="mix_values",
    )(order, place, weights, values)


def place_tiles(returned, tile_owner, groups, n, capacity):
    _, rows, width = returned.shape
    piece = rows // capacity
    count = tile_owner.shape[0]

    def body(own_ref, in_ref, out_ref, seen):
        for k in range(groups):
            seen[k] = 0
        for i in range(count):
            owner = own_ref[i]
            rank = seen[owner]
            seen[owner] = rank + 1
            at = pl.multiple_of(rank * piece, piece)
            for g in range(n):
                source = (owner // 2 * 2 + g % 2) * n + g // 2 * 2 + lax.rem(owner, 2)
                out_ref[i, :, g * width : (g + 1) * width] = in_ref[source, pl.ds(at, piece), :]

    return pl.pallas_call(
        body,
        out_shape=jax.ShapeDtypeStruct((count, piece, n * width), returned.dtype),
        in_specs=[smem(), vmem()],
        out_specs=vmem(),
        scratch_shapes=[pltpu.SMEM((groups,), jnp.int32)],
        name="place_tiles",
    )(tile_owner, returned)


def transposed(tokens, w_qkv, q_gain, k_gain, modulation, tile_owner, clip_dims):
    groups, n = lax.axis_size("bal"), lax.axis_size("seq")
    planes, lines = groups // 2, n // 2
    owned_tiles, piece, width = tokens.shape
    capacity = owned_tiles // min(groups, owned_tiles)
    heads, dim = q_gain.shape
    features = heads * n * dim

    def send(value, to):
        pairs = []
        for b in range(groups):
            for s in range(n):
                z, x, y, c = to(b // 2, b % 2, s // 2, s % 2)
                pairs.append((b * n + s, (z * 2 + x) * n + y * 2 + c))
        return lax.ppermute(value, AXES, pairs)

    def swap(value):
        return send(value, lambda z, x, y, c: (z, c, y, x))

    def ring(value):
        return send(value, lambda z, x, y, c: ((z + 1) % planes, x, y, c))

    def other_core(value):
        return send(value, lambda z, x, y, c: (z, x, y, 1 - c))

    bal, seq = lax.axis_index("bal"), lax.axis_index("seq")
    z, x, y, c = bal // 2, bal % 2, seq // 2, seq % 2
    ids = jnp.stack([bal, z * 2 + c]).astype(jnp.int32)

    by_head = jnp.transpose(w_qkv, (1, 0, 2))
    qk_own = [swap(by_head[:, :, : 2 * dim])]
    v_first = by_head[:, :, 2 * dim :]

    outgoing = pick_tiles(tokens, tile_owner, ids, groups, capacity)

    def to_owner(k):
        def to(z, x, y, c):
            owner = (z * 2 + x + k) % groups
            return owner // 2, c, y, owner % 2

        return to

    arrived = [send(outgoing[k], to_owner(k)) for k in range(groups)]
    table = swap(modulation[0])
    clips = swap(clip_dims[0])
    gains = (swap(q_gain), swap(k_gain))
    member, tile_mask = tile_layout(clips)
    if groups * capacity == TILES_OWN:
        place = jnp.arange(TILES_OWN, dtype=jnp.int32)
    else:
        named = lax.all_gather(tile_owner, "bal", axis=0) == ids[1]
        live = jnp.arange(capacity)[None, :] < jnp.sum(named, axis=1, dtype=jnp.int32)[:, None]
        live = live.reshape(-1)
        place = jnp.where(live, jnp.cumsum(live.astype(jnp.int32)) - 1, TILES_OWN).astype(jnp.int32)
    normed = norm_tiles(arrived, table, member, place, ids, groups)

    xs, order = [], []
    for py in range(lines):
        for px in range(2):
            if py == 0 and px == 0:
                xs.append(normed)
            else:
                xs.append(send(normed, lambda z, x, y, c: (z, x ^ px, (y - py) % lines, c)))
            order.append((y + py) % lines * 2 + (x ^ px))
    order = jnp.stack(order).astype(jnp.int32)

    for step in range(1, planes):
        qk_own.append(ring(qk_own[-1]))
    v_first, _ = lax.optimization_barrier((v_first, qk_own[0]))
    v_own = [swap(v_first)]
    for step in range(1, planes):
        last = v_own[-1]
        if step == 1:
            last, _ = lax.optimization_barrier((last, qk_own[-2]))
        v_own.append(ring(last))

    at = [
        jnp.stack([(z - step) % planes * 2 + c, (z - step) % planes * 2 + 1 - c]).astype(jnp.int32)
        for step in range(planes)
    ]
    qk = None
    for step in range(planes):
        qk, *sums = project(xs, qk_own[step], other_core(qk_own[step]), at[step], qk, step == planes - 1)
    partial_sums = [sums[0]]
    for py in range(lines):
        for px in range(2):
            if py or px:
                partial_sums.append(send(sums[0], lambda z, x, y, c: (z, x ^ px, (y - py) % lines, c)))

    spread = jnp.repeat(jnp.repeat(tile_mask.astype(jnp.float32), piece, axis=0), piece, axis=1)
    mask = jnp.tile(spread, (1, n))
    weights = soft_weights(qk, partial_sums, gains, mask, features)

    values = None
    for step in range(planes):
        values, *_ = project(xs, v_own[step], other_core(v_own[step]), at[step], values, False)
    mixed = mix_values(weights, values, order, place, groups, capacity, piece)
    returned = lax.all_to_all(
        mixed.reshape(groups * n, capacity * piece, heads * dim), AXES, split_axis=0, concat_axis=0, tiled=True
    )
    return place_tiles(returned, tile_owner, groups, n, capacity)


def solution(mesh):
    return jax.shard_map(
        transposed,
        mesh=mesh,
        in_specs=(
            P("bal", "seq", None),
            P("bal", "seq", None),
            P("seq", None),
            P("seq", None),
            P("bal", None, None, None),
            P("bal"),
            P("bal", None, None),
        ),
        out_specs=P("bal", "seq", None),
        check_vma=False,
    )
```

```python
import functools

import jax
import jax.numpy as jnp
from jax import lax
from jax.experimental import pallas as pl
from jax.experimental.pallas import tpu as pltpu
from jax.sharding import PartitionSpec as P

TILES_OWN = 16
AXES = ("bal", "seq")

eps_norm = 1e-06
score_fill = -1e30


def tile_layout(clip_shape):
    frames_of = clip_shape[:, 0]
    rows_of = clip_shape[:, 1]
    cols_of = clip_shape[:, 2]
    clip_sizes = frames_of * rows_of * cols_of
    clip_ends = jnp.cumsum(clip_sizes)
    clip_starts = clip_ends - clip_sizes
    local_index = jnp.arange(TILES_OWN, dtype=jnp.int32)
    member = jnp.sum((local_index[:, None] >= clip_ends[None, :]).astype(jnp.int32), axis=1)
    onehot = member[:, None] == jnp.arange(clip_shape.shape[0], dtype=jnp.int32)[None, :]

    def select_clip(values):
        return jnp.sum(jnp.where(onehot, values[None, :], 0), axis=1)

    offset = local_index - select_clip(clip_starts)
    height = jnp.maximum(select_clip(rows_of), 1)
    width_tiles = jnp.maximum(select_clip(cols_of), 1)
    frame_index = offset // (height * width_tiles)
    row_index = offset // width_tiles % height
    column = offset % width_tiles

    def within_one(coords):
        return jnp.abs(coords[:, None] - coords[None, :]) <= 1

    tile_mask = (
        (member[:, None] == member[None, :])
        & within_one(frame_index)
        & within_one(row_index)
        & within_one(column)
    )
    return (member.astype(jnp.int32), tile_mask)


def smem():
    return pl.BlockSpec(memory_space=pltpu.SMEM)


def vmem():
    return pl.BlockSpec(memory_space=pltpu.VMEM)


def pick_tiles(tokens, tile_owner, ids, groups, capacity):
    count = tokens.shape[0]

    def body(own_ref, ids_ref, tok_ref, *rest):
        outs, seen, index = rest[:groups], rest[groups], rest[groups + 1]
        for k in range(groups):
            seen[k] = 0
        for k in range(groups * capacity):
            index[k] = 0
        for i in range(count):
            k = lax.rem(own_ref[i] - ids_ref[0] + groups, groups)
            r = seen[k]
            seen[k] = r + 1
            index[k * capacity + r] = i
        for k in range(groups):
            for j in range(capacity):
                outs[k][j] = tok_ref[index[k * capacity + j]]

    shape = jax.ShapeDtypeStruct((capacity,) + tokens.shape[1:], tokens.dtype)
    return pl.pallas_call(
        body,
        out_shape=[shape] * groups,
        in_specs=[smem(), smem(), vmem()],
        out_specs=[vmem()] * groups,
        scratch_shapes=[
            pltpu.SMEM((groups,), jnp.int32),
            pltpu.SMEM((groups * capacity,), jnp.int32),
        ],
        name="pick_tiles",
    )(tile_owner, ids, tokens)


def norm_tiles(pieces, table, member, place, ids, groups):
    capacity, piece, width = pieces[0].shape
    tiles = TILES_OWN
    depth = width // groups

    def body(member_ref, place_ref, ids_ref, table_ref, *rest):
        ins, out_ref, held = rest[:groups], rest[groups], rest[groups + 1]
        for k in range(groups):
            source = lax.rem(ids_ref[1] - k + groups, groups)
            for j in range(capacity):
                held[place_ref[source * capacity + j]] = ins[k][j]

        def one(r, carry):
            values = held[r].astype(jnp.float32)
            center = jnp.mean(values, axis=-1, keepdims=True)
            values = values - center
            spread = jnp.mean(jnp.square(values), axis=-1, keepdims=True)
            values = values * lax.rsqrt(spread + eps_norm)
            rows = table_ref[member_ref[r]]
            done = (values * (1.0 + rows[1:2]) + rows[0:1]).astype(out_ref.dtype)
            at = pl.multiple_of(r * piece, piece)
            for g in range(groups):
                out_ref[g, pl.ds(at, piece), :] = done[:, g * depth : (g + 1) * depth]
            return carry

        lax.fori_loop(0, tiles, one, 0)

    return pl.pallas_call(
        body,
        out_shape=jax.ShapeDtypeStruct((groups, tiles * piece, depth), pieces[0].dtype),
        in_specs=[smem(), smem(), smem(), vmem()] + [vmem()] * groups,
        out_specs=vmem(),
        scratch_shapes=[pltpu.VMEM((tiles + 1, piece, width), pieces[0].dtype)],
        cost_estimate=pl.CostEstimate(
            flops=12 * tiles * piece * width,
            bytes_accessed=4 * tiles * piece * width,
            transcendentals=0,
        ),
        name="norm_tiles",
    )(member, place, ids, table, *pieces)


def project(x, blocks, at, acc, sums):
    heads, depth, cols = blocks[0].shape
    _, total, _ = x.shape
    n = len(blocks)

    def body(at_ref, *refs):
        x_refs, w_refs, rest = refs[:n], refs[n : 2 * n], list(refs[2 * n :])
        acc_ref = rest.pop(0) if acc is not None else None
        out_ref = rest.pop(0)
        part = jnp.dot(x_refs[0][0], w_refs[0][0], preferred_element_type=jnp.float32)
        for j in range(1, n):
            part += jnp.dot(x_refs[j][0], w_refs[j][0], preferred_element_type=jnp.float32)
        if acc is not None:
            part += acc_ref[0]
        out_ref[0] = part
        if sums:
            sums_ref, squares = rest
            head = pl.program_id(0)

            @pl.when(head == 0)
            def _():
                squares[...] = jnp.square(part)

            @pl.when(head > 0)
            def _():
                squares[...] += jnp.square(part)

            @pl.when(head == heads - 1)
            def _():
                lane = lax.broadcasted_iota(jnp.int32, (8, cols), 1)
                row = lax.broadcasted_iota(jnp.int32, (8, cols), 0)
                sums_ref[...] = lax.dot_general(
                    (lane // (cols // 2) == row).astype(jnp.float32),
                    squares[...],
                    (((1,), (1,)), ((), ())),
                    precision=lax.Precision.HIGHEST,
                    preferred_element_type=jnp.float32,
                )

    specs = [pl.BlockSpec((1, total, depth), lambda h, a, j=j: (a[j], 0, 0)) for j in range(n)]
    specs += [pl.BlockSpec((1, depth, cols), lambda h, a: (h, 0, 0))] * n
    args = [x] * n + list(blocks)
    acc_spec = pl.BlockSpec((1, total, cols), lambda h, a: (h, 0, 0))
    aliases = {}
    if acc is not None:
        aliases = {1 + len(args): 0}
        specs.append(acc_spec)
        args.append(acc)
    out_shape = [jax.ShapeDtypeStruct((heads, total, cols), jnp.float32)]
    out_specs = [acc_spec]
    scratch = []
    if sums:
        out_shape.append(jax.ShapeDtypeStruct((8, total), jnp.float32))
        out_specs.append(pl.BlockSpec((8, total), lambda h, a: (0, 0)))
        scratch.append(pltpu.VMEM((total, cols), jnp.float32))
    return pl.pallas_call(
        body,
        out_shape=out_shape,
        grid_spec=pltpu.PrefetchScalarGridSpec(
            num_scalar_prefetch=1, grid=(heads,), in_specs=specs, out_specs=out_specs, scratch_shapes=scratch
        ),
        input_output_aliases=aliases,
        cost_estimate=pl.CostEstimate(
            flops=2 * n * total * depth * cols * heads,
            bytes_accessed=2 * n * (total + cols * heads) * depth + 8 * total * cols * heads,
            transcendentals=0,
        ),
        name="project",
    )(at, *args)


def soft_weights(qk, partial_sums, gains, mask, features):
    heads, total, cols = qk.shape
    dim = cols // 2
    rows = mask.shape[0]
    n = len(partial_sums)

    def body(*refs):
        q_ref, k_ref = refs[0], refs[1]
        sum_refs = refs[2 : 2 + n]
        qg_ref, kg_ref, mask_ref, out_ref, scales, keys = refs[2 + n :]
        head, block = pl.program_id(0), pl.program_id(1)

        @pl.when((head == 0) & (block == 0))
        def _():
            for p in range(n):
                whole = None
                for q in range(n):
                    there = (p // 2 - q // 2) % (n // 2) * 2 + (p % 2 ^ q % 2)
                    part = sum_refs[q][:, there * rows : (there + 1) * rows]
                    whole = part if whole is None else whole + part
                scales[p * rows : (p + 1) * rows] = jnp.transpose(lax.rsqrt(whole / features + eps_norm))

        @pl.when(block == 0)
        def _():
            keys[...] = (k_ref[0] * scales[:, 1:2] * kg_ref[pl.ds(head, 1), :]).astype(keys.dtype)

        at = pl.multiple_of(block * rows, rows)
        query = q_ref[0] * scales[pl.ds(at, rows), 0:1] * qg_ref[pl.ds(head, 1), :]
        scores = lax.dot_general(
            query.astype(keys.dtype),
            keys[...],
            (((1,), (1,)), ((), ())),
            preferred_element_type=jnp.float32,
        ) * dim ** (-0.5)
        scores = jnp.where(mask_ref[...] > 0.5, scores, score_fill)
        largest = jnp.max(scores, axis=-1, keepdims=True)
        powers = jnp.exp(scores - largest)
        share = 1.0 / jnp.sum(powers, axis=-1, keepdims=True)
        out_ref[0] = (powers * share).astype(out_ref.dtype)

    whole_sum = pl.BlockSpec((8, total), lambda h, b: (0, 0))
    gain = pl.BlockSpec((heads, dim), lambda h, b: (0, 0))
    return pl.pallas_call(
        body,
        out_shape=jax.ShapeDtypeStruct((heads, total, total), jnp.bfloat16),
        grid=(heads, total // rows),
        in_specs=[
            pl.BlockSpec((1, rows, dim), lambda h, b: (h, b, 0)),
            pl.BlockSpec((1, total, dim), lambda h, b: (h, 0, 1)),
        ]
        + [whole_sum] * n
        + [gain, gain, pl.BlockSpec(mask.shape, lambda h, b: (0, 0))],
        out_specs=pl.BlockSpec((1, rows, total), lambda h, b: (h, b, 0)),
        scratch_shapes=[pltpu.VMEM((total, 8), jnp.float32), pltpu.VMEM((total, dim), jnp.bfloat16)],
        cost_estimate=pl.CostEstimate(
            flops=(2 * dim + 8) * heads * total * total,
            bytes_accessed=heads * total * (2 * total + 4 * cols),
            transcendentals=heads * total * total,
        ),
        name="soft_weights",
    )(qk, qk, *partial_sums, *gains, mask)


def mix_values(weights, values, order, place, groups, capacity, piece):
    heads, total, _ = weights.shape
    packed, _, cols = values.shape
    dim = packed * cols // heads
    share = heads // packed
    n = order.shape[0]
    rows = total // n
    full = groups * capacity == TILES_OWN

    def body(order_ref, place_ref, w_ref, v_ref, out_ref, *staged):
        held = v_ref[0].astype(weights.dtype)
        mixed = jnp.dot(w_ref[0], held, preferred_element_type=jnp.float32)
        for p in range(n):
            block = mixed[p * rows : (p + 1) * rows]
            if full:
                out_ref[:, order_ref[p]] = block.astype(out_ref.dtype).reshape(groups, capacity * piece, dim)
                continue
            staged[0][...] = block
            for slot in range(groups * capacity):
                tile = jnp.minimum(place_ref[slot], TILES_OWN - 1)
                tile_rows = staged[0][pl.ds(pl.multiple_of(tile * piece, piece), piece), :]
                at = slot % capacity * piece
                out_ref[slot // capacity, order_ref[p], at : at + piece] = tile_rows.astype(out_ref.dtype)

    return pl.pallas_call(
        body,
        out_shape=jax.ShapeDtypeStruct((groups, n, capacity * piece, heads * dim), jnp.bfloat16),
        grid_spec=pltpu.PrefetchScalarGridSpec(
            num_scalar_prefetch=2,
            grid=(heads,),
            in_specs=[
                pl.BlockSpec((1, total, total), lambda h, o, s: (h, 0, 0)),
                pl.BlockSpec((1, total, dim), lambda h, o, s: (h // share, 0, h % share)),
            ],
            out_specs=pl.BlockSpec((groups, n, capacity * piece, dim), lambda h, o, s: (0, 0, 0, h)),
            scratch_shapes=[pltpu.VMEM((rows, dim), jnp.float32)] * (not full),
        ),
        cost_estimate=pl.CostEstimate(
            flops=2 * heads * total * total * dim,
            bytes_accessed=heads * total * (2 * total + 6 * dim),
            transcendentals=0,
        ),
        name="mix_values",
    )(order, place, weights, values)


def place_tiles(returned, tile_owner, groups, n, capacity):
    _, rows, width = returned.shape
    piece = rows // capacity
    count = tile_owner.shape[0]

    def body(own_ref, in_ref, out_ref, seen):
        for k in range(groups):
            seen[k] = 0
        for i in range(count):
            owner = own_ref[i]
            rank = seen[owner]
            seen[owner] = rank + 1
            at = pl.multiple_of(rank * piece, piece)
            for g in range(n):
                source = (owner // 2 * 2 + g % 2) * n + g // 2 * 2 + lax.rem(owner, 2)
                out_ref[i, :, g * width : (g + 1) * width] = in_ref[source, pl.ds(at, piece), :]

    return pl.pallas_call(
        body,
        out_shape=jax.ShapeDtypeStruct((count, piece, n * width), returned.dtype),
        in_specs=[smem(), vmem()],
        out_specs=vmem(),
        scratch_shapes=[pltpu.SMEM((groups,), jnp.int32)],
        name="place_tiles",
    )(tile_owner, returned)


def transposed(tokens, w_qkv, q_gain, k_gain, modulation, tile_owner, clip_dims):
    groups, n = lax.axis_size("bal"), lax.axis_size("seq")
    planes, lines = groups // 2, n // 2
    owned_tiles, piece, width = tokens.shape
    capacity = owned_tiles // min(groups, owned_tiles)
    heads, dim = q_gain.shape
    features = heads * n * dim

    def send(value, to):
        pairs = []
        for b in range(groups):
            for s in range(n):
                z, x, y, c = to(b // 2, b % 2, s // 2, s % 2)
                pairs.append((b * n + s, (z * 2 + x) * n + y * 2 + c))
        return lax.ppermute(value, AXES, pairs)

    def swap(value):
        return send(value, lambda z, x, y, c: (z, c, y, x))

    def ring(value):
        return send(value, lambda z, x, y, c: ((z + 1) % planes, x, y, c))

    def other_core(value):
        return send(value, lambda z, x, y, c: (z, x, y, 1 - c))

    bal, seq = lax.axis_index("bal"), lax.axis_index("seq")
    z, x, y, c = bal // 2, bal % 2, seq // 2, seq % 2
    ids = jnp.stack([bal, z * 2 + c]).astype(jnp.int32)

    outgoing = pick_tiles(tokens, tile_owner, ids, groups, capacity)

    by_head = jnp.transpose(w_qkv, (1, 0, 2))
    pair = 2 if heads % 2 == 0 else 1
    v_columns = by_head[:, :, 2 * dim :]
    v_columns = jnp.concatenate([v_columns[i::pair] for i in range(pair)], axis=2)
    qk_own = [swap(by_head[:, :, : 2 * dim])]

    def to_owner(k):
        def to(z, x, y, c):
            owner = (z * 2 + x + k) % groups
            return owner // 2, c, y, owner % 2

        return to

    arrived = [send(outgoing[k], to_owner(k)) for k in range(groups)]
    table = swap(modulation[0])
    clips = swap(clip_dims[0])
    gains = (swap(q_gain), swap(k_gain))
    member, tile_mask = tile_layout(clips)
    if groups * capacity == TILES_OWN:
        place = jnp.arange(TILES_OWN, dtype=jnp.int32)
    else:
        named = lax.all_gather(tile_owner, "bal", axis=0) == ids[1]
        live = jnp.arange(capacity)[None, :] < jnp.sum(named, axis=1, dtype=jnp.int32)[:, None]
        live = live.reshape(-1)
        place = jnp.where(live, jnp.cumsum(live.astype(jnp.int32)) - 1, TILES_OWN).astype(jnp.int32)
    normed = norm_tiles(arrived, table, member, place, ids, groups)

    def along_x(value):
        return send(value, lambda z, x, y, c: (z, x ^ 1, y, c))

    def along_y(value, py):
        return send(value, lambda z, x, y, c: (z, x, (y - py) % lines, c))

    across = along_x(normed)
    pieces = [normed, across]
    order = [y * 2 + x, y * 2 + (x ^ 1)]
    half = groups // 2
    for py in range(1, lines):
        beside = along_y(normed, py)
        corner = jnp.concatenate([along_x(beside[:half]), along_y(across[half:], py)], axis=0)
        pieces += [beside, corner]
        order += [(y + py) % lines * 2 + x, (y + py) % lines * 2 + (x ^ 1)]
    whole_x = jnp.concatenate(pieces, axis=1)
    order = jnp.stack(order).astype(jnp.int32)

    def after(value, *others):
        return lax.optimization_barrier((value, *others))[0]

    def blocks_of(own, steps):
        blocks, at = [], []
        for step in steps:
            blocks += [own[step], other_core(own[step])]
            at += [(z - step) % planes * 2 + c, (z - step) % planes * 2 + 1 - c]
        return blocks, jnp.stack(at).astype(jnp.int32)

    early, late = range(planes - 1), [planes - 1]
    qk_own[0] = after(qk_own[0], outgoing[0])
    for step in range(1, planes):
        qk_own.append(ring(qk_own[-1]))
    v_own = [swap(after(v_columns, outgoing[0]))]
    v_own.append(ring(after(v_own[0], qk_own[-2])))

    qk, *_ = project(whole_x, *blocks_of(qk_own, early), None, False)
    for step in range(2, planes - 1):
        v_own.append(ring(after(v_own[-1], qk)))
    qk, sums = project(whole_x, *blocks_of(qk_own, late), qk, True)
    v_own.append(ring(after(v_own[-1], sums)))
    partial_sums = [sums, along_x(sums)]
    for py in range(1, lines):
        partial_sums.append(along_y(sums, py))
        partial_sums.append(send(sums, lambda z, x, y, c: (z, x ^ 1, (y - py) % lines, c)))

    spread = jnp.repeat(jnp.repeat(tile_mask.astype(jnp.float32), piece, axis=0), piece, axis=1)
    mask = jnp.tile(spread, (1, n))
    weights = soft_weights(qk, partial_sums, gains, mask, features)

    blocks, at = blocks_of(v_own, early)
    blocks[0] = after(blocks[0], weights)
    values, *_ = project(whole_x, blocks, at, None, False)
    values, *_ = project(whole_x, *blocks_of(v_own, late), values, False)
    mixed = mix_values(weights, values, order, place, groups, capacity, piece)
    returned = lax.all_to_all(
        mixed.reshape(groups * n, capacity * piece, heads * dim), AXES, split_axis=0, concat_axis=0, tiled=True
    )
    return place_tiles(returned, tile_owner, groups, n, capacity)


def solution(mesh):
    return jax.shard_map(
        transposed,
        mesh=mesh,
        in_specs=(
            P("bal", "seq", None),
            P("bal", "seq", None),
            P("seq", None),
            P("seq", None),
            P("bal", None, None, None),
            P("bal"),
            P("bal", None, None),
        ),
        out_specs=P("bal", "seq", None),
        check_vma=False,
    )
```

```python
import jax
import jax.numpy as jnp
from jax import lax
from jax.experimental import pallas as pl
from jax.experimental.pallas import tpu as pltpu
from jax.sharding import PartitionSpec as P


TILES_OWN = 16
AXES = ("bal", "seq")

eps_norm = 1e-06
score_fill = -1e30


def tile_layout(clip_shape):
    frames_of = clip_shape[:, 0]
    rows_of = clip_shape[:, 1]
    cols_of = clip_shape[:, 2]
    clip_sizes = frames_of * rows_of * cols_of
    clip_ends = jnp.cumsum(clip_sizes)
    clip_starts = clip_ends - clip_sizes
    local_index = jnp.arange(TILES_OWN, dtype=jnp.int32)
    member = jnp.sum((local_index[:, None] >= clip_ends[None, :]).astype(jnp.int32), axis=1)
    onehot = member[:, None] == jnp.arange(clip_shape.shape[0], dtype=jnp.int32)[None, :]

    def select_clip(values):
        return jnp.sum(jnp.where(onehot, values[None, :], 0), axis=1)

    offset = local_index - select_clip(clip_starts)
    height = jnp.maximum(select_clip(rows_of), 1)
    width_tiles = jnp.maximum(select_clip(cols_of), 1)
    frame_index = offset // (height * width_tiles)
    row_index = offset // width_tiles % height
    column = offset % width_tiles

    def within_one(coords):
        return jnp.abs(coords[:, None] - coords[None, :]) <= 1

    tile_mask = (
        (member[:, None] == member[None, :])
        & within_one(frame_index)
        & within_one(row_index)
        & within_one(column)
    )
    return (member.astype(jnp.int32), tile_mask)


def smem():
    return pl.BlockSpec(memory_space=pltpu.SMEM)


def vmem():
    return pl.BlockSpec(memory_space=pltpu.VMEM)


def pick_tiles(tokens, tile_owner, ids, groups, capacity):
    count = tokens.shape[0]

    def body(own_ref, ids_ref, tok_ref, *rest):
        outs, seen, index = rest[:groups], rest[groups], rest[groups + 1]
        for k in range(groups):
            seen[k] = 0
        for k in range(groups * capacity):
            index[k] = 0
        for i in range(count):
            k = lax.rem(own_ref[i] - ids_ref[0] + groups, groups)
            r = seen[k]
            seen[k] = r + 1
            index[k * capacity + r] = i
        for k in range(groups):
            for j in range(capacity):
                outs[k][j] = tok_ref[index[k * capacity + j]]

    shape = jax.ShapeDtypeStruct((capacity,) + tokens.shape[1:], tokens.dtype)
    return pl.pallas_call(
        body,
        out_shape=[shape] * groups,
        in_specs=[smem(), smem(), vmem()],
        out_specs=[vmem()] * groups,
        scratch_shapes=[
            pltpu.SMEM((groups,), jnp.int32),
            pltpu.SMEM((groups * capacity,), jnp.int32),
        ],
        name="pick_tiles",
    )(tile_owner, ids, tokens)


def norm_tiles(pieces, table, member, place, ids, groups):
    capacity, piece, width = pieces[0].shape
    tiles = TILES_OWN
    depth = width // groups

    def body(member_ref, place_ref, ids_ref, table_ref, *rest):
        ins, out_ref, held = rest[:groups], rest[groups], rest[groups + 1]
        for k in range(groups):
            source = lax.rem(ids_ref[1] - k + groups, groups)
            for j in range(capacity):
                held[place_ref[source * capacity + j]] = ins[k][j]

        def one(r, carry):
            values = held[r].astype(jnp.float32)
            center = jnp.mean(values, axis=-1, keepdims=True)
            values = values - center
            spread = jnp.mean(jnp.square(values), axis=-1, keepdims=True)
            values = values * lax.rsqrt(spread + eps_norm)
            rows = table_ref[member_ref[r]]
            done = (values * (1.0 + rows[1:2]) + rows[0:1]).astype(out_ref.dtype)
            at = pl.multiple_of(r * piece, piece)
            for g in range(groups):
                out_ref[g, pl.ds(at, piece), :] = done[:, g * depth : (g + 1) * depth]
            return carry

        lax.fori_loop(0, tiles, one, 0)

    return pl.pallas_call(
        body,
        out_shape=jax.ShapeDtypeStruct((groups, tiles * piece, depth), pieces[0].dtype),
        in_specs=[smem(), smem(), smem(), vmem()] + [vmem()] * groups,
        out_specs=vmem(),
        scratch_shapes=[pltpu.VMEM((tiles + 1, piece, width), pieces[0].dtype)],
        cost_estimate=pl.CostEstimate(
            flops=12 * tiles * piece * width,
            bytes_accessed=4 * tiles * piece * width,
            transcendentals=0,
        ),
        name="norm_tiles",
    )(member, place, ids, table, *pieces)


def project(xs, blocks, at, acc, sums):
    heads, depth, cols = blocks[0].shape
    sizes = [x.shape[1] for x in xs]
    total, m, n = sum(sizes), len(xs), len(blocks)

    def body(at_ref, *refs):
        x_refs, w_refs, rest = refs[: m * n], refs[m * n : (m + 1) * n], list(refs[(m + 1) * n :])
        acc_ref = rest.pop(0) if acc is not None else None
        out_ref = rest.pop(0)
        left = [jnp.concatenate([x_refs[i * n + j][0] for j in range(n)], axis=1) for i in range(m)]
        right = jnp.concatenate([ref[0] for ref in w_refs], axis=0)
        part = jnp.dot(jnp.concatenate(left, axis=0), right, preferred_element_type=jnp.float32)
        if acc is not None:
            part += acc_ref[0]
        out_ref[0] = part
        if sums:
            sums_ref, squares = rest
            head = pl.program_id(0)

            @pl.when(head == 0)
            def _():
                squares[...] = jnp.square(part)

            @pl.when(head > 0)
            def _():
                squares[...] += jnp.square(part)

            @pl.when(head == heads - 1)
            def _():
                lane = lax.broadcasted_iota(jnp.int32, (8, cols), 1)
                row = lax.broadcasted_iota(jnp.int32, (8, cols), 0)
                sums_ref[...] = lax.dot_general(
                    (lane // (cols // 2) == row).astype(jnp.float32),
                    squares[...],
                    (((1,), (1,)), ((), ())),
                    precision=lax.Precision.HIGHEST,
                    preferred_element_type=jnp.float32,
                )

    specs = [pl.BlockSpec((1, size, depth), lambda h, a, j=j: (a[j], 0, 0)) for size in sizes for j in range(n)]
    specs += [pl.BlockSpec((1, depth, cols), lambda h, a: (h, 0, 0))] * n
    args = [x for x in xs for _ in range(n)] + list(blocks)
    acc_spec = pl.BlockSpec((1, total, cols), lambda h, a: (h, 0, 0))
    aliases = {}
    if acc is not None:
        aliases = {1 + len(args): 0}
        specs.append(acc_spec)
        args.append(acc)
    out_shape = [jax.ShapeDtypeStruct((heads, total, cols), jnp.float32)]
    out_specs = [acc_spec]
    scratch = []
    if sums:
        out_shape.append(jax.ShapeDtypeStruct((8, total), jnp.float32))
        out_specs.append(pl.BlockSpec((8, total), lambda h, a: (0, 0)))
        scratch.append(pltpu.VMEM((total, cols), jnp.float32))
    return pl.pallas_call(
        body,
        out_shape=out_shape,
        grid_spec=pltpu.PrefetchScalarGridSpec(
            num_scalar_prefetch=1, grid=(heads,), in_specs=specs, out_specs=out_specs, scratch_shapes=scratch
        ),
        input_output_aliases=aliases,
        cost_estimate=pl.CostEstimate(
            flops=2 * n * total * depth * cols * heads,
            bytes_accessed=2 * n * (total + cols * heads) * depth + 8 * total * cols * heads,
            transcendentals=0,
        ),
        name="project",
    )(at, *args)


def soft_weights(qk, partial_sums, gains, mask, features, first, count):
    heads, total, cols = qk.shape
    dim = cols // 2
    rows = mask.shape[0]
    n = len(partial_sums)

    def body(*refs):
        q_ref, k_ref = refs[0], refs[1]
        sum_refs = refs[2 : 2 + n]
        qg_ref, kg_ref, mask_ref, out_ref, scales, keys = refs[2 + n :]
        head, block = pl.program_id(0), pl.program_id(1)

        @pl.when((head == 0) & (block == 0))
        def _():
            for p in range(n):
                whole = None
                for q in range(n):
                    there = (p // 2 - q // 2) % (n // 2) * 2 + (p % 2 ^ q % 2)
                    part = sum_refs[q][:, there * rows : (there + 1) * rows]
                    whole = part if whole is None else whole + part
                scales[p * rows : (p + 1) * rows] = jnp.transpose(lax.rsqrt(whole / features + eps_norm))

        @pl.when(block == 0)
        def _():
            keys[...] = (k_ref[0] * scales[:, 1:2] * kg_ref[pl.ds(first + head, 1), :]).astype(keys.dtype)

        at = pl.multiple_of(block * rows, rows)
        query = q_ref[0] * scales[pl.ds(at, rows), 0:1] * qg_ref[pl.ds(first + head, 1), :]
        scores = lax.dot_general(
            query.astype(keys.dtype),
            keys[...],
            (((1,), (1,)), ((), ())),
            preferred_element_type=jnp.float32,
        ) * dim ** (-0.5)
        scores = jnp.where(mask_ref[...] > 0.5, scores, score_fill)
        largest = jnp.max(scores, axis=-1, keepdims=True)
        powers = jnp.exp(scores - largest)
        share = 1.0 / jnp.sum(powers, axis=-1, keepdims=True)
        out_ref[0] = (powers * share).astype(out_ref.dtype)

    whole_sum = pl.BlockSpec((8, total), lambda h, b: (0, 0))
    gain = pl.BlockSpec((heads, dim), lambda h, b: (0, 0))
    return pl.pallas_call(
        body,
        out_shape=jax.ShapeDtypeStruct((count, total, total), jnp.bfloat16),
        grid=(count, total // rows),
        in_specs=[
            pl.BlockSpec((1, rows, dim), lambda h, b: (first + h, b, 0)),
            pl.BlockSpec((1, total, dim), lambda h, b: (first + h, 0, 1)),
        ]
        + [whole_sum] * n
        + [gain, gain, pl.BlockSpec(mask.shape, lambda h, b: (0, 0))],
        out_specs=pl.BlockSpec((1, rows, total), lambda h, b: (h, b, 0)),
        scratch_shapes=[pltpu.VMEM((total, 8), jnp.float32), pltpu.VMEM((total, dim), jnp.bfloat16)],
        cost_estimate=pl.CostEstimate(
            flops=(2 * dim + 8) * count * total * total,
            bytes_accessed=count * total * (2 * total + 4 * cols),
            transcendentals=count * total * total,
        ),
        name="soft_weights",
    )(qk, qk, *partial_sums, *gains, mask)


def mix_values(weights, values, order, place, groups, capacity, piece):
    parts, (count, total, _) = len(weights), weights[0].shape
    heads = parts * count
    packed, _, cols = values.shape
    dim = packed * cols // heads
    share = heads // packed
    n = order.shape[0]
    rows = total // n
    full = groups * capacity == TILES_OWN

    def body(order_ref, place_ref, *refs):
        w_refs, (v_ref, out_ref, *staged) = refs[:parts], refs[parts:]
        for i in range(parts):

            @pl.when(pl.program_id(0) // count == i)
            def _(w_ref=w_refs[i]):
                one_head(order_ref, place_ref, w_ref, v_ref, out_ref, staged)

    def one_head(order_ref, place_ref, w_ref, v_ref, out_ref, staged):
        held = v_ref[0].astype(w_ref.dtype)
        mixed = jnp.dot(w_ref[0], held, preferred_element_type=jnp.float32)
        for p in range(n):
            block = mixed[p * rows : (p + 1) * rows]
            if full:
                out_ref[:, order_ref[p]] = block.astype(out_ref.dtype).reshape(groups, capacity * piece, dim)
                continue
            staged[0][...] = block
            for slot in range(groups * capacity):
                tile = jnp.minimum(place_ref[slot], TILES_OWN - 1)
                tile_rows = staged[0][pl.ds(pl.multiple_of(tile * piece, piece), piece), :]
                at = slot % capacity * piece
                out_ref[slot // capacity, order_ref[p], at : at + piece] = tile_rows.astype(out_ref.dtype)

    return pl.pallas_call(
        body,
        out_shape=jax.ShapeDtypeStruct((groups, n, capacity * piece, heads * dim), jnp.bfloat16),
        grid_spec=pltpu.PrefetchScalarGridSpec(
            num_scalar_prefetch=2,
            grid=(heads,),
            in_specs=[
                pl.BlockSpec((1, total, total), lambda h, o, s, i=i: (jnp.clip(h - i * count, 0, count - 1), 0, 0))
                for i in range(parts)
            ]
            + [
                pl.BlockSpec((1, total, dim), lambda h, o, s: (h // share, 0, h % share)),
            ],
            out_specs=pl.BlockSpec((groups, n, capacity * piece, dim), lambda h, o, s: (0, 0, 0, h)),
            scratch_shapes=[pltpu.VMEM((rows, dim), jnp.float32)] * (not full),
        ),
        cost_estimate=pl.CostEstimate(
            flops=2 * heads * total * total * dim,
            bytes_accessed=heads * total * (2 * total + 6 * dim),
            transcendentals=0,
        ),
        name="mix_values",
    )(order, place, *weights, values)


def place_tiles(returned, tile_owner, groups, n, capacity):
    _, rows, width = returned.shape
    piece = rows // capacity
    count = tile_owner.shape[0]

    def body(own_ref, in_ref, out_ref, seen):
        for k in range(groups):
            seen[k] = 0
        for i in range(count):
            owner = own_ref[i]
            rank = seen[owner]
            seen[owner] = rank + 1
            at = pl.multiple_of(rank * piece, piece)
            for g in range(n):
                source = (owner // 2 * 2 + g % 2) * n + g // 2 * 2 + lax.rem(owner, 2)
                out_ref[i, :, g * width : (g + 1) * width] = in_ref[source, pl.ds(at, piece), :]

    return pl.pallas_call(
        body,
        out_shape=jax.ShapeDtypeStruct((count, piece, n * width), returned.dtype),
        in_specs=[smem(), vmem()],
        out_specs=vmem(),
        scratch_shapes=[pltpu.SMEM((groups,), jnp.int32)],
        name="place_tiles",
    )(tile_owner, returned)


def transposed(tokens, w_qkv, q_gain, k_gain, modulation, tile_owner, clip_dims):
    groups, n = lax.axis_size("bal"), lax.axis_size("seq")
    planes, lines = groups // 2, n // 2
    owned_tiles, piece, _ = tokens.shape
    capacity = owned_tiles // min(groups, owned_tiles)
    heads, dim = q_gain.shape
    features = heads * n * dim

    def send(value, to):
        pairs = []
        for b in range(groups):
            for s in range(n):
                z, x, y, c = to(b // 2, b % 2, s // 2, s % 2)
                pairs.append((b * n + s, (z * 2 + x) * n + y * 2 + c))
        return lax.ppermute(value, AXES, pairs)

    def swap(value):
        return send(value, lambda z, x, y, c: (z, c, y, x))

    def ring(value):
        return send(value, lambda z, x, y, c: ((z + 1) % planes, x, y, c))

    def other_core(value):
        return send(value, lambda z, x, y, c: (z, x, y, 1 - c))

    bal, seq = lax.axis_index("bal"), lax.axis_index("seq")
    z, x, y, c = bal // 2, bal % 2, seq // 2, seq % 2
    ids = jnp.stack([bal, z * 2 + c]).astype(jnp.int32)

    outgoing = pick_tiles(tokens, tile_owner, ids, groups, capacity)

    by_head = jnp.transpose(w_qkv, (1, 0, 2))
    pair = 2 if heads % 2 == 0 else 1
    v_columns = by_head[:, :, 2 * dim :]
    v_columns = jnp.concatenate([v_columns[i::pair] for i in range(pair)], axis=2)
    qk_own = [swap(by_head[:, :, : 2 * dim])]

    def to_owner(k):
        def to(z, x, y, c):
            owner = (z * 2 + x + k) % groups
            return owner // 2, c, y, owner % 2

        return to

    arrived = []
    for k in range(groups):
        arrived.append(send(outgoing[k], to_owner(k)))
    table = swap(modulation[0])
    clips = swap(clip_dims[0])
    gains = (swap(q_gain), swap(k_gain))
    member, tile_mask = tile_layout(clips)
    if groups * capacity == TILES_OWN:
        place = jnp.arange(TILES_OWN, dtype=jnp.int32)
    else:
        named = lax.all_gather(tile_owner, "bal", axis=0) == ids[1]
        live = jnp.arange(capacity)[None, :] < jnp.sum(named, axis=1, dtype=jnp.int32)[:, None]
        live = live.reshape(-1)
        place = jnp.where(live, jnp.cumsum(live.astype(jnp.int32)) - 1, TILES_OWN).astype(jnp.int32)
    gated = jnp.maximum(lax.optimization_barrier(member), 0)
    normed = norm_tiles(arrived, table, gated, place, ids, groups)

    def along_x(value):
        return send(value, lambda z, x, y, c: (z, x ^ 1, y, c))

    def along_y(value, py):
        return send(value, lambda z, x, y, c: (z, x, (y - py) % lines, c))

    across = along_x(normed)
    pieces = [normed, across]
    order = [y * 2 + x, y * 2 + (x ^ 1)]
    half = normed.shape[1] // 2
    for py in range(1, lines):
        beside = along_y(normed, py)
        corner = [along_x(beside[:, :half]), along_y(across[:, half:], py)]
        pieces += [beside, *corner]
        order += [(y + py) % lines * 2 + x, (y + py) % lines * 2 + (x ^ 1)]
    order = jnp.stack(order).astype(jnp.int32)

    def after(value, *others):
        return lax.optimization_barrier((value, *others))[0]

    def start_planes(own):
        if planes == 4:
            two = send(own, lambda z, x, y, c: (z ^ 2, x, y, c))
            return [own, send(own, lambda z, x, y, c: (z ^ 1, x, y, c)), two]
        got = [own]
        for _ in range(planes - 2):
            got.append(ring(got[-1]))
        return got

    def end_planes(got, *earlier):
        if planes == 4:
            own, _, two = got
            return [send_some(after(own, two, *earlier), {1: 2, 2: 1}), send_some(after(two, *earlier), {1: 0, 2: 3})]
        return [ring(after(got[-1], *earlier))]

    def last_plane(ends, *earlier):
        return sum(ends[1:], after(ends[0], *earlier))

    def send_some(value, hops):
        pairs = []
        for b in range(groups):
            for s in range(n):
                if b // 2 in hops:
                    pairs.append((b * n + s, (hops[b // 2] * 2 + b % 2) * n + s))
        return lax.ppermute(value, AXES, pairs)

    def plane_at(step):
        return z ^ step if planes == 4 else (z - step) % planes

    def blocks_of(own, steps):
        blocks, at = [], []
        for step in steps:
            blocks += [own[step], other_core(own[step])]
            at += [plane_at(step) * 2 + c, plane_at(step) * 2 + 1 - c]
        return blocks, jnp.stack(at).astype(jnp.int32)

    early, late = range(planes - 1), [planes - 1]
    qk_own = start_planes(after(qk_own[0], outgoing[0]))
    v_first = swap(after(v_columns, outgoing[0]))
    qk_ends = end_planes(qk_own)
    v_own = start_planes(after(v_first, *pieces[-2:]))

    blocks, at = blocks_of(qk_own, early)
    qk, *_ = project(pieces, blocks, at, None, False)
    qk_own.append(last_plane(qk_ends, qk))
    qk, sums = project(pieces, *blocks_of(qk_own, late), qk, True)
    partial_sums = [sums, along_x(sums)]
    for py in range(1, lines):
        partial_sums.append(along_y(sums, py))
        partial_sums.append(send(sums, lambda z, x, y, c: (z, x ^ 1, (y - py) % lines, c)))

    spread = jnp.repeat(jnp.repeat(tile_mask.astype(jnp.float32), piece, axis=0), piece, axis=1)
    mask = jnp.tile(spread, (1, n))
    parts = 2 if heads % 2 == 0 else 1
    weights = []
    for i in range(parts):
        part = soft_weights(qk, partial_sums, gains, mask, features, i * heads // parts, heads // parts)
        weights.append(part)
        if i == 0:
            v_ends = end_planes(v_own, weights[0])
    blocks, at = blocks_of(v_own, early)
    blocks[0] = after(blocks[0], weights[-1])
    values, *_ = project(pieces, blocks, at, None, False)
    v_own.append(last_plane(v_ends, values))
    values, *_ = project(pieces, *blocks_of(v_own, late), values, False)
    mixed = mix_values(weights, values, order, place, groups, capacity, piece)
    returned = lax.all_to_all(
        mixed.reshape(groups * n, capacity * piece, heads * dim), AXES, split_axis=0, concat_axis=0, tiled=True
    )
    return place_tiles(returned, tile_owner, groups, n, capacity)


def solution(mesh):
    return jax.shard_map(
        transposed,
        mesh=mesh,
        in_specs=(
            P("bal", "seq", None),
            P("bal", "seq", None),
            P("seq", None),
            P("seq", None),
            P("bal", None, None, None),
            P("bal"),
            P("bal", None, None),
        ),
        out_specs=P("bal", "seq", None),
        check_vma=False,
    )
```

```python
import jax
import jax.numpy as jnp
from jax import lax
from jax.experimental import pallas as pl
from jax.experimental.pallas import tpu as pltpu
from jax.sharding import PartitionSpec as P


TILES_OWN = 16
AXES = ("bal", "seq")

eps_norm = 1e-06
score_fill = -1e30


def tile_layout(clip_shape):
    frames_of = clip_shape[:, 0]
    rows_of = clip_shape[:, 1]
    cols_of = clip_shape[:, 2]
    clip_sizes = frames_of * rows_of * cols_of
    clip_ends = jnp.cumsum(clip_sizes)
    clip_starts = clip_ends - clip_sizes
    local_index = jnp.arange(TILES_OWN, dtype=jnp.int32)
    member = jnp.sum((local_index[:, None] >= clip_ends[None, :]).astype(jnp.int32), axis=1)
    onehot = member[:, None] == jnp.arange(clip_shape.shape[0], dtype=jnp.int32)[None, :]

    def select_clip(values):
        return jnp.sum(jnp.where(onehot, values[None, :], 0), axis=1)

    offset = local_index - select_clip(clip_starts)
    height = jnp.maximum(select_clip(rows_of), 1)
    width_tiles = jnp.maximum(select_clip(cols_of), 1)
    frame_index = offset // (height * width_tiles)
    row_index = offset // width_tiles % height
    column = offset % width_tiles

    def within_one(coords):
        return jnp.abs(coords[:, None] - coords[None, :]) <= 1

    tile_mask = (
        (member[:, None] == member[None, :])
        & within_one(frame_index)
        & within_one(row_index)
        & within_one(column)
    )
    return (member.astype(jnp.int32), tile_mask)


def smem():
    return pl.BlockSpec(memory_space=pltpu.SMEM)


def vmem():
    return pl.BlockSpec(memory_space=pltpu.VMEM)


def pick_tiles(tokens, tile_owner, ids, groups, capacity):
    count = tokens.shape[0]

    def body(own_ref, ids_ref, tok_ref, *rest):
        outs, seen, index = rest[:groups], rest[groups], rest[groups + 1]
        for k in range(groups):
            seen[k] = 0
        for k in range(groups * capacity):
            index[k] = 0
        for i in range(count):
            k = lax.rem(own_ref[i] - ids_ref[0] + groups, groups)
            r = seen[k]
            seen[k] = r + 1
            index[k * capacity + r] = i
        for k in range(groups):
            for j in range(capacity):
                outs[k][j] = tok_ref[index[k * capacity + j]]

    shape = jax.ShapeDtypeStruct((capacity,) + tokens.shape[1:], tokens.dtype)
    return pl.pallas_call(
        body,
        out_shape=[shape] * groups,
        in_specs=[smem(), smem(), vmem()],
        out_specs=[vmem()] * groups,
        scratch_shapes=[
            pltpu.SMEM((groups,), jnp.int32),
            pltpu.SMEM((groups * capacity,), jnp.int32),
        ],
        name="pick_tiles",
    )(tile_owner, ids, tokens)


def norm_tiles(pieces, table, member, place, ids, groups):
    capacity, piece, width = pieces[0].shape
    tiles = TILES_OWN
    depth = width // groups

    def body(member_ref, place_ref, ids_ref, table_ref, *rest):
        ins, out_ref, held = rest[:groups], rest[groups], rest[groups + 1]
        for k in range(groups):
            source = lax.rem(ids_ref[1] - k + groups, groups)
            for j in range(capacity):
                held[place_ref[source * capacity + j]] = ins[k][j]

        def one(r, carry):
            values = held[r].astype(jnp.float32)
            center = jnp.mean(values, axis=-1, keepdims=True)
            values = values - center
            spread = jnp.mean(jnp.square(values), axis=-1, keepdims=True)
            values = values * lax.rsqrt(spread + eps_norm)
            rows = table_ref[member_ref[r]]
            done = (values * (1.0 + rows[1:2]) + rows[0:1]).astype(out_ref.dtype)
            at = pl.multiple_of(r * piece, piece)
            for g in range(groups):
                out_ref[g, pl.ds(at, piece), :] = done[:, g * depth : (g + 1) * depth]
            return carry

        lax.fori_loop(0, tiles, one, 0)

    return pl.pallas_call(
        body,
        out_shape=jax.ShapeDtypeStruct((groups, tiles * piece, depth), pieces[0].dtype),
        in_specs=[smem(), smem(), smem(), vmem()] + [vmem()] * groups,
        out_specs=vmem(),
        scratch_shapes=[pltpu.VMEM((tiles + 1, piece, width), pieces[0].dtype)],
        cost_estimate=pl.CostEstimate(
            flops=12 * tiles * piece * width,
            bytes_accessed=4 * tiles * piece * width,
            transcendentals=0,
        ),
        name="norm_tiles",
    )(member, place, ids, table, *pieces)


def project(xs, blocks, at, acc, sums):
    heads, depth, cols = blocks[0].shape
    sizes = [x.shape[1] for x in xs]
    total, m, n = sum(sizes), len(xs), len(blocks)

    def body(at_ref, *refs):
        x_refs, w_refs, rest = refs[: m * n], refs[m * n : (m + 1) * n], list(refs[(m + 1) * n :])
        acc_ref = rest.pop(0) if acc is not None else None
        out_ref = rest.pop(0)
        left = [jnp.concatenate([x_refs[i * n + j][0] for j in range(n)], axis=1) for i in range(m)]
        right = jnp.concatenate([ref[0] for ref in w_refs], axis=0)
        part = jnp.dot(jnp.concatenate(left, axis=0), right, preferred_element_type=jnp.float32)
        if acc is not None:
            part += acc_ref[0]
        out_ref[0] = part
        if sums:
            sums_ref, squares = rest
            head = pl.program_id(0)

            @pl.when(head == 0)
            def _():
                squares[...] = jnp.square(part)

            @pl.when(head > 0)
            def _():
                squares[...] += jnp.square(part)

            @pl.when(head == heads - 1)
            def _():
                lane = lax.broadcasted_iota(jnp.int32, (8, cols), 1)
                row = lax.broadcasted_iota(jnp.int32, (8, cols), 0)
                sums_ref[...] = lax.dot_general(
                    (lane // (cols // 2) == row).astype(jnp.float32),
                    squares[...],
                    (((1,), (1,)), ((), ())),
                    precision=lax.Precision.HIGHEST,
                    preferred_element_type=jnp.float32,
                )

    specs = [pl.BlockSpec((1, size, depth), lambda h, a, j=j: (a[j], 0, 0)) for size in sizes for j in range(n)]
    specs += [pl.BlockSpec((1, depth, cols), lambda h, a: (h, 0, 0))] * n
    args = [x for x in xs for _ in range(n)] + list(blocks)
    acc_spec = pl.BlockSpec((1, total, cols), lambda h, a: (h, 0, 0))
    aliases = {}
    if acc is not None:
        aliases = {1 + len(args): 0}
        specs.append(acc_spec)
        args.append(acc)
    out_shape = [jax.ShapeDtypeStruct((heads, total, cols), jnp.float32)]
    out_specs = [acc_spec]
    scratch = []
    if sums:
        out_shape.append(jax.ShapeDtypeStruct((8, total), jnp.float32))
        out_specs.append(pl.BlockSpec((8, total), lambda h, a: (0, 0)))
        scratch.append(pltpu.VMEM((total, cols), jnp.float32))
    return pl.pallas_call(
        body,
        out_shape=out_shape,
        grid_spec=pltpu.PrefetchScalarGridSpec(
            num_scalar_prefetch=1, grid=(heads,), in_specs=specs, out_specs=out_specs, scratch_shapes=scratch
        ),
        input_output_aliases=aliases,
        cost_estimate=pl.CostEstimate(
            flops=2 * n * total * depth * cols * heads,
            bytes_accessed=2 * n * (total + cols * heads) * depth + 8 * total * cols * heads,
            transcendentals=0,
        ),
        name="project",
    )(at, *args)


def soft_weights(qk, partial_sums, gains, mask, features, first, count):
    heads, total, cols = qk.shape
    dim = cols // 2
    rows = mask.shape[0]
    n = len(partial_sums)

    def body(*refs):
        q_ref, k_ref = refs[0], refs[1]
        sum_refs = refs[2 : 2 + n]
        qg_ref, kg_ref, mask_ref, out_ref, scales, keys = refs[2 + n :]
        head, block = pl.program_id(0), pl.program_id(1)

        @pl.when((head == 0) & (block == 0))
        def _():
            for p in range(n):
                whole = None
                for q in range(n):
                    there = (p // 2 - q // 2) % (n // 2) * 2 + (p % 2 ^ q % 2)
                    part = sum_refs[q][:, there * rows : (there + 1) * rows]
                    whole = part if whole is None else whole + part
                scales[p * rows : (p + 1) * rows] = jnp.transpose(lax.rsqrt(whole / features + eps_norm))

        @pl.when(block == 0)
        def _():
            keys[...] = (k_ref[0] * scales[:, 1:2] * kg_ref[pl.ds(first + head, 1), :]).astype(keys.dtype)

        at = pl.multiple_of(block * rows, rows)
        query = q_ref[0] * scales[pl.ds(at, rows), 0:1] * qg_ref[pl.ds(first + head, 1), :]
        scores = lax.dot_general(
            query.astype(keys.dtype),
            keys[...],
            (((1,), (1,)), ((), ())),
            preferred_element_type=jnp.float32,
        ) * dim ** (-0.5)
        scores = jnp.where(mask_ref[...] > 0.5, scores, score_fill)
        largest = jnp.max(scores, axis=-1, keepdims=True)
        powers = jnp.exp(scores - largest)
        share = 1.0 / jnp.sum(powers, axis=-1, keepdims=True)
        out_ref[0] = (powers * share).astype(out_ref.dtype)

    whole_sum = pl.BlockSpec((8, total), lambda h, b: (0, 0))
    gain = pl.BlockSpec((heads, dim), lambda h, b: (0, 0))
    return pl.pallas_call(
        body,
        out_shape=jax.ShapeDtypeStruct((count, total, total), jnp.bfloat16),
        grid=(count, total // rows),
        in_specs=[
            pl.BlockSpec((1, rows, dim), lambda h, b: (first + h, b, 0)),
            pl.BlockSpec((1, total, dim), lambda h, b: (first + h, 0, 1)),
        ]
        + [whole_sum] * n
        + [gain, gain, pl.BlockSpec(mask.shape, lambda h, b: (0, 0))],
        out_specs=pl.BlockSpec((1, rows, total), lambda h, b: (h, b, 0)),
        scratch_shapes=[pltpu.VMEM((total, 8), jnp.float32), pltpu.VMEM((total, dim), jnp.bfloat16)],
        cost_estimate=pl.CostEstimate(
            flops=(2 * dim + 8) * count * total * total,
            bytes_accessed=count * total * (2 * total + 4 * cols),
            transcendentals=count * total * total,
        ),
        name="soft_weights",
    )(qk, qk, *partial_sums, *gains, mask)


def mix_values(weights, values, order, place, groups, capacity, piece):
    parts, (count, total, _) = len(weights), weights[0].shape
    heads = parts * count
    packed, _, cols = values.shape
    dim = packed * cols // heads
    share = heads // packed
    n = order.shape[0]
    rows = total // n
    full = groups * capacity == TILES_OWN

    def body(order_ref, place_ref, *refs):
        w_refs, (v_ref, out_ref, *staged) = refs[:parts], refs[parts:]
        for i in range(parts):

            @pl.when(pl.program_id(0) // count == i)
            def _(w_ref=w_refs[i]):
                one_head(order_ref, place_ref, w_ref, v_ref, out_ref, staged)

    def one_head(order_ref, place_ref, w_ref, v_ref, out_ref, staged):
        held = v_ref[0].astype(w_ref.dtype)
        mixed = jnp.dot(w_ref[0], held, preferred_element_type=jnp.float32)
        for p in range(n):
            block = mixed[p * rows : (p + 1) * rows]
            if full:
                out_ref[:, order_ref[p]] = block.astype(out_ref.dtype).reshape(groups, capacity * piece, dim)
                continue
            staged[0][...] = block
            for slot in range(groups * capacity):
                tile = jnp.minimum(place_ref[slot], TILES_OWN - 1)
                tile_rows = staged[0][pl.ds(pl.multiple_of(tile * piece, piece), piece), :]
                at = slot % capacity * piece
                out_ref[slot // capacity, order_ref[p], at : at + piece] = tile_rows.astype(out_ref.dtype)

    return pl.pallas_call(
        body,
        out_shape=jax.ShapeDtypeStruct((groups, n, capacity * piece, heads * dim), jnp.bfloat16),
        grid_spec=pltpu.PrefetchScalarGridSpec(
            num_scalar_prefetch=2,
            grid=(heads,),
            in_specs=[
                pl.BlockSpec((1, total, total), lambda h, o, s, i=i: (jnp.clip(h - i * count, 0, count - 1), 0, 0))
                for i in range(parts)
            ]
            + [
                pl.BlockSpec((1, total, dim), lambda h, o, s: (h // share, 0, h % share)),
            ],
            out_specs=pl.BlockSpec((groups, n, capacity * piece, dim), lambda h, o, s: (0, 0, 0, h)),
            scratch_shapes=[pltpu.VMEM((rows, dim), jnp.float32)] * (not full),
        ),
        cost_estimate=pl.CostEstimate(
            flops=2 * heads * total * total * dim,
            bytes_accessed=heads * total * (2 * total + 6 * dim),
            transcendentals=0,
        ),
        name="mix_values",
    )(order, place, *weights, values)


def place_tiles(returned, tile_owner, groups, n, capacity):
    _, rows, width = returned.shape
    piece = rows // capacity
    count = tile_owner.shape[0]

    def body(own_ref, in_ref, out_ref, seen):
        for k in range(groups):
            seen[k] = 0
        for i in range(count):
            owner = own_ref[i]
            rank = seen[owner]
            seen[owner] = rank + 1
            at = pl.multiple_of(rank * piece, piece)
            for g in range(n):
                source = (owner // 2 * 2 + g % 2) * n + g // 2 * 2 + lax.rem(owner, 2)
                out_ref[i, :, g * width : (g + 1) * width] = in_ref[source, pl.ds(at, piece), :]

    return pl.pallas_call(
        body,
        out_shape=jax.ShapeDtypeStruct((count, piece, n * width), returned.dtype),
        in_specs=[smem(), vmem()],
        out_specs=vmem(),
        scratch_shapes=[pltpu.SMEM((groups,), jnp.int32)],
        name="place_tiles",
    )(tile_owner, returned)


def transposed(tokens, w_qkv, q_gain, k_gain, modulation, tile_owner, clip_dims):
    groups, n = lax.axis_size("bal"), lax.axis_size("seq")
    planes, lines = groups // 2, n // 2
    owned_tiles, piece, _ = tokens.shape
    capacity = owned_tiles // min(groups, owned_tiles)
    heads, dim = q_gain.shape
    features = heads * n * dim

    def send(value, to):
        pairs = []
        for b in range(groups):
            for s in range(n):
                z, x, y, c = to(b // 2, b % 2, s // 2, s % 2)
                pairs.append((b * n + s, (z * 2 + x) * n + y * 2 + c))
        return lax.ppermute(value, AXES, pairs)

    def swap(value):
        return send(value, lambda z, x, y, c: (z, c, y, x))

    def ring(value):
        return send(value, lambda z, x, y, c: ((z + 1) % planes, x, y, c))

    def other_core(value):
        return send(value, lambda z, x, y, c: (z, x, y, 1 - c))

    bal, seq = lax.axis_index("bal"), lax.axis_index("seq")
    z, x, y, c = bal // 2, bal % 2, seq // 2, seq % 2
    ids = jnp.stack([bal, z * 2 + c]).astype(jnp.int32)

    outgoing = pick_tiles(tokens, tile_owner, ids, groups, capacity)

    by_head = jnp.transpose(w_qkv, (1, 0, 2))
    pair = 2 if heads % 2 == 0 else 1
    v_columns = by_head[:, :, 2 * dim :]
    v_columns = jnp.concatenate([v_columns[i::pair] for i in range(pair)], axis=2)
    qk_own = [swap(by_head[:, :, : 2 * dim])]

    def to_owner(k):
        def to(z, x, y, c):
            owner = (z * 2 + x + k) % groups
            return owner // 2, c, y, owner % 2

        return to

    arrived = []
    for k in range(groups):
        arrived.append(send(outgoing[k], to_owner(k)))
    table = swap(modulation[0])
    clips = swap(clip_dims[0])
    gains = (swap(q_gain), swap(k_gain))
    member, tile_mask = tile_layout(clips)
    if groups * capacity == TILES_OWN:
        place = jnp.arange(TILES_OWN, dtype=jnp.int32)
    else:
        named = lax.all_gather(tile_owner, "bal", axis=0) == ids[1]
        live = jnp.arange(capacity)[None, :] < jnp.sum(named, axis=1, dtype=jnp.int32)[:, None]
        live = live.reshape(-1)
        place = jnp.where(live, jnp.cumsum(live.astype(jnp.int32)) - 1, TILES_OWN).astype(jnp.int32)
    gated = jnp.maximum(lax.optimization_barrier(member), 0)
    normed = norm_tiles(arrived, table, gated, place, ids, groups)

    def along_x(value):
        return send(value, lambda z, x, y, c: (z, x ^ 1, y, c))

    def along_y(value, py):
        return send(value, lambda z, x, y, c: (z, x, (y - py) % lines, c))

    across = along_x(normed)
    pieces = [normed, across]
    order = [y * 2 + x, y * 2 + (x ^ 1)]
    half = normed.shape[1] // 2
    for py in range(1, lines):
        beside = along_y(normed, py)
        corner = [along_x(beside[:, :half]), along_y(across[:, half:], py)]
        pieces += [beside, *corner]
        order += [(y + py) % lines * 2 + x, (y + py) % lines * 2 + (x ^ 1)]
    order = jnp.stack(order).astype(jnp.int32)

    def after(value, *others):
        return lax.optimization_barrier((value, *others))[0]

    def start_planes(own, *earlier):
        if planes == 4:
            one = send(own, lambda z, x, y, c: (z ^ 1, x, y, c))
            return [own, one, send(after(own, *earlier), lambda z, x, y, c: (z ^ 2, x, y, c))]
        got = [own]
        for _ in range(planes - 2):
            got.append(ring(got[-1]))
        return got

    def end_planes(got, *earlier):
        if planes == 4:
            own, _, two = got
            return [send_some(after(own, two, *earlier), {1: 2, 2: 1}), send_some(after(two, *earlier), {1: 0, 2: 3})]
        return [ring(after(got[-1], *earlier))]

    def last_plane(ends, *earlier):
        return sum(ends[1:], after(ends[0], *earlier))

    def send_some(value, hops):
        pairs = []
        for b in range(groups):
            for s in range(n):
                if b // 2 in hops:
                    pairs.append((b * n + s, (hops[b // 2] * 2 + b % 2) * n + s))
        return lax.ppermute(value, AXES, pairs)

    def plane_at(step):
        return z ^ step if planes == 4 else (z - step) % planes

    def blocks_of(own, steps):
        blocks, at = [], []
        for step in steps:
            blocks += [own[step], other_core(own[step])]
            at += [plane_at(step) * 2 + c, plane_at(step) * 2 + 1 - c]
        return blocks, jnp.stack(at).astype(jnp.int32)

    early, late = range(planes - 1), [planes - 1]
    qk_own = start_planes(after(qk_own[0], outgoing[0]), *arrived)
    v_first = swap(after(v_columns, outgoing[0]))
    qk_ends = end_planes(qk_own)
    v_own = start_planes(after(v_first, *pieces[-2:]))

    blocks, at = blocks_of(qk_own, early)
    qk, *_ = project(pieces, blocks, at, None, False)
    qk_own.append(last_plane(qk_ends, qk))
    qk, sums = project(pieces, *blocks_of(qk_own, late), qk, True)
    partial_sums = [sums, along_x(sums)]
    for py in range(1, lines):
        partial_sums.append(along_y(sums, py))
        partial_sums.append(send(sums, lambda z, x, y, c: (z, x ^ 1, (y - py) % lines, c)))

    spread = jnp.repeat(jnp.repeat(tile_mask.astype(jnp.float32), piece, axis=0), piece, axis=1)
    mask = jnp.tile(spread, (1, n))
    parts = 2 if heads % 2 == 0 else 1
    weights = []
    for i in range(parts):
        part = soft_weights(qk, partial_sums, gains, mask, features, i * heads // parts, heads // parts)
        weights.append(part)
        if i == 0:
            v_ends = end_planes(v_own, weights[0])
    blocks, at = blocks_of(v_own, early)
    blocks[0] = after(blocks[0], weights[-1])
    values, *_ = project(pieces, blocks, at, None, False)
    v_own.append(last_plane(v_ends, values))
    values, *_ = project(pieces, *blocks_of(v_own, late), values, False)
    mixed = mix_values(weights, values, order, place, groups, capacity, piece)
    returned = lax.all_to_all(
        mixed.reshape(groups * n, capacity * piece, heads * dim), AXES, split_axis=0, concat_axis=0, tiled=True
    )
    return place_tiles(returned, tile_owner, groups, n, capacity)


def solution(mesh):
    return jax.shard_map(
        transposed,
        mesh=mesh,
        in_specs=(
            P("bal", "seq", None),
            P("bal", "seq", None),
            P("seq", None),
            P("seq", None),
            P("bal", None, None, None),
            P("bal"),
            P("bal", None, None),
        ),
        out_specs=P("bal", "seq", None),
        check_vma=False,
    )
```

```python
import jax
import jax.numpy as jnp
from jax import lax
from jax.experimental import pallas as pl
from jax.experimental.pallas import tpu as pltpu
from jax.sharding import PartitionSpec as P


TILES_OWN = 16
AXES = ("bal", "seq")

eps_norm = 1e-06
log2_e = 1.4426950408889634
mask_bias = -3e38


def tile_layout(clip_shape):
    frames_of = clip_shape[:, 0]
    rows_of = clip_shape[:, 1]
    cols_of = clip_shape[:, 2]
    clip_sizes = frames_of * rows_of * cols_of
    clip_ends = jnp.cumsum(clip_sizes)
    clip_starts = clip_ends - clip_sizes
    local_index = jnp.arange(TILES_OWN, dtype=jnp.int32)
    member = jnp.sum((local_index[:, None] >= clip_ends[None, :]).astype(jnp.int32), axis=1)
    onehot = member[:, None] == jnp.arange(clip_shape.shape[0], dtype=jnp.int32)[None, :]

    def select_clip(values):
        return jnp.sum(jnp.where(onehot, values[None, :], 0), axis=1)

    offset = local_index - select_clip(clip_starts)
    height = jnp.maximum(select_clip(rows_of), 1)
    width_tiles = jnp.maximum(select_clip(cols_of), 1)
    frame_index = offset // (height * width_tiles)
    row_index = offset // width_tiles % height
    column = offset % width_tiles

    def within_one(coords):
        return jnp.abs(coords[:, None] - coords[None, :]) <= 1

    tile_mask = (
        (member[:, None] == member[None, :])
        & within_one(frame_index)
        & within_one(row_index)
        & within_one(column)
    )
    return (member.astype(jnp.int32), tile_mask)


def smem():
    return pl.BlockSpec(memory_space=pltpu.SMEM)


def vmem():
    return pl.BlockSpec(memory_space=pltpu.VMEM)


def pick_tiles(tokens, tile_owner, ids, groups, capacity):
    count = tokens.shape[0]

    def body(own_ref, ids_ref, tok_ref, *rest):
        outs, seen, index = rest[:groups], rest[groups], rest[groups + 1]
        for k in range(groups):
            seen[k] = 0
        for k in range(groups * capacity):
            index[k] = 0
        for i in range(count):
            k = lax.rem(own_ref[i] - ids_ref[0] + groups, groups)
            r = seen[k]
            seen[k] = r + 1
            index[k * capacity + r] = i
        for k in range(groups):
            for j in range(capacity):
                outs[k][j] = tok_ref[index[k * capacity + j]]

    shape = jax.ShapeDtypeStruct((capacity,) + tokens.shape[1:], tokens.dtype)
    return pl.pallas_call(
        body,
        out_shape=[shape] * groups,
        in_specs=[smem(), smem(), vmem()],
        out_specs=[vmem()] * groups,
        scratch_shapes=[
            pltpu.SMEM((groups,), jnp.int32),
            pltpu.SMEM((groups * capacity,), jnp.int32),
        ],
        name="pick_tiles",
    )(tile_owner, ids, tokens)


def norm_tiles(pieces, table, member, place, ids, groups):
    capacity, piece, width = pieces[0].shape
    tiles = TILES_OWN
    depth = width // groups

    def body(member_ref, place_ref, ids_ref, table_ref, *rest):
        ins, out_ref, held = rest[:groups], rest[groups], rest[groups + 1]
        for k in range(groups):
            source = lax.rem(ids_ref[1] - k + groups, groups)
            for j in range(capacity):
                held[place_ref[source * capacity + j]] = ins[k][j]

        def one(r, carry):
            values = held[r].astype(jnp.float32)
            center = jnp.mean(values, axis=-1, keepdims=True)
            values = values - center
            spread = jnp.mean(jnp.square(values), axis=-1, keepdims=True)
            values = values * lax.rsqrt(spread + eps_norm)
            rows = table_ref[member_ref[r]]
            done = (values * (1.0 + rows[1:2]) + rows[0:1]).astype(out_ref.dtype)
            at = pl.multiple_of(r * piece, piece)
            for g in range(groups):
                out_ref[g, pl.ds(at, piece), :] = done[:, g * depth : (g + 1) * depth]
            return carry

        lax.fori_loop(0, tiles, one, 0)

    return pl.pallas_call(
        body,
        out_shape=jax.ShapeDtypeStruct((groups, tiles * piece, depth), pieces[0].dtype),
        in_specs=[smem(), smem(), smem(), vmem()] + [vmem()] * groups,
        out_specs=vmem(),
        scratch_shapes=[pltpu.VMEM((tiles + 1, piece, width), pieces[0].dtype)],
        cost_estimate=pl.CostEstimate(
            flops=12 * tiles * piece * width,
            bytes_accessed=4 * tiles * piece * width,
            transcendentals=0,
        ),
        name="norm_tiles",
    )(member, place, ids, table, *pieces)


def project(xs, blocks, at, acc, sums):
    heads, depth, cols = blocks[0].shape
    sizes = [x.shape[1] for x in xs]
    total, m, n = sum(sizes), len(xs), len(blocks)

    def body(at_ref, *refs):
        x_refs, w_refs, rest = refs[: m * n], refs[m * n : (m + 1) * n], list(refs[(m + 1) * n :])
        acc_ref = rest.pop(0) if acc is not None else None
        out_ref = rest.pop(0)
        left = [jnp.concatenate([x_refs[i * n + j][0] for j in range(n)], axis=1) for i in range(m)]
        right = jnp.concatenate([ref[0] for ref in w_refs], axis=0)
        part = jnp.dot(jnp.concatenate(left, axis=0), right, preferred_element_type=jnp.float32)
        if acc is not None:
            part += acc_ref[0]
        out_ref[0] = part
        if sums:
            sums_ref, squares = rest
            head = pl.program_id(0)

            @pl.when(head == 0)
            def _():
                squares[...] = jnp.square(part)

            @pl.when(head > 0)
            def _():
                squares[...] += jnp.square(part)

            @pl.when(head == heads - 1)
            def _():
                lane = lax.broadcasted_iota(jnp.int32, (8, cols), 1)
                row = lax.broadcasted_iota(jnp.int32, (8, cols), 0)
                sums_ref[...] = lax.dot_general(
                    (lane // (cols // 2) == row).astype(jnp.float32),
                    squares[...],
                    (((1,), (1,)), ((), ())),
                    precision=lax.Precision.HIGHEST,
                    preferred_element_type=jnp.float32,
                )

    specs = [pl.BlockSpec((1, size, depth), lambda h, a, j=j: (a[j], 0, 0)) for size in sizes for j in range(n)]
    specs += [pl.BlockSpec((1, depth, cols), lambda h, a: (h, 0, 0))] * n
    args = [x for x in xs for _ in range(n)] + list(blocks)
    acc_spec = pl.BlockSpec((1, total, cols), lambda h, a: (h, 0, 0))
    aliases = {}
    if acc is not None:
        aliases = {1 + len(args): 0}
        specs.append(acc_spec)
        args.append(acc)
    out_shape = [jax.ShapeDtypeStruct((heads, total, cols), jnp.float32)]
    out_specs = [acc_spec]
    scratch = []
    if sums:
        out_shape.append(jax.ShapeDtypeStruct((8, total), jnp.float32))
        out_specs.append(pl.BlockSpec((8, total), lambda h, a: (0, 0)))
        scratch.append(pltpu.VMEM((total, cols), jnp.float32))
    return pl.pallas_call(
        body,
        out_shape=out_shape,
        grid_spec=pltpu.PrefetchScalarGridSpec(
            num_scalar_prefetch=1, grid=(heads,), in_specs=specs, out_specs=out_specs, scratch_shapes=scratch
        ),
        input_output_aliases=aliases,
        cost_estimate=pl.CostEstimate(
            flops=2 * n * total * depth * cols * heads,
            bytes_accessed=2 * n * (total + cols * heads) * depth + 8 * total * cols * heads,
            transcendentals=0,
        ),
        name="project",
    )(at, *args)


def soft_weights(qk, partial_sums, gains, bias, features, first, count):
    heads, total, cols = qk.shape
    dim = cols // 2
    n = len(partial_sums)
    rows = total // n
    extra = bias.shape[1]

    def body(*refs):
        q_ref, k_ref = refs[0], refs[1]
        sum_refs = refs[2 : 2 + n]
        qg_ref, kg_ref, bias_ref, out_ref, scales, keys = refs[2 + n :]
        head, block = pl.program_id(0), pl.program_id(1)

        @pl.when((head == 0) & (block == 0))
        def _():
            keys[:, dim:] = bias_ref[...]
            for p in range(n):
                whole = None
                for q in range(n):
                    there = (p // 2 - q // 2) % (n // 2) * 2 + (p % 2 ^ q % 2)
                    part = sum_refs[q][:, there * rows : (there + 1) * rows]
                    whole = part if whole is None else whole + part
                scales[p * rows : (p + 1) * rows] = jnp.transpose(lax.rsqrt(whole / features + eps_norm))

        @pl.when(block == 0)
        def _():
            keys[:, :dim] = (k_ref[0] * scales[:, 1:2] * kg_ref[pl.ds(first + head, 1), :]).astype(keys.dtype)

        at = pl.multiple_of(block * rows, rows)
        query = q_ref[0] * scales[pl.ds(at, rows), 0:1] * qg_ref[pl.ds(first + head, 1), :]
        lane = lax.broadcasted_iota(jnp.int32, (rows, extra), 1)
        row = lax.broadcasted_iota(jnp.int32, (rows, extra), 0)
        tile = (row // (rows // TILES_OWN) == lane).astype(keys.dtype)
        scores = lax.dot_general(
            jnp.concatenate([query.astype(keys.dtype), tile], axis=1),
            keys[...],
            (((1,), (1,)), ((), ())),
            preferred_element_type=jnp.float32,
        )
        largest = jnp.max(scores, axis=-1, keepdims=True)
        powers = jnp.exp2((scores - largest) * (dim ** (-0.5) * log2_e))
        share = 1.0 / jnp.sum(powers, axis=-1, keepdims=True)
        out_ref[0] = (powers * share).astype(out_ref.dtype)

    whole_sum = pl.BlockSpec((8, total), lambda h, b: (0, 0))
    gain = pl.BlockSpec((heads, dim), lambda h, b: (0, 0))
    return pl.pallas_call(
        body,
        out_shape=jax.ShapeDtypeStruct((count, total, total), jnp.bfloat16),
        grid=(count, total // rows),
        in_specs=[
            pl.BlockSpec((1, rows, dim), lambda h, b: (first + h, b, 0)),
            pl.BlockSpec((1, total, dim), lambda h, b: (first + h, 0, 1)),
        ]
        + [whole_sum] * n
        + [gain, gain, pl.BlockSpec(bias.shape, lambda h, b: (0, 0))],
        out_specs=pl.BlockSpec((1, rows, total), lambda h, b: (h, b, 0)),
        scratch_shapes=[pltpu.VMEM((total, 8), jnp.float32), pltpu.VMEM((total, dim + extra), jnp.bfloat16)],
        cost_estimate=pl.CostEstimate(
            flops=(2 * dim + 8) * count * total * total,
            bytes_accessed=count * total * (2 * total + 4 * cols),
            transcendentals=count * total * total,
        ),
        name="soft_weights",
    )(qk, qk, *partial_sums, *gains, bias)


def mix_values(weights, values, xs, blocks, at, order, place, groups, capacity, piece):
    parts, (count, total, _) = len(weights), weights[0].shape
    heads = parts * count
    packed, _, cols = values.shape
    depth = blocks[0].shape[1]
    dim = packed * cols // heads
    share = heads // packed
    n = order.shape[0]
    rows = total // n
    sizes = [x.shape[1] for x in xs]
    m, k = len(xs), len(blocks)
    full = groups * capacity == TILES_OWN

    def body(order_ref, place_ref, at_ref, *refs):
        weight_refs, x_refs, refs = refs[:parts], refs[parts : parts + m * k], refs[parts + m * k :]
        w_refs, (acc_ref, out_ref, held, *staged) = refs[:k], refs[k:]
        head = pl.program_id(0)

        @pl.when(head % share == 0)
        def _():
            left = [jnp.concatenate([x_refs[i * k + j][0] for j in range(k)], axis=1) for i in range(m)]
            right = jnp.concatenate([ref[0] for ref in w_refs], axis=0)
            done = acc_ref[0] + jnp.dot(jnp.concatenate(left, axis=0), right, preferred_element_type=jnp.float32)
            for i in range(share):
                held[i] = done[:, i * dim : (i + 1) * dim].astype(held.dtype)

        for i in range(parts):

            @pl.when(head // count == i)
            def _(weight_ref=weight_refs[i]):
                mixed = jnp.dot(weight_ref[0], held[head % share], preferred_element_type=jnp.float32)
                for p in range(n):
                    block = mixed[p * rows : (p + 1) * rows]
                    if full:
                        out_ref[:, order_ref[p]] = block.astype(out_ref.dtype).reshape(groups, capacity * piece, dim)
                        continue
                    staged[0][...] = block
                    for slot in range(groups * capacity):
                        tile = jnp.minimum(place_ref[slot], TILES_OWN - 1)
                        tile_rows = staged[0][pl.ds(pl.multiple_of(tile * piece, piece), piece), :]
                        to = slot % capacity * piece
                        out_ref[slot // capacity, order_ref[p], to : to + piece] = tile_rows.astype(out_ref.dtype)

    def weight_block(i):
        return pl.BlockSpec((1, total, total), lambda h, o, s, a: (jnp.clip(h - i * count, 0, count - 1), 0, 0))

    return pl.pallas_call(
        body,
        out_shape=jax.ShapeDtypeStruct((groups, n, capacity * piece, heads * dim), jnp.bfloat16),
        grid_spec=pltpu.PrefetchScalarGridSpec(
            num_scalar_prefetch=3,
            grid=(heads,),
            in_specs=[weight_block(i) for i in range(parts)]
            + [pl.BlockSpec((1, size, depth), lambda h, o, s, a, j=j: (a[j], 0, 0)) for size in sizes for j in range(k)]
            + [pl.BlockSpec((1, depth, cols), lambda h, o, s, a: (h // share, 0, 0))] * k
            + [pl.BlockSpec((1, total, cols), lambda h, o, s, a: (h // share, 0, 0))],
            out_specs=pl.BlockSpec((groups, n, capacity * piece, dim), lambda h, o, s, a: (0, 0, 0, h)),
            scratch_shapes=[pltpu.VMEM((share, total, dim), jnp.bfloat16)]
            + [pltpu.VMEM((rows, dim), jnp.float32)] * (not full),
        ),
        cost_estimate=pl.CostEstimate(
            flops=2 * heads * total * (total + k * depth) * dim,
            bytes_accessed=heads * total * (2 * total + 6 * dim),
            transcendentals=0,
        ),
        name="mix_values",
    )(order, place, at, *weights, *[x for x in xs for _ in range(k)], *blocks, values)


def place_tiles(returned, tile_owner, groups, n, capacity):
    _, rows, width = returned.shape
    piece = rows // capacity
    count = tile_owner.shape[0]

    def body(own_ref, in_ref, out_ref, seen):
        for k in range(groups):
            seen[k] = 0
        for i in range(count):
            owner = own_ref[i]
            rank = seen[owner]
            seen[owner] = rank + 1
            at = pl.multiple_of(rank * piece, piece)
            for g in range(n):
                source = (owner // 2 * 2 + g % 2) * n + g // 2 * 2 + lax.rem(owner, 2)
                out_ref[i, :, g * width : (g + 1) * width] = in_ref[source, pl.ds(at, piece), :]

    return pl.pallas_call(
        body,
        out_shape=jax.ShapeDtypeStruct((count, piece, n * width), returned.dtype),
        in_specs=[smem(), vmem()],
        out_specs=vmem(),
        scratch_shapes=[pltpu.SMEM((groups,), jnp.int32)],
        name="place_tiles",
    )(tile_owner, returned)


def transposed(tokens, w_qkv, q_gain, k_gain, modulation, tile_owner, clip_dims):
    groups, n = lax.axis_size("bal"), lax.axis_size("seq")
    planes, lines = groups // 2, n // 2
    owned_tiles, piece, _ = tokens.shape
    capacity = owned_tiles // min(groups, owned_tiles)
    heads, dim = q_gain.shape
    features = heads * n * dim

    def send(value, to):
        pairs = []
        for b in range(groups):
            for s in range(n):
                z, x, y, c = to(b // 2, b % 2, s // 2, s % 2)
                pairs.append((b * n + s, (z * 2 + x) * n + y * 2 + c))
        return lax.ppermute(value, AXES, pairs)

    def swap(value):
        return send(value, lambda z, x, y, c: (z, c, y, x))

    def ring(value):
        return send(value, lambda z, x, y, c: ((z + 1) % planes, x, y, c))

    def other_core(value):
        return send(value, lambda z, x, y, c: (z, x, y, 1 - c))

    bal, seq = lax.axis_index("bal"), lax.axis_index("seq")
    z, x, y, c = bal // 2, bal % 2, seq // 2, seq % 2
    ids = jnp.stack([bal, z * 2 + c]).astype(jnp.int32)

    outgoing = pick_tiles(tokens, tile_owner, ids, groups, capacity)

    by_head = jnp.transpose(w_qkv, (1, 0, 2))
    pair = 2 if heads % 2 == 0 else 1
    v_columns = by_head[:, :, 2 * dim :]
    v_columns = jnp.concatenate([v_columns[i::pair] for i in range(pair)], axis=2)
    qk_own = [swap(by_head[:, :, : 2 * dim])]

    def to_owner(k):
        def to(z, x, y, c):
            owner = (z * 2 + x + k) % groups
            return owner // 2, c, y, owner % 2

        return to

    arrived = []
    for k in range(groups):
        arrived.append(send(outgoing[k], to_owner(k)))
    table = swap(modulation[0])
    clips = swap(clip_dims[0])
    gains = (swap(q_gain), swap(k_gain))
    member, tile_mask = tile_layout(clips)
    if groups * capacity == TILES_OWN:
        place = jnp.arange(TILES_OWN, dtype=jnp.int32)
    else:
        named = lax.all_gather(tile_owner, "bal", axis=0) == ids[1]
        live = jnp.arange(capacity)[None, :] < jnp.sum(named, axis=1, dtype=jnp.int32)[:, None]
        live = live.reshape(-1)
        place = jnp.where(live, jnp.cumsum(live.astype(jnp.int32)) - 1, TILES_OWN).astype(jnp.int32)
    gated = jnp.maximum(lax.optimization_barrier(member), 0)
    normed = norm_tiles(arrived, table, gated, place, ids, groups)

    def along_x(value):
        return send(value, lambda z, x, y, c: (z, x ^ 1, y, c))

    def along_y(value, py):
        return send(value, lambda z, x, y, c: (z, x, (y - py) % lines, c))

    across = along_x(normed)
    pieces = [normed, across]
    order = [y * 2 + x, y * 2 + (x ^ 1)]
    half = normed.shape[1] // 2
    for py in range(1, lines):
        beside = along_y(normed, py)
        corner = [along_x(beside[:, :half]), along_y(across[:, half:], py)]
        pieces += [beside, *corner]
        order += [(y + py) % lines * 2 + x, (y + py) % lines * 2 + (x ^ 1)]
    order = jnp.stack(order).astype(jnp.int32)

    def after(value, *others):
        return lax.optimization_barrier((value, *others))[0]

    def start_planes(own, *earlier):
        if planes == 4:
            one = send(own, lambda z, x, y, c: (z ^ 1, x, y, c))
            return [own, one, send(after(own, *earlier), lambda z, x, y, c: (z ^ 2, x, y, c))]
        got = [own]
        for _ in range(planes - 2):
            got.append(ring(got[-1]))
        return got

    def end_planes(got, *earlier):
        if planes == 4:
            own, _, two = got
            return [send_some(after(own, two, *earlier), {1: 2, 2: 1}), send_some(after(two, *earlier), {1: 0, 2: 3})]
        return [ring(after(got[-1], *earlier))]

    def last_plane(ends, *earlier):
        return sum(ends[1:], after(ends[0], *earlier))

    def send_some(value, hops):
        pairs = []
        for b in range(groups):
            for s in range(n):
                if b // 2 in hops:
                    pairs.append((b * n + s, (hops[b // 2] * 2 + b % 2) * n + s))
        return lax.ppermute(value, AXES, pairs)

    def plane_at(step):
        return z ^ step if planes == 4 else (z - step) % planes

    def blocks_of(own, steps):
        blocks, at = [], []
        for step in steps:
            blocks += [own[step], other_core(own[step])]
            at += [plane_at(step) * 2 + c, plane_at(step) * 2 + 1 - c]
        return blocks, jnp.stack(at).astype(jnp.int32)

    early, late = range(planes - 1), [planes - 1]
    qk_own = start_planes(after(qk_own[0], outgoing[0]), *arrived)
    v_first = swap(after(v_columns, outgoing[0]))
    qk_ends = end_planes(qk_own)
    blocks, at = blocks_of(qk_own, early)
    qk, *_ = project(pieces, blocks, at, None, False)
    v_own = start_planes(after(v_first, *pieces[-2:]), *qk_ends)
    qk_own.append(last_plane(qk_ends, qk))
    blocks, at = blocks_of(qk_own, late)
    qk, sums = project(pieces, blocks, at, qk, True)
    partial_sums = [sums, along_x(sums)]
    for py in range(1, lines):
        partial_sums.append(along_y(sums, py))
        partial_sums.append(send(sums, lambda z, x, y, c: (z, x ^ 1, (y - py) % lines, c)))

    bias = jnp.where(tile_mask.T, 0.0, mask_bias).astype(jnp.bfloat16)
    bias = jnp.pad(bias, ((0, 0), (0, dim - TILES_OWN)))
    bias = jnp.tile(jnp.repeat(bias, piece, axis=0), (n, 1))
    parts = 2 if heads % 2 == 0 else 1
    weights = []
    for i in range(parts):
        part = soft_weights(qk, partial_sums, gains, bias, features, i * heads // parts, heads // parts)
        weights.append(part)
        if i == 0:
            v_ends = end_planes(v_own, weights[0])
    blocks, at = blocks_of(v_own, early)
    blocks[0] = after(blocks[0], weights[-1])
    values, *_ = project(pieces, blocks, at, None, False)
    v_own.append(last_plane(v_ends, values))
    blocks, at = blocks_of(v_own, late)
    mixed = mix_values(weights, values, pieces, blocks, at, order, place, groups, capacity, piece)
    returned = lax.all_to_all(
        mixed.reshape(groups * n, capacity * piece, heads * dim), AXES, split_axis=0, concat_axis=0, tiled=True
    )
    return place_tiles(returned, tile_owner, groups, n, capacity)


def solution(mesh):
    return jax.shard_map(
        transposed,
        mesh=mesh,
        in_specs=(
            P("bal", "seq", None),
            P("bal", "seq", None),
            P("seq", None),
            P("seq", None),
            P("bal", None, None, None),
            P("bal"),
            P("bal", None, None),
        ),
        out_specs=P("bal", "seq", None),
        check_vma=False,
    )
```

```python
import jax
import jax.numpy as jnp
from jax import lax
from jax.experimental import pallas as pl
from jax.experimental.pallas import tpu as pltpu
from jax.sharding import PartitionSpec as P


TILES_OWN = 16
AXES = ("bal", "seq")

eps_norm = 1e-06
log2_e = 1.4426950408889634
mask_bias = -3e38


def tile_layout(clip_shape):
    frames_of = clip_shape[:, 0]
    rows_of = clip_shape[:, 1]
    cols_of = clip_shape[:, 2]
    clip_sizes = frames_of * rows_of * cols_of
    clip_ends = jnp.cumsum(clip_sizes)
    clip_starts = clip_ends - clip_sizes
    local_index = jnp.arange(TILES_OWN, dtype=jnp.int32)
    member = jnp.sum((local_index[:, None] >= clip_ends[None, :]).astype(jnp.int32), axis=1)
    onehot = member[:, None] == jnp.arange(clip_shape.shape[0], dtype=jnp.int32)[None, :]

    def select_clip(values):
        return jnp.sum(jnp.where(onehot, values[None, :], 0), axis=1)

    offset = local_index - select_clip(clip_starts)
    height = jnp.maximum(select_clip(rows_of), 1)
    width_tiles = jnp.maximum(select_clip(cols_of), 1)
    frame_index = offset // (height * width_tiles)
    row_index = offset // width_tiles % height
    column = offset % width_tiles

    def within_one(coords):
        return jnp.abs(coords[:, None] - coords[None, :]) <= 1

    tile_mask = (
        (member[:, None] == member[None, :])
        & within_one(frame_index)
        & within_one(row_index)
        & within_one(column)
    )
    return (member.astype(jnp.int32), tile_mask)


def smem():
    return pl.BlockSpec(memory_space=pltpu.SMEM)


def vmem():
    return pl.BlockSpec(memory_space=pltpu.VMEM)


def pick_tiles(tokens, tile_owner, ids, groups, capacity):
    count = tokens.shape[0]

    def body(own_ref, ids_ref, tok_ref, *rest):
        outs, seen, index = rest[:groups], rest[groups], rest[groups + 1]
        for k in range(groups):
            seen[k] = 0
        for k in range(groups * capacity):
            index[k] = 0
        for i in range(count):
            k = lax.rem(own_ref[i] - ids_ref[0] + groups, groups)
            r = seen[k]
            seen[k] = r + 1
            index[k * capacity + r] = i
        for k in range(groups):
            for j in range(capacity):
                outs[k][j] = tok_ref[index[k * capacity + j]]

    shape = jax.ShapeDtypeStruct((capacity,) + tokens.shape[1:], tokens.dtype)
    return pl.pallas_call(
        body,
        out_shape=[shape] * groups,
        in_specs=[smem(), smem(), vmem()],
        out_specs=[vmem()] * groups,
        scratch_shapes=[
            pltpu.SMEM((groups,), jnp.int32),
            pltpu.SMEM((groups * capacity,), jnp.int32),
        ],
        name="pick_tiles",
    )(tile_owner, ids, tokens)


def norm_tiles(pieces, table, member, place, ids, groups):
    capacity, piece, width = pieces[0].shape
    tiles = TILES_OWN
    depth = width // groups

    def body(member_ref, place_ref, ids_ref, table_ref, *rest):
        ins, out_ref, held = rest[:groups], rest[groups], rest[groups + 1]
        for k in range(groups):
            source = lax.rem(ids_ref[1] - k + groups, groups)
            for j in range(capacity):
                held[place_ref[source * capacity + j]] = ins[k][j]

        def one(r, carry):
            values = held[r].astype(jnp.float32)
            center = jnp.mean(values, axis=-1, keepdims=True)
            values = values - center
            spread = jnp.mean(jnp.square(values), axis=-1, keepdims=True)
            values = values * lax.rsqrt(spread + eps_norm)
            rows = table_ref[member_ref[r]]
            done = (values * (1.0 + rows[1:2]) + rows[0:1]).astype(out_ref.dtype)
            at = pl.multiple_of(r * piece, piece)
            for g in range(groups):
                out_ref[g, pl.ds(at, piece), :] = done[:, g * depth : (g + 1) * depth]
            return carry

        lax.fori_loop(0, tiles, one, 0)

    return pl.pallas_call(
        body,
        out_shape=jax.ShapeDtypeStruct((groups, tiles * piece, depth), pieces[0].dtype),
        in_specs=[smem(), smem(), smem(), vmem()] + [vmem()] * groups,
        out_specs=vmem(),
        scratch_shapes=[pltpu.VMEM((tiles + 1, piece, width), pieces[0].dtype)],
        cost_estimate=pl.CostEstimate(
            flops=12 * tiles * piece * width,
            bytes_accessed=4 * tiles * piece * width,
            transcendentals=0,
        ),
        name="norm_tiles",
    )(member, place, ids, table, *pieces)


def project(xs, blocks, at, acc, sums):
    heads, depth, cols = blocks[0].shape
    sizes = [x.shape[1] for x in xs]
    total, m, n = sum(sizes), len(xs), len(blocks)

    def body(at_ref, *refs):
        x_refs, w_refs, rest = refs[: m * n], refs[m * n : (m + 1) * n], list(refs[(m + 1) * n :])
        acc_ref = rest.pop(0) if acc is not None else None
        out_ref = rest.pop(0)
        left = [jnp.concatenate([x_refs[i * n + j][0] for j in range(n)], axis=1) for i in range(m)]
        right = jnp.concatenate([ref[0] for ref in w_refs], axis=0)
        part = jnp.dot(jnp.concatenate(left, axis=0), right, preferred_element_type=jnp.float32)
        if acc is not None:
            part += acc_ref[0]
        out_ref[0] = part
        if sums:
            sums_ref, squares = rest
            head = pl.program_id(0)

            @pl.when(head == 0)
            def _():
                squares[...] = jnp.square(part)

            @pl.when(head > 0)
            def _():
                squares[...] += jnp.square(part)

            @pl.when(head == heads - 1)
            def _():
                lane = lax.broadcasted_iota(jnp.int32, (8, cols), 1)
                row = lax.broadcasted_iota(jnp.int32, (8, cols), 0)
                sums_ref[...] = lax.dot_general(
                    (lane // (cols // 2) == row).astype(jnp.float32),
                    squares[...],
                    (((1,), (1,)), ((), ())),
                    precision=lax.Precision.HIGHEST,
                    preferred_element_type=jnp.float32,
                )

    specs = [pl.BlockSpec((1, size, depth), lambda h, a, j=j: (a[j], 0, 0)) for size in sizes for j in range(n)]
    specs += [pl.BlockSpec((1, depth, cols), lambda h, a: (h, 0, 0))] * n
    args = [x for x in xs for _ in range(n)] + list(blocks)
    acc_spec = pl.BlockSpec((1, total, cols), lambda h, a: (h, 0, 0))
    aliases = {}
    if acc is not None:
        aliases = {1 + len(args): 0}
        specs.append(acc_spec)
        args.append(acc)
    out_shape = [jax.ShapeDtypeStruct((heads, total, cols), jnp.float32)]
    out_specs = [acc_spec]
    scratch = []
    if sums:
        out_shape.append(jax.ShapeDtypeStruct((8, total), jnp.float32))
        out_specs.append(pl.BlockSpec((8, total), lambda h, a: (0, 0)))
        scratch.append(pltpu.VMEM((total, cols), jnp.float32))
    return pl.pallas_call(
        body,
        out_shape=out_shape,
        grid_spec=pltpu.PrefetchScalarGridSpec(
            num_scalar_prefetch=1, grid=(heads,), in_specs=specs, out_specs=out_specs, scratch_shapes=scratch
        ),
        input_output_aliases=aliases,
        cost_estimate=pl.CostEstimate(
            flops=2 * n * total * depth * cols * heads,
            bytes_accessed=2 * n * (total + cols * heads) * depth + 8 * total * cols * heads,
            transcendentals=0,
        ),
        name="project",
    )(at, *args)


def soft_weights(qk, partial_sums, gains, bias, features, first, count):
    heads, total, cols = qk.shape
    dim = cols // 2
    n = len(partial_sums)
    rows = total // n
    extra = bias.shape[1]

    def body(*refs):
        q_ref, k_ref = refs[0], refs[1]
        sum_refs = refs[2 : 2 + n]
        qg_ref, kg_ref, bias_ref, out_ref, scales, keys = refs[2 + n :]
        head = pl.program_id(0)

        @pl.when(head == 0)
        def _():
            keys[:, dim:] = bias_ref[...]
            for p in range(n):
                whole = None
                for q in range(n):
                    there = (p // 2 - q // 2) % (n // 2) * 2 + (p % 2 ^ q % 2)
                    part = sum_refs[q][:, there * rows : (there + 1) * rows]
                    whole = part if whole is None else whole + part
                scales[p * rows : (p + 1) * rows] = jnp.transpose(lax.rsqrt(whole / features + eps_norm))

        keys[:, :dim] = (k_ref[0] * scales[:, 1:2] * kg_ref[pl.ds(first + head, 1), :]).astype(keys.dtype)
        lane = lax.broadcasted_iota(jnp.int32, (rows, extra), 1)
        row = lax.broadcasted_iota(jnp.int32, (rows, extra), 0)
        tile = (row // (rows // TILES_OWN) == lane).astype(keys.dtype)
        for p in range(n):
            here = slice(p * rows, (p + 1) * rows)
            query = q_ref[0, here] * scales[here, 0:1] * qg_ref[pl.ds(first + head, 1), :]
            scores = lax.dot_general(
                jnp.concatenate([query.astype(keys.dtype), tile], axis=1),
                keys[...],
                (((1,), (1,)), ((), ())),
                preferred_element_type=jnp.float32,
            )
            largest = jnp.max(scores, axis=-1, keepdims=True)
            powers = jnp.exp2((scores - largest) * (dim ** (-0.5) * log2_e))
            share = 1.0 / jnp.sum(powers, axis=-1, keepdims=True)
            out_ref[0, here] = (powers * share).astype(out_ref.dtype)

    whole_sum = pl.BlockSpec((8, total), lambda h: (0, 0))
    gain = pl.BlockSpec((heads, dim), lambda h: (0, 0))
    return pl.pallas_call(
        body,
        out_shape=jax.ShapeDtypeStruct((count, total, total), jnp.bfloat16),
        grid=(count,),
        in_specs=[
            pl.BlockSpec((1, total, dim), lambda h: (first + h, 0, 0)),
            pl.BlockSpec((1, total, dim), lambda h: (first + h, 0, 1)),
        ]
        + [whole_sum] * n
        + [gain, gain, pl.BlockSpec(bias.shape, lambda h: (0, 0))],
        out_specs=pl.BlockSpec((1, total, total), lambda h: (h, 0, 0)),
        scratch_shapes=[pltpu.VMEM((total, 8), jnp.float32), pltpu.VMEM((total, dim + extra), jnp.bfloat16)],
        cost_estimate=pl.CostEstimate(
            flops=(2 * dim + 8) * count * total * total,
            bytes_accessed=count * total * (2 * total + 4 * cols),
            transcendentals=count * total * total,
        ),
        name="soft_weights",
    )(qk, qk, *partial_sums, *gains, bias)


def mix_values(weights, values, xs, blocks, at, order, place, groups, capacity, piece):
    parts, (count, total, _) = len(weights), weights[0].shape
    heads = parts * count
    packed, _, cols = values.shape
    depth = blocks[0].shape[1]
    dim = packed * cols // heads
    share = heads // packed
    n = order.shape[0]
    rows = total // n
    sizes = [x.shape[1] for x in xs]
    m, k = len(xs), len(blocks)
    full = groups * capacity == TILES_OWN

    def body(order_ref, place_ref, at_ref, *refs):
        weight_refs, x_refs, refs = refs[:parts], refs[parts : parts + m * k], refs[parts + m * k :]
        w_refs, (acc_ref, out_ref, held, *staged) = refs[:k], refs[k:]
        head = pl.program_id(0)

        @pl.when(head % share == 0)
        def _():
            left = [jnp.concatenate([x_refs[i * k + j][0] for j in range(k)], axis=1) for i in range(m)]
            right = jnp.concatenate([ref[0] for ref in w_refs], axis=0)
            done = acc_ref[0] + jnp.dot(jnp.concatenate(left, axis=0), right, preferred_element_type=jnp.float32)
            for i in range(share):
                held[i] = done[:, i * dim : (i + 1) * dim].astype(held.dtype)

        for i in range(parts):

            @pl.when(head // count == i)
            def _(weight_ref=weight_refs[i]):
                mixed = jnp.dot(weight_ref[0], held[head % share], preferred_element_type=jnp.float32)
                for p in range(n):
                    block = mixed[p * rows : (p + 1) * rows]
                    if full:
                        out_ref[:, order_ref[p]] = block.astype(out_ref.dtype).reshape(groups, capacity * piece, dim)
                        continue
                    staged[0][...] = block
                    for slot in range(groups * capacity):
                        tile = jnp.minimum(place_ref[slot], TILES_OWN - 1)
                        tile_rows = staged[0][pl.ds(pl.multiple_of(tile * piece, piece), piece), :]
                        to = slot % capacity * piece
                        out_ref[slot // capacity, order_ref[p], to : to + piece] = tile_rows.astype(out_ref.dtype)

    def weight_block(i):
        return pl.BlockSpec((1, total, total), lambda h, o, s, a: (jnp.clip(h - i * count, 0, count - 1), 0, 0))

    return pl.pallas_call(
        body,
        out_shape=jax.ShapeDtypeStruct((groups, n, capacity * piece, heads * dim), jnp.bfloat16),
        grid_spec=pltpu.PrefetchScalarGridSpec(
            num_scalar_prefetch=3,
            grid=(heads,),
            in_specs=[weight_block(i) for i in range(parts)]
            + [pl.BlockSpec((1, size, depth), lambda h, o, s, a, j=j: (a[j], 0, 0)) for size in sizes for j in range(k)]
            + [pl.BlockSpec((1, depth, cols), lambda h, o, s, a: (h // share, 0, 0))] * k
            + [pl.BlockSpec((1, total, cols), lambda h, o, s, a: (h // share, 0, 0))],
            out_specs=pl.BlockSpec((groups, n, capacity * piece, dim), lambda h, o, s, a: (0, 0, 0, h)),
            scratch_shapes=[pltpu.VMEM((share, total, dim), jnp.bfloat16)]
            + [pltpu.VMEM((rows, dim), jnp.float32)] * (not full),
        ),
        cost_estimate=pl.CostEstimate(
            flops=2 * heads * total * (total + k * depth) * dim,
            bytes_accessed=heads * total * (2 * total + 6 * dim),
            transcendentals=0,
        ),
        name="mix_values",
    )(order, place, at, *weights, *[x for x in xs for _ in range(k)], *blocks, values)


def place_tiles(returned, tile_owner, groups, n, capacity):
    _, rows, width = returned.shape
    piece = rows // capacity
    count = tile_owner.shape[0]

    def body(own_ref, in_ref, out_ref, seen):
        for k in range(groups):
            seen[k] = 0
        for i in range(count):
            owner = own_ref[i]
            rank = seen[owner]
            seen[owner] = rank + 1
            at = pl.multiple_of(rank * piece, piece)
            for g in range(n):
                source = (owner // 2 * 2 + g % 2) * n + g // 2 * 2 + lax.rem(owner, 2)
                out_ref[i, :, g * width : (g + 1) * width] = in_ref[source, pl.ds(at, piece), :]

    return pl.pallas_call(
        body,
        out_shape=jax.ShapeDtypeStruct((count, piece, n * width), returned.dtype),
        in_specs=[smem(), vmem()],
        out_specs=vmem(),
        scratch_shapes=[pltpu.SMEM((groups,), jnp.int32)],
        name="place_tiles",
    )(tile_owner, returned)


def transposed(tokens, w_qkv, q_gain, k_gain, modulation, tile_owner, clip_dims):
    groups, n = lax.axis_size("bal"), lax.axis_size("seq")
    planes, lines = groups // 2, n // 2
    owned_tiles, piece, _ = tokens.shape
    capacity = owned_tiles // min(groups, owned_tiles)
    heads, dim = q_gain.shape
    features = heads * n * dim

    def send(value, to):
        pairs = []
        for b in range(groups):
            for s in range(n):
                z, x, y, c = to(b // 2, b % 2, s // 2, s % 2)
                pairs.append((b * n + s, (z * 2 + x) * n + y * 2 + c))
        return lax.ppermute(value, AXES, pairs)

    def swap(value):
        return send(value, lambda z, x, y, c: (z, c, y, x))

    def ring(value):
        return send(value, lambda z, x, y, c: ((z + 1) % planes, x, y, c))

    def other_core(value):
        return send(value, lambda z, x, y, c: (z, x, y, 1 - c))

    def after(value, *others):
        return lax.optimization_barrier((value, *others))[0]

    bal, seq = lax.axis_index("bal"), lax.axis_index("seq")
    z, x, y, c = bal // 2, bal % 2, seq // 2, seq % 2
    ids = jnp.stack([bal, z * 2 + c]).astype(jnp.int32)

    outgoing = pick_tiles(tokens, tile_owner, ids, groups, capacity)

    by_head = after(jnp.transpose(w_qkv, (1, 0, 2)), outgoing[0])
    pair = 2 if heads % 2 == 0 else 1
    v_columns = by_head[:, :, 2 * dim :]
    v_columns = jnp.concatenate([v_columns[i::pair] for i in range(pair)], axis=2)
    qk_own = [swap(by_head[:, :, : 2 * dim])]

    def to_owner(k):
        def to(z, x, y, c):
            owner = (z * 2 + x + k) % groups
            return owner // 2, c, y, owner % 2

        return to

    arrived = []
    for k in range(groups):
        arrived.append(send(outgoing[k], to_owner(k)))
    table = swap(after(modulation[0], outgoing[0]))
    clips = swap(after(clip_dims[0], outgoing[0]))
    gains = (swap(q_gain), swap(k_gain))
    member, tile_mask = tile_layout(clips)
    if groups * capacity == TILES_OWN:
        place = jnp.arange(TILES_OWN, dtype=jnp.int32)
    else:
        named = lax.all_gather(tile_owner, "bal", axis=0) == ids[1]
        live = jnp.arange(capacity)[None, :] < jnp.sum(named, axis=1, dtype=jnp.int32)[:, None]
        live = live.reshape(-1)
        place = jnp.where(live, jnp.cumsum(live.astype(jnp.int32)) - 1, TILES_OWN).astype(jnp.int32)
    gated = jnp.maximum(lax.optimization_barrier(member), 0)
    normed = norm_tiles(arrived, table, gated, place, ids, groups)

    def along_x(value):
        return send(value, lambda z, x, y, c: (z, x ^ 1, y, c))

    def along_y(value, py):
        return send(value, lambda z, x, y, c: (z, x, (y - py) % lines, c))

    across = along_x(normed)
    pieces = [normed, across]
    order = [y * 2 + x, y * 2 + (x ^ 1)]
    half = normed.shape[1] // 2
    for py in range(1, lines):
        beside = along_y(normed, py)
        corner = [along_x(beside[:, :half]), along_y(across[:, half:], py)]
        pieces += [beside, *corner]
        order += [(y + py) % lines * 2 + x, (y + py) % lines * 2 + (x ^ 1)]
    order = jnp.stack(order).astype(jnp.int32)

    def near_planes(own):
        if planes == 4:
            return [own, send(own, lambda z, x, y, c: (z ^ 1, x, y, c))]
        got = [own]
        for _ in range(planes - 2):
            got.append(ring(got[-1]))
        return got

    def far_plane(got, *earlier):
        if planes != 4:
            return got
        return [*got, send(after(got[0], *earlier), lambda z, x, y, c: (z ^ 2, x, y, c))]

    def end_planes(got, *earlier):
        if planes == 4:
            own, _, two = got
            return [send_some(after(own, two, *earlier), {1: 2, 2: 1}), send_some(after(two, *earlier), {1: 0, 2: 3})]
        return [ring(after(got[-1], *earlier))]

    def last_plane(ends, *earlier):
        return sum(ends[1:], after(ends[0], *earlier))

    def send_some(value, hops):
        pairs = []
        for b in range(groups):
            for s in range(n):
                if b // 2 in hops:
                    pairs.append((b * n + s, (hops[b // 2] * 2 + b % 2) * n + s))
        return lax.ppermute(value, AXES, pairs)

    def plane_at(step):
        return z ^ step if planes == 4 else (z - step) % planes

    def blocks_of(own, steps):
        blocks, at = [], []
        for step in steps:
            blocks += [own[step], other_core(own[step])]
            at += [plane_at(step) * 2 + c, plane_at(step) * 2 + 1 - c]
        return blocks, jnp.stack(at).astype(jnp.int32)

    qk_own = near_planes(qk_own[0])
    qk_own = far_plane(qk_own, *arrived)
    v_first = swap(v_columns)
    v_own = near_planes(after(v_first, *arrived))
    qk_ends = end_planes(qk_own)

    blocks, at = blocks_of(qk_own, range(planes - 1))
    qk, *_ = project(pieces, blocks, at, None, False)
    split = max(planes - 2, 1)
    blocks, at = blocks_of(v_own, range(split))
    blocks[0] = after(blocks[0], qk)
    values, *_ = project(pieces, blocks, at, None, False)
    v_own = far_plane(v_own, *qk_ends)
    qk_own.append(last_plane(qk_ends, values))
    blocks, at = blocks_of(qk_own, [planes - 1])
    qk, sums = project(pieces, blocks, at, qk, True)
    partial_sums = [sums, along_x(sums)]
    for py in range(1, lines):
        partial_sums.append(along_y(sums, py))
        partial_sums.append(send(sums, lambda z, x, y, c: (z, x ^ 1, (y - py) % lines, c)))

    bias = jnp.where(tile_mask.T, 0.0, mask_bias).astype(jnp.bfloat16)
    bias = jnp.pad(bias, ((0, 0), (0, dim - TILES_OWN)))
    bias = jnp.tile(jnp.repeat(bias, piece, axis=0), (n, 1))
    parts = 2 if heads % 2 == 0 else 1
    weights = []
    for i in range(parts):
        part = soft_weights(qk, partial_sums, gains, bias, features, i * heads // parts, heads // parts)
        weights.append(part)
        if i == 0:
            v_ends = end_planes(v_own, weights[0])
    v_own.append(last_plane(v_ends, weights[-1]))
    blocks, at = blocks_of(v_own, range(split, planes))
    mixed = mix_values(weights, values, pieces, blocks, at, order, place, groups, capacity, piece)
    returned = lax.all_to_all(
        mixed.reshape(groups * n, capacity * piece, heads * dim), AXES, split_axis=0, concat_axis=0, tiled=True
    )
    return place_tiles(returned, tile_owner, groups, n, capacity)


def solution(mesh):
    return jax.shard_map(
        transposed,
        mesh=mesh,
        in_specs=(
            P("bal", "seq", None),
            P("bal", "seq", None),
            P("seq", None),
            P("seq", None),
            P("bal", None, None, None),
            P("bal"),
            P("bal", None, None),
        ),
        out_specs=P("bal", "seq", None),
        check_vma=False,
    )
```

```python
import jax
import jax.numpy as jnp
from jax import lax
from jax.experimental import pallas as pl
from jax.experimental.pallas import tpu as pltpu
from jax.sharding import PartitionSpec as P


TILES_OWN = 16
AXES = ("bal", "seq")

eps_norm = 1e-06
log2_e = 1.4426950408889634
mask_bias = -3e38


def tile_layout(clip_shape):
    frames_of = clip_shape[:, 0]
    rows_of = clip_shape[:, 1]
    cols_of = clip_shape[:, 2]
    clip_sizes = frames_of * rows_of * cols_of
    clip_ends = jnp.cumsum(clip_sizes)
    clip_starts = clip_ends - clip_sizes
    local_index = jnp.arange(TILES_OWN, dtype=jnp.int32)
    member = jnp.sum((local_index[:, None] >= clip_ends[None, :]).astype(jnp.int32), axis=1)
    onehot = member[:, None] == jnp.arange(clip_shape.shape[0], dtype=jnp.int32)[None, :]

    def select_clip(values):
        return jnp.sum(jnp.where(onehot, values[None, :], 0), axis=1)

    offset = local_index - select_clip(clip_starts)
    height = jnp.maximum(select_clip(rows_of), 1)
    width_tiles = jnp.maximum(select_clip(cols_of), 1)
    frame_index = offset // (height * width_tiles)
    row_index = offset // width_tiles % height
    column = offset % width_tiles

    def within_one(coords):
        return jnp.abs(coords[:, None] - coords[None, :]) <= 1

    tile_mask = (
        (member[:, None] == member[None, :])
        & within_one(frame_index)
        & within_one(row_index)
        & within_one(column)
    )
    return (member.astype(jnp.int32), tile_mask)


def smem():
    return pl.BlockSpec(memory_space=pltpu.SMEM)


def vmem():
    return pl.BlockSpec(memory_space=pltpu.VMEM)


def pick_tiles(tokens, tile_owner, ids, groups, capacity):
    count = tokens.shape[0]

    def body(own_ref, ids_ref, tok_ref, *rest):
        outs, seen, index = rest[:groups], rest[groups], rest[groups + 1]
        for k in range(groups):
            seen[k] = 0
        for k in range(groups * capacity):
            index[k] = 0
        for i in range(count):
            k = lax.rem(own_ref[i] - ids_ref[0] + groups, groups)
            r = seen[k]
            seen[k] = r + 1
            index[k * capacity + r] = i
        for k in range(groups):
            for j in range(capacity):
                outs[k][j] = tok_ref[index[k * capacity + j]]

    shape = jax.ShapeDtypeStruct((capacity,) + tokens.shape[1:], tokens.dtype)
    return pl.pallas_call(
        body,
        out_shape=[shape] * groups,
        in_specs=[smem(), smem(), vmem()],
        out_specs=[vmem()] * groups,
        scratch_shapes=[
            pltpu.SMEM((groups,), jnp.int32),
            pltpu.SMEM((groups * capacity,), jnp.int32),
        ],
        name="pick_tiles",
    )(tile_owner, ids, tokens)


def norm_tiles(pieces, table, member, place, ids, groups):
    capacity, piece, width = pieces[0].shape
    tiles = TILES_OWN
    depth = width // groups

    def body(member_ref, place_ref, ids_ref, table_ref, *rest):
        ins, out_ref, held = rest[:groups], rest[groups], rest[groups + 1]
        for k in range(groups):
            source = lax.rem(ids_ref[1] - k + groups, groups)
            for j in range(capacity):
                held[place_ref[source * capacity + j]] = ins[k][j]

        def one(r, carry):
            values = held[r].astype(jnp.float32)
            center = jnp.mean(values, axis=-1, keepdims=True)
            values = values - center
            spread = jnp.mean(jnp.square(values), axis=-1, keepdims=True)
            values = values * lax.rsqrt(spread + eps_norm)
            rows = table_ref[member_ref[r]]
            done = (values * (1.0 + rows[1:2]) + rows[0:1]).astype(out_ref.dtype)
            at = pl.multiple_of(r * piece, piece)
            for g in range(groups):
                out_ref[g, pl.ds(at, piece), :] = done[:, g * depth : (g + 1) * depth]
            return carry

        lax.fori_loop(0, tiles, one, 0)

    return pl.pallas_call(
        body,
        out_shape=jax.ShapeDtypeStruct((groups, tiles * piece, depth), pieces[0].dtype),
        in_specs=[smem(), smem(), smem(), vmem()] + [vmem()] * groups,
        out_specs=vmem(),
        scratch_shapes=[pltpu.VMEM((tiles + 1, piece, width), pieces[0].dtype)],
        cost_estimate=pl.CostEstimate(
            flops=12 * tiles * piece * width,
            bytes_accessed=4 * tiles * piece * width,
            transcendentals=0,
        ),
        name="norm_tiles",
    )(member, place, ids, table, *pieces)


def project(xs, blocks, at, acc, sums):
    heads, depth, cols = blocks[0].shape
    sizes = [x.shape[1] for x in xs]
    total, m, n = sum(sizes), len(xs), len(blocks)

    def body(at_ref, *refs):
        x_refs, w_refs, rest = refs[: m * n], refs[m * n : (m + 1) * n], list(refs[(m + 1) * n :])
        acc_ref = rest.pop(0) if acc is not None else None
        out_ref = rest.pop(0)
        left = [jnp.concatenate([x_refs[i * n + j][0] for j in range(n)], axis=1) for i in range(m)]
        right = jnp.concatenate([ref[0] for ref in w_refs], axis=0)
        part = jnp.dot(jnp.concatenate(left, axis=0), right, preferred_element_type=jnp.float32)
        if acc is not None:
            part += acc_ref[0]
        out_ref[0] = part
        if sums:
            sums_ref, squares = rest
            head = pl.program_id(0)

            @pl.when(head == 0)
            def _():
                squares[...] = jnp.square(part)

            @pl.when(head > 0)
            def _():
                squares[...] += jnp.square(part)

            @pl.when(head == heads - 1)
            def _():
                lane = lax.broadcasted_iota(jnp.int32, (8, cols), 1)
                row = lax.broadcasted_iota(jnp.int32, (8, cols), 0)
                sums_ref[...] = lax.dot_general(
                    (lane // (cols // 2) == row).astype(jnp.float32),
                    squares[...],
                    (((1,), (1,)), ((), ())),
                    precision=lax.Precision.HIGHEST,
                    preferred_element_type=jnp.float32,
                )

    specs = [pl.BlockSpec((1, size, depth), lambda h, a, j=j: (a[j], 0, 0)) for size in sizes for j in range(n)]
    specs += [pl.BlockSpec((1, depth, cols), lambda h, a: (h, 0, 0))] * n
    args = [x for x in xs for _ in range(n)] + list(blocks)
    acc_spec = pl.BlockSpec((1, total, cols), lambda h, a: (h, 0, 0))
    aliases = {}
    if acc is not None:
        aliases = {1 + len(args): 0}
        specs.append(acc_spec)
        args.append(acc)
    out_shape = [jax.ShapeDtypeStruct((heads, total, cols), jnp.float32)]
    out_specs = [acc_spec]
    scratch = []
    if sums:
        out_shape.append(jax.ShapeDtypeStruct((8, total), jnp.float32))
        out_specs.append(pl.BlockSpec((8, total), lambda h, a: (0, 0)))
        scratch.append(pltpu.VMEM((total, cols), jnp.float32))
    return pl.pallas_call(
        body,
        out_shape=out_shape,
        grid_spec=pltpu.PrefetchScalarGridSpec(
            num_scalar_prefetch=1, grid=(heads,), in_specs=specs, out_specs=out_specs, scratch_shapes=scratch
        ),
        input_output_aliases=aliases,
        cost_estimate=pl.CostEstimate(
            flops=2 * n * total * depth * cols * heads,
            bytes_accessed=2 * n * (total + cols * heads) * depth + 8 * total * cols * heads,
            transcendentals=0,
        ),
        name="project",
    )(at, *args)


def soft_weights(qk, partial_sums, gains, bias, features, first, count):
    heads, total, cols = qk.shape
    dim = cols // 2
    n = len(partial_sums)
    rows = total // n
    extra = bias.shape[1]

    def body(*refs):
        q_ref, k_ref = refs[0], refs[1]
        sum_refs = refs[2 : 2 + n]
        qg_ref, kg_ref, bias_ref, out_ref, scales, keys = refs[2 + n :]
        head = pl.program_id(0)

        @pl.when(head == 0)
        def _():
            keys[:, dim:] = bias_ref[...]
            for p in range(n):
                whole = None
                for q in range(n):
                    there = (p // 2 - q // 2) % (n // 2) * 2 + (p % 2 ^ q % 2)
                    part = sum_refs[q][:, there * rows : (there + 1) * rows]
                    whole = part if whole is None else whole + part
                scales[p * rows : (p + 1) * rows] = jnp.transpose(lax.rsqrt(whole / features + eps_norm))

        keys[:, :dim] = (k_ref[0] * scales[:, 1:2] * kg_ref[pl.ds(first + head, 1), :]).astype(keys.dtype)
        lane = lax.broadcasted_iota(jnp.int32, (rows, extra), 1)
        row = lax.broadcasted_iota(jnp.int32, (rows, extra), 0)
        tile = (row // (rows // TILES_OWN) == lane).astype(keys.dtype)
        for p in range(n):
            here = slice(p * rows, (p + 1) * rows)
            query = q_ref[0, here] * scales[here, 0:1] * qg_ref[pl.ds(first + head, 1), :]
            scores = lax.dot_general(
                jnp.concatenate([query.astype(keys.dtype), tile], axis=1),
                keys[...],
                (((1,), (1,)), ((), ())),
                preferred_element_type=jnp.float32,
            )
            largest = jnp.max(scores, axis=-1, keepdims=True)
            powers = jnp.exp2((scores - largest) * (dim ** (-0.5) * log2_e))
            share = 1.0 / jnp.sum(powers, axis=-1, keepdims=True)
            out_ref[0, here] = (powers * share).astype(out_ref.dtype)

    whole_sum = pl.BlockSpec((8, total), lambda h: (0, 0))
    gain = pl.BlockSpec((heads, dim), lambda h: (0, 0))
    return pl.pallas_call(
        body,
        out_shape=jax.ShapeDtypeStruct((count, total, total), jnp.bfloat16),
        grid=(count,),
        in_specs=[
            pl.BlockSpec((1, total, dim), lambda h: (first + h, 0, 0)),
            pl.BlockSpec((1, total, dim), lambda h: (first + h, 0, 1)),
        ]
        + [whole_sum] * n
        + [gain, gain, pl.BlockSpec(bias.shape, lambda h: (0, 0))],
        out_specs=pl.BlockSpec((1, total, total), lambda h: (h, 0, 0)),
        scratch_shapes=[pltpu.VMEM((total, 8), jnp.float32), pltpu.VMEM((total, dim + extra), jnp.bfloat16)],
        cost_estimate=pl.CostEstimate(
            flops=(2 * dim + 8) * count * total * total,
            bytes_accessed=count * total * (2 * total + 4 * cols),
            transcendentals=count * total * total,
        ),
        name="soft_weights",
    )(qk, qk, *partial_sums, *gains, bias)


def mix_values(weights, values, xs, blocks, at, order, place, groups, capacity, piece):
    parts, (count, total, _) = len(weights), weights[0].shape
    heads = parts * count
    packed, _, cols = values.shape
    depth = blocks[0].shape[1]
    dim = packed * cols // heads
    share = heads // packed
    n = order.shape[0]
    rows = total // n
    sizes = [x.shape[1] for x in xs]
    m, k = len(xs), len(blocks)
    full = groups * capacity == TILES_OWN

    def body(order_ref, place_ref, at_ref, *refs):
        weight_refs, x_refs, refs = refs[:parts], refs[parts : parts + m * k], refs[parts + m * k :]
        w_refs, (acc_ref, out_ref, held, *staged) = refs[:k], refs[k:]
        head = pl.program_id(0)

        @pl.when(head % share == 0)
        def _():
            left = [jnp.concatenate([x_refs[i * k + j][0] for j in range(k)], axis=1) for i in range(m)]
            right = jnp.concatenate([ref[0] for ref in w_refs], axis=0)
            done = acc_ref[0] + jnp.dot(jnp.concatenate(left, axis=0), right, preferred_element_type=jnp.float32)
            for i in range(share):
                held[i] = done[:, i * dim : (i + 1) * dim].astype(held.dtype)

        for i in range(parts):

            @pl.when(head // count == i)
            def _(weight_ref=weight_refs[i]):
                mixed = jnp.dot(weight_ref[0], held[head % share], preferred_element_type=jnp.float32)
                for p in range(n):
                    block = mixed[p * rows : (p + 1) * rows]
                    if full:
                        out_ref[:, order_ref[p]] = block.astype(out_ref.dtype).reshape(groups, capacity * piece, dim)
                        continue
                    staged[0][...] = block
                    for slot in range(groups * capacity):
                        tile = jnp.minimum(place_ref[slot], TILES_OWN - 1)
                        tile_rows = staged[0][pl.ds(pl.multiple_of(tile * piece, piece), piece), :]
                        to = slot % capacity * piece
                        out_ref[slot // capacity, order_ref[p], to : to + piece] = tile_rows.astype(out_ref.dtype)

    def weight_block(i):
        return pl.BlockSpec((1, total, total), lambda h, o, s, a: (jnp.clip(h - i * count, 0, count - 1), 0, 0))

    return pl.pallas_call(
        body,
        out_shape=jax.ShapeDtypeStruct((groups, n, capacity * piece, heads * dim), jnp.bfloat16),
        grid_spec=pltpu.PrefetchScalarGridSpec(
            num_scalar_prefetch=3,
            grid=(heads,),
            in_specs=[weight_block(i) for i in range(parts)]
            + [pl.BlockSpec((1, size, depth), lambda h, o, s, a, j=j: (a[j], 0, 0)) for size in sizes for j in range(k)]
            + [pl.BlockSpec((1, depth, cols), lambda h, o, s, a: (h // share, 0, 0))] * k
            + [pl.BlockSpec((1, total, cols), lambda h, o, s, a: (h // share, 0, 0))],
            out_specs=pl.BlockSpec((groups, n, capacity * piece, dim), lambda h, o, s, a: (0, 0, 0, h)),
            scratch_shapes=[pltpu.VMEM((share, total, dim), jnp.bfloat16)]
            + [pltpu.VMEM((rows, dim), jnp.float32)] * (not full),
        ),
        cost_estimate=pl.CostEstimate(
            flops=2 * heads * total * (total + k * depth) * dim,
            bytes_accessed=heads * total * (2 * total + 6 * dim),
            transcendentals=0,
        ),
        name="mix_values",
    )(order, place, at, *weights, *[x for x in xs for _ in range(k)], *blocks, values)


def place_tiles(returned, tile_owner, groups, n, capacity):
    _, rows, width = returned.shape
    piece = rows // capacity
    count = tile_owner.shape[0]

    def body(own_ref, in_ref, out_ref, seen):
        for k in range(groups):
            seen[k] = 0
        for i in range(count):
            owner = own_ref[i]
            rank = seen[owner]
            seen[owner] = rank + 1
            at = pl.multiple_of(rank * piece, piece)
            for g in range(n):
                source = (owner // 2 * 2 + g % 2) * n + g // 2 * 2 + lax.rem(owner, 2)
                out_ref[i, :, g * width : (g + 1) * width] = in_ref[source, pl.ds(at, piece), :]

    return pl.pallas_call(
        body,
        out_shape=jax.ShapeDtypeStruct((count, piece, n * width), returned.dtype),
        in_specs=[smem(), vmem()],
        out_specs=vmem(),
        scratch_shapes=[pltpu.SMEM((groups,), jnp.int32)],
        name="place_tiles",
    )(tile_owner, returned)


def transposed(tokens, w_qkv, q_gain, k_gain, modulation, tile_owner, clip_dims):
    groups, n = lax.axis_size("bal"), lax.axis_size("seq")
    planes, lines = groups // 2, n // 2
    owned_tiles, piece, _ = tokens.shape
    capacity = owned_tiles // min(groups, owned_tiles)
    heads, dim = q_gain.shape
    features = heads * n * dim

    def send(value, to):
        pairs = []
        for b in range(groups):
            for s in range(n):
                z, x, y, c = to(b // 2, b % 2, s // 2, s % 2)
                pairs.append((b * n + s, (z * 2 + x) * n + y * 2 + c))
        return lax.ppermute(value, AXES, pairs)

    def swap(value):
        return send(value, lambda z, x, y, c: (z, c, y, x))

    def ring(value):
        return send(value, lambda z, x, y, c: ((z + 1) % planes, x, y, c))

    def other_core(value):
        return send(value, lambda z, x, y, c: (z, x, y, 1 - c))

    def after(value, *others):
        return lax.optimization_barrier((value, *others))[0]

    bal, seq = lax.axis_index("bal"), lax.axis_index("seq")
    z, x, y, c = bal // 2, bal % 2, seq // 2, seq % 2
    ids = jnp.stack([bal, z * 2 + c]).astype(jnp.int32)

    outgoing = pick_tiles(tokens, tile_owner, ids, groups, capacity)

    by_head = after(jnp.transpose(w_qkv, (1, 0, 2)), outgoing[0])
    pair = 2 if heads % 2 == 0 else 1
    v_columns = by_head[:, :, 2 * dim :]
    v_columns = jnp.concatenate([v_columns[i::pair] for i in range(pair)], axis=2)
    qk_own = [swap(by_head[:, :, : 2 * dim])]

    def to_owner(k):
        def to(z, x, y, c):
            owner = (z * 2 + x + k) % groups
            return owner // 2, c, y, owner % 2

        return to

    arrived = []
    for k in range(groups):
        arrived.append(send(outgoing[k], to_owner(k)))
    table = swap(after(modulation[0], outgoing[0]))
    clips = swap(after(clip_dims[0], outgoing[0]))
    gains = (swap(q_gain), swap(k_gain))
    member, tile_mask = tile_layout(clips)
    if groups * capacity == TILES_OWN:
        place = jnp.arange(TILES_OWN, dtype=jnp.int32)
    else:
        named = lax.all_gather(tile_owner, "bal", axis=0) == ids[1]
        live = jnp.arange(capacity)[None, :] < jnp.sum(named, axis=1, dtype=jnp.int32)[:, None]
        live = live.reshape(-1)
        place = jnp.where(live, jnp.cumsum(live.astype(jnp.int32)) - 1, TILES_OWN).astype(jnp.int32)
    gated = jnp.maximum(lax.optimization_barrier(member), 0)
    normed = norm_tiles(arrived, table, gated, place, ids, groups)

    def along_x(value):
        return send(value, lambda z, x, y, c: (z, x ^ 1, y, c))

    def along_y(value, py):
        return send(value, lambda z, x, y, c: (z, x, (y - py) % lines, c))

    across = along_x(normed)
    pieces = [normed, across]
    order = [y * 2 + x, y * 2 + (x ^ 1)]
    half = normed.shape[1] // 2
    for py in range(1, lines):
        beside = along_y(normed, py)
        corner = [along_x(beside[:, :half]), along_y(across[:, half:], py)]
        pieces += [beside, *corner]
        order += [(y + py) % lines * 2 + x, (y + py) % lines * 2 + (x ^ 1)]
    order = jnp.stack(order).astype(jnp.int32)

    def near_planes(own):
        if planes == 4:
            return [own, send(own, lambda z, x, y, c: (z ^ 1, x, y, c))]
        got = [own]
        for _ in range(planes - 2):
            got.append(ring(got[-1]))
        return got

    def send_some(value, hops):
        pairs = []
        for b in range(groups):
            for s in range(n):
                if b // 2 in hops:
                    pairs.append((b * n + s, (hops[b // 2] * 2 + b % 2) * n + s))
        return lax.ppermute(value, AXES, pairs)

    def cross(value):
        return send_some(value, {1: 2, 2: 1})

    def outward(value):
        return send_some(value, {1: 0, 2: 3})

    def plane_at(step):
        if planes != 4:
            return (z - step) % planes
        low = z < 2
        return [z, z ^ 1, jnp.where(low, 2, 1), jnp.where(low, 3, 0)][step]

    def blocks_of(own, steps):
        blocks, at = [], []
        for step in steps:
            blocks += [own[step], other_core(own[step])]
            at += [plane_at(step) * 2 + c, plane_at(step) * 2 + 1 - c]
        return blocks, jnp.stack(at).astype(jnp.int32)

    qk_own = near_planes(qk_own[0])
    v_first = swap(v_columns)
    v_own = near_planes(after(v_first, *arrived))
    if planes == 4:
        crossed = cross(after(qk_own[0], *arrived))
        crossed_next = cross(after(qk_own[1], crossed))
        qk_own.append(crossed + outward(crossed))
        passed = outward(crossed_next)
        v_crossed = cross(after(v_own[0], crossed_next))
        v_crossed_next = cross(after(v_own[1], v_crossed))
        v_passed = [outward(after(v_crossed, passed)), outward(after(v_crossed_next, passed))]

    blocks, at = blocks_of(qk_own, range(planes - 1))
    qk, *_ = project(pieces, blocks, at, None, False)
    qk_own.append(after(crossed_next, qk) + passed if planes == 4 else ring(after(qk_own[-1], qk)))
    blocks, at = blocks_of(qk_own, [planes - 1])
    qk, sums = project(pieces, blocks, at, qk, True)
    split = max(planes - 2, 1)
    blocks, at = blocks_of(v_own, range(split))
    blocks[0] = after(blocks[0], sums)
    values, *_ = project(pieces, blocks, at, None, False)
    partial_sums = [sums]
    partial_sums.append(along_x(sums))
    for py in range(1, lines):
        partial_sums.append(along_y(sums, py))
        partial_sums.append(send(sums, lambda z, x, y, c: (z, x ^ 1, (y - py) % lines, c)))

    bias = jnp.where(tile_mask.T, 0.0, mask_bias).astype(jnp.bfloat16)
    bias = jnp.pad(bias, ((0, 0), (0, dim - TILES_OWN)))
    bias = jnp.tile(jnp.repeat(bias, piece, axis=0), (n, 1))
    weights = [soft_weights(qk, partial_sums, gains, after(bias, values), features, 0, heads)]
    if planes == 4:
        v_own.append(after(v_crossed, weights[0]) + v_passed[0])
        v_own.append(after(v_crossed_next, weights[0]) + v_passed[1])
    else:
        v_own.append(ring(after(v_own[-1], sums)))
    blocks, at = blocks_of(v_own, range(split, planes))
    mixed = mix_values(weights, values, pieces, blocks, at, order, place, groups, capacity, piece)
    returned = lax.all_to_all(
        mixed.reshape(groups * n, capacity * piece, heads * dim), AXES, split_axis=0, concat_axis=0, tiled=True
    )
    return place_tiles(returned, tile_owner, groups, n, capacity)


def solution(mesh):
    return jax.shard_map(
        transposed,
        mesh=mesh,
        in_specs=(
            P("bal", "seq", None),
            P("bal", "seq", None),
            P("seq", None),
            P("seq", None),
            P("bal", None, None, None),
            P("bal"),
            P("bal", None, None),
        ),
        out_specs=P("bal", "seq", None),
        check_vma=False,
    )
```

```python
import jax
import jax.numpy as jnp
from jax import lax
from jax.experimental import pallas as pl
from jax.experimental.pallas import tpu as pltpu
from jax.sharding import PartitionSpec as P


TILES_OWN = 16
AXES = ("bal", "seq")

eps_norm = 1e-06
log2_e = 1.4426950408889634
mask_bias = -3e38


def tile_layout(clip_shape):
    frames_of = clip_shape[:, 0]
    rows_of = clip_shape[:, 1]
    cols_of = clip_shape[:, 2]
    clip_sizes = frames_of * rows_of * cols_of
    clip_ends = jnp.cumsum(clip_sizes)
    clip_starts = clip_ends - clip_sizes
    local_index = jnp.arange(TILES_OWN, dtype=jnp.int32)
    member = jnp.sum((local_index[:, None] >= clip_ends[None, :]).astype(jnp.int32), axis=1)
    onehot = member[:, None] == jnp.arange(clip_shape.shape[0], dtype=jnp.int32)[None, :]

    def select_clip(values):
        return jnp.sum(jnp.where(onehot, values[None, :], 0), axis=1)

    offset = local_index - select_clip(clip_starts)
    height = jnp.maximum(select_clip(rows_of), 1)
    width_tiles = jnp.maximum(select_clip(cols_of), 1)
    frame_index = offset // (height * width_tiles)
    row_index = offset // width_tiles % height
    column = offset % width_tiles

    def within_one(coords):
        return jnp.abs(coords[:, None] - coords[None, :]) <= 1

    tile_mask = (
        (member[:, None] == member[None, :])
        & within_one(frame_index)
        & within_one(row_index)
        & within_one(column)
    )
    return (member.astype(jnp.int32), tile_mask)


def smem():
    return pl.BlockSpec(memory_space=pltpu.SMEM)


def vmem():
    return pl.BlockSpec(memory_space=pltpu.VMEM)


def pick_tiles(tokens, tile_owner, ids, groups, capacity):
    count = tokens.shape[0]

    def body(own_ref, ids_ref, tok_ref, *rest):
        outs, seen, index = rest[:groups], rest[groups], rest[groups + 1]
        for k in range(groups):
            seen[k] = 0
        for k in range(groups * capacity):
            index[k] = 0
        for i in range(count):
            k = lax.rem(own_ref[i] - ids_ref[0] + groups, groups)
            r = seen[k]
            seen[k] = r + 1
            index[k * capacity + r] = i
        for k in range(groups):
            for j in range(capacity):
                outs[k][j] = tok_ref[index[k * capacity + j]]

    shape = jax.ShapeDtypeStruct((capacity,) + tokens.shape[1:], tokens.dtype)
    return pl.pallas_call(
        body,
        out_shape=[shape] * groups,
        in_specs=[smem(), smem(), vmem()],
        out_specs=[vmem()] * groups,
        scratch_shapes=[
            pltpu.SMEM((groups,), jnp.int32),
            pltpu.SMEM((groups * capacity,), jnp.int32),
        ],
        name="pick_tiles",
    )(tile_owner, ids, tokens)


def norm_tiles(pieces, table, member, place, ids, groups):
    capacity, piece, width = pieces[0].shape
    tiles = TILES_OWN
    depth = width // groups

    def body(member_ref, place_ref, ids_ref, table_ref, *rest):
        ins, out_ref, held = rest[:groups], rest[groups], rest[groups + 1]
        for k in range(groups):
            source = lax.rem(ids_ref[1] - k + groups, groups)
            for j in range(capacity):
                held[place_ref[source * capacity + j]] = ins[k][j]

        def one(r, carry):
            values = held[r].astype(jnp.float32)
            center = jnp.mean(values, axis=-1, keepdims=True)
            values = values - center
            spread = jnp.mean(jnp.square(values), axis=-1, keepdims=True)
            values = values * lax.rsqrt(spread + eps_norm)
            rows = table_ref[member_ref[r]]
            done = (values * (1.0 + rows[1:2]) + rows[0:1]).astype(out_ref.dtype)
            at = pl.multiple_of(r * piece, piece)
            for g in range(groups):
                out_ref[g, pl.ds(at, piece), :] = done[:, g * depth : (g + 1) * depth]
            return carry

        lax.fori_loop(0, tiles, one, 0)

    return pl.pallas_call(
        body,
        out_shape=jax.ShapeDtypeStruct((groups, tiles * piece, depth), pieces[0].dtype),
        in_specs=[smem(), smem(), smem(), vmem()] + [vmem()] * groups,
        out_specs=vmem(),
        scratch_shapes=[pltpu.VMEM((tiles + 1, piece, width), pieces[0].dtype)],
        cost_estimate=pl.CostEstimate(
            flops=12 * tiles * piece * width,
            bytes_accessed=4 * tiles * piece * width,
            transcendentals=0,
        ),
        name="norm_tiles",
    )(member, place, ids, table, *pieces)


def project(xs, blocks, at, acc, sums):
    heads, depth, cols = blocks[0].shape
    sizes = [x.shape[1] for x in xs]
    total, m, n = sum(sizes), len(xs), len(blocks)

    def body(at_ref, *refs):
        x_refs, w_refs, rest = refs[: m * n], refs[m * n : (m + 1) * n], list(refs[(m + 1) * n :])
        acc_ref = rest.pop(0) if acc is not None else None
        out_ref = rest.pop(0)
        left = [jnp.concatenate([x_refs[i * n + j][0] for j in range(n)], axis=1) for i in range(m)]
        right = jnp.concatenate([ref[0] for ref in w_refs], axis=0)
        part = jnp.dot(jnp.concatenate(left, axis=0), right, preferred_element_type=jnp.float32)
        if acc is not None:
            part += acc_ref[0]
        out_ref[0] = part
        if sums:
            sums_ref, squares = rest
            head = pl.program_id(0)

            @pl.when(head == 0)
            def _():
                squares[...] = jnp.square(part)

            @pl.when(head > 0)
            def _():
                squares[...] += jnp.square(part)

            @pl.when(head == heads - 1)
            def _():
                lane = lax.broadcasted_iota(jnp.int32, (8, cols), 1)
                row = lax.broadcasted_iota(jnp.int32, (8, cols), 0)
                sums_ref[...] = lax.dot_general(
                    (lane // (cols // 2) == row).astype(jnp.float32),
                    squares[...],
                    (((1,), (1,)), ((), ())),
                    precision=lax.Precision.HIGHEST,
                    preferred_element_type=jnp.float32,
                )

    specs = [pl.BlockSpec((1, size, depth), lambda h, a, j=j: (a[j], 0, 0)) for size in sizes for j in range(n)]
    specs += [pl.BlockSpec((1, depth, cols), lambda h, a: (h, 0, 0))] * n
    args = [x for x in xs for _ in range(n)] + list(blocks)
    acc_spec = pl.BlockSpec((1, total, cols), lambda h, a: (h, 0, 0))
    aliases = {}
    if acc is not None:
        aliases = {1 + len(args): 0}
        specs.append(acc_spec)
        args.append(acc)
    out_shape = [jax.ShapeDtypeStruct((heads, total, cols), jnp.float32)]
    out_specs = [acc_spec]
    scratch = []
    if sums:
        out_shape.append(jax.ShapeDtypeStruct((8, total), jnp.float32))
        out_specs.append(pl.BlockSpec((8, total), lambda h, a: (0, 0)))
        scratch.append(pltpu.VMEM((total, cols), jnp.float32))
    return pl.pallas_call(
        body,
        out_shape=out_shape,
        grid_spec=pltpu.PrefetchScalarGridSpec(
            num_scalar_prefetch=1, grid=(heads,), in_specs=specs, out_specs=out_specs, scratch_shapes=scratch
        ),
        input_output_aliases=aliases,
        cost_estimate=pl.CostEstimate(
            flops=2 * n * total * depth * cols * heads,
            bytes_accessed=2 * n * (total + cols * heads) * depth + 8 * total * cols * heads,
            transcendentals=0,
        ),
        name="project",
    )(at, *args)


def soft_weights(qk, partial_sums, gains, bias, features, first, count):
    heads, total, cols = qk.shape
    dim = cols // 2
    n = len(partial_sums)
    rows = total // n
    extra = bias.shape[1]

    def body(*refs):
        q_ref, k_ref = refs[0], refs[1]
        sum_refs = refs[2 : 2 + n]
        qg_ref, kg_ref, bias_ref, out_ref, scales, keys = refs[2 + n :]
        head = pl.program_id(0)

        @pl.when(head == 0)
        def _():
            keys[:, dim:] = bias_ref[...]
            for p in range(n):
                whole = None
                for q in range(n):
                    there = (p // 2 - q // 2) % (n // 2) * 2 + (p % 2 ^ q % 2)
                    part = sum_refs[q][:, there * rows : (there + 1) * rows]
                    whole = part if whole is None else whole + part
                scales[p * rows : (p + 1) * rows] = jnp.transpose(lax.rsqrt(whole / features + eps_norm))

        keys[:, :dim] = (k_ref[0] * scales[:, 1:2] * kg_ref[pl.ds(first + head, 1), :]).astype(keys.dtype)
        lane = lax.broadcasted_iota(jnp.int32, (rows, extra), 1)
        row = lax.broadcasted_iota(jnp.int32, (rows, extra), 0)
        tile = (row // (rows // TILES_OWN) == lane).astype(keys.dtype)
        for p in range(n):
            here = slice(p * rows, (p + 1) * rows)
            query = q_ref[0, here] * scales[here, 0:1] * qg_ref[pl.ds(first + head, 1), :]
            scores = lax.dot_general(
                jnp.concatenate([query.astype(keys.dtype), tile], axis=1),
                keys[...],
                (((1,), (1,)), ((), ())),
                preferred_element_type=jnp.float32,
            )
            largest = jnp.max(scores, axis=-1, keepdims=True)
            powers = jnp.exp2((scores - largest) * (dim ** (-0.5) * log2_e))
            share = 1.0 / jnp.sum(powers, axis=-1, keepdims=True)
            out_ref[0, here] = (powers * share).astype(out_ref.dtype)

    whole_sum = pl.BlockSpec((8, total), lambda h: (0, 0))
    gain = pl.BlockSpec((heads, dim), lambda h: (0, 0))
    return pl.pallas_call(
        body,
        out_shape=jax.ShapeDtypeStruct((count, total, total), jnp.bfloat16),
        grid=(count,),
        in_specs=[
            pl.BlockSpec((1, total, dim), lambda h: (first + h, 0, 0)),
            pl.BlockSpec((1, total, dim), lambda h: (first + h, 0, 1)),
        ]
        + [whole_sum] * n
        + [gain, gain, pl.BlockSpec(bias.shape, lambda h: (0, 0))],
        out_specs=pl.BlockSpec((1, total, total), lambda h: (h, 0, 0)),
        scratch_shapes=[pltpu.VMEM((total, 8), jnp.float32), pltpu.VMEM((total, dim + extra), jnp.bfloat16)],
        cost_estimate=pl.CostEstimate(
            flops=(2 * dim + 8) * count * total * total,
            bytes_accessed=count * total * (2 * total + 4 * cols),
            transcendentals=count * total * total,
        ),
        name="soft_weights",
    )(qk, qk, *partial_sums, *gains, bias)


def mix_values(weights, values, xs, blocks, at, order, place, groups, capacity, piece):
    parts, (count, total, _) = len(weights), weights[0].shape
    heads = parts * count
    packed, _, cols = values.shape
    depth = blocks[0].shape[1]
    dim = packed * cols // heads
    share = heads // packed
    n = order.shape[0]
    rows = total // n
    sizes = [x.shape[1] for x in xs]
    m, k = len(xs), len(blocks)
    full = groups * capacity == TILES_OWN

    def body(order_ref, place_ref, at_ref, *refs):
        weight_refs, x_refs, refs = refs[:parts], refs[parts : parts + m * k], refs[parts + m * k :]
        w_refs, (acc_ref, out_ref, held, *staged) = refs[:k], refs[k:]
        head = pl.program_id(0)

        @pl.when(head % share == 0)
        def _():
            left = [jnp.concatenate([x_refs[i * k + j][0] for j in range(k)], axis=1) for i in range(m)]
            right = jnp.concatenate([ref[0] for ref in w_refs], axis=0)
            done = acc_ref[0] + jnp.dot(jnp.concatenate(left, axis=0), right, preferred_element_type=jnp.float32)
            for i in range(share):
                held[i] = done[:, i * dim : (i + 1) * dim].astype(held.dtype)

        for i in range(parts):

            @pl.when(head // count == i)
            def _(weight_ref=weight_refs[i]):
                mixed = jnp.dot(weight_ref[0], held[head % share], preferred_element_type=jnp.float32)
                for p in range(n):
                    block = mixed[p * rows : (p + 1) * rows]
                    if full:
                        out_ref[:, order_ref[p]] = block.astype(out_ref.dtype).reshape(groups, capacity * piece, dim)
                        continue
                    staged[0][...] = block
                    for slot in range(groups * capacity):
                        tile = jnp.minimum(place_ref[slot], TILES_OWN - 1)
                        tile_rows = staged[0][pl.ds(pl.multiple_of(tile * piece, piece), piece), :]
                        to = slot % capacity * piece
                        out_ref[slot // capacity, order_ref[p], to : to + piece] = tile_rows.astype(out_ref.dtype)

    def weight_block(i):
        return pl.BlockSpec((1, total, total), lambda h, o, s, a: (jnp.clip(h - i * count, 0, count - 1), 0, 0))

    return pl.pallas_call(
        body,
        out_shape=jax.ShapeDtypeStruct((groups, n, capacity * piece, heads * dim), jnp.bfloat16),
        grid_spec=pltpu.PrefetchScalarGridSpec(
            num_scalar_prefetch=3,
            grid=(heads,),
            in_specs=[weight_block(i) for i in range(parts)]
            + [pl.BlockSpec((1, size, depth), lambda h, o, s, a, j=j: (a[j], 0, 0)) for size in sizes for j in range(k)]
            + [pl.BlockSpec((1, depth, cols), lambda h, o, s, a: (h // share, 0, 0))] * k
            + [pl.BlockSpec((1, total, cols), lambda h, o, s, a: (h // share, 0, 0))],
            out_specs=pl.BlockSpec((groups, n, capacity * piece, dim), lambda h, o, s, a: (0, 0, 0, h)),
            scratch_shapes=[pltpu.VMEM((share, total, dim), jnp.bfloat16)]
            + [pltpu.VMEM((rows, dim), jnp.float32)] * (not full),
        ),
        cost_estimate=pl.CostEstimate(
            flops=2 * heads * total * (total + k * depth) * dim,
            bytes_accessed=heads * total * (2 * total + 6 * dim),
            transcendentals=0,
        ),
        name="mix_values",
    )(order, place, at, *weights, *[x for x in xs for _ in range(k)], *blocks, values)


def place_tiles(returned, tile_owner, groups, n, capacity):
    _, rows, width = returned.shape
    piece = rows // capacity
    count = tile_owner.shape[0]

    def body(own_ref, in_ref, out_ref, seen):
        for k in range(groups):
            seen[k] = 0
        for i in range(count):
            owner = own_ref[i]
            rank = seen[owner]
            seen[owner] = rank + 1
            at = pl.multiple_of(rank * piece, piece)
            for g in range(n):
                source = (owner // 2 * 2 + g % 2) * n + g // 2 * 2 + lax.rem(owner, 2)
                out_ref[i, :, g * width : (g + 1) * width] = in_ref[source, pl.ds(at, piece), :]

    return pl.pallas_call(
        body,
        out_shape=jax.ShapeDtypeStruct((count, piece, n * width), returned.dtype),
        in_specs=[smem(), vmem()],
        out_specs=vmem(),
        scratch_shapes=[pltpu.SMEM((groups,), jnp.int32)],
        name="place_tiles",
    )(tile_owner, returned)


def transposed(tokens, w_qkv, q_gain, k_gain, modulation, tile_owner, clip_dims):
    groups, n = lax.axis_size("bal"), lax.axis_size("seq")
    planes, lines = groups // 2, n // 2
    owned_tiles, piece, _ = tokens.shape
    capacity = owned_tiles // min(groups, owned_tiles)
    heads, dim = q_gain.shape
    features = heads * n * dim

    def send(value, to):
        pairs = []
        for b in range(groups):
            for s in range(n):
                z, x, y, c = to(b // 2, b % 2, s // 2, s % 2)
                pairs.append((b * n + s, (z * 2 + x) * n + y * 2 + c))
        return lax.ppermute(value, AXES, pairs)

    def swap(value):
        return send(value, lambda z, x, y, c: (z, c, y, x))

    def ring(value):
        return send(value, lambda z, x, y, c: ((z + 1) % planes, x, y, c))

    def other_core(value):
        return send(value, lambda z, x, y, c: (z, x, y, 1 - c))

    def after(value, *others):
        return lax.optimization_barrier((value, *others))[0]

    bal, seq = lax.axis_index("bal"), lax.axis_index("seq")
    z, x, y, c = bal // 2, bal % 2, seq // 2, seq % 2
    ids = jnp.stack([bal, z * 2 + c]).astype(jnp.int32)

    outgoing = pick_tiles(tokens, tile_owner, ids, groups, capacity)

    by_head = after(jnp.transpose(w_qkv, (1, 0, 2)), outgoing[0])
    pair = 2 if heads % 2 == 0 else 1
    v_columns = by_head[:, :, 2 * dim :]
    v_columns = jnp.concatenate([v_columns[i::pair] for i in range(pair)], axis=2)
    qk_own = [swap(by_head[:, :, : 2 * dim])]

    def to_owner(k):
        def to(z, x, y, c):
            owner = (z * 2 + x + k) % groups
            return owner // 2, c, y, owner % 2

        return to

    arrived = []
    for k in range(groups):
        arrived.append(send(outgoing[k], to_owner(k)))
    table = swap(after(modulation[0], outgoing[0]))
    clips = swap(after(clip_dims[0], outgoing[0]))
    gains = (swap(q_gain), swap(k_gain))
    member, tile_mask = tile_layout(clips)
    if groups * capacity == TILES_OWN:
        place = jnp.arange(TILES_OWN, dtype=jnp.int32)
    else:
        named = lax.all_gather(tile_owner, "bal", axis=0) == ids[1]
        live = jnp.arange(capacity)[None, :] < jnp.sum(named, axis=1, dtype=jnp.int32)[:, None]
        live = live.reshape(-1)
        place = jnp.where(live, jnp.cumsum(live.astype(jnp.int32)) - 1, TILES_OWN).astype(jnp.int32)
    gated = jnp.maximum(lax.optimization_barrier(member), 0)
    normed = norm_tiles(arrived, table, gated, place, ids, groups)

    def along_x(value):
        return send(value, lambda z, x, y, c: (z, x ^ 1, y, c))

    def along_y(value, py):
        return send(value, lambda z, x, y, c: (z, x, (y - py) % lines, c))

    across = along_x(normed)
    pieces = [normed, across]
    order = [y * 2 + x, y * 2 + (x ^ 1)]
    half = normed.shape[1] // 2
    for py in range(1, lines):
        beside = along_y(normed, py)
        corner = [along_x(beside[:, :half]), along_y(across[:, half:], py)]
        pieces += [beside, *corner]
        order += [(y + py) % lines * 2 + x, (y + py) % lines * 2 + (x ^ 1)]
    order = jnp.stack(order).astype(jnp.int32)

    def near_planes(own):
        if planes == 4:
            return [own, send(own, lambda z, x, y, c: (z ^ 1, x, y, c))]
        got = [own]
        for _ in range(planes - 2):
            got.append(ring(got[-1]))
        return got

    def send_some(value, hops):
        pairs = []
        for b in range(groups):
            for s in range(n):
                if b // 2 in hops:
                    pairs.append((b * n + s, (hops[b // 2] * 2 + b % 2) * n + s))
        return lax.ppermute(value, AXES, pairs)

    def cross(value):
        return send_some(value, {1: 2, 2: 1})

    def outward(value):
        return send_some(value, {1: 0, 2: 3})

    def plane_at(step):
        if planes != 4:
            return (z - step) % planes
        low = z < 2
        return [z, z ^ 1, jnp.where(low, 2, 1), jnp.where(low, 3, 0)][step]

    def blocks_of(own, steps):
        blocks, at = [], []
        for step in steps:
            blocks += [own[step], other_core(own[step])]
            at += [plane_at(step) * 2 + c, plane_at(step) * 2 + 1 - c]
        return blocks, jnp.stack(at).astype(jnp.int32)

    qk_own = near_planes(qk_own[0])
    v_first = swap(v_columns)
    v_own = near_planes(after(v_first, *arrived))
    if planes == 4:
        crossed = cross(after(qk_own[0], *arrived))
        crossed_next = cross(after(qk_own[1], crossed))
        qk_own.append(crossed + outward(crossed))
        passed = outward(crossed_next)
        v_crossed = cross(after(v_own[0], crossed_next))
        v_crossed_next = cross(after(v_own[1], crossed_next))
        v_passed = [outward(after(v_crossed, passed)), outward(after(v_crossed_next, passed))]

    blocks, at = blocks_of(qk_own, range(planes - 1))
    qk, *_ = project(pieces, blocks, at, None, False)
    split = max(planes - 2, 1)
    blocks, at = blocks_of(v_own, range(split))
    blocks[0] = after(blocks[0], qk)
    values, *_ = project(pieces, blocks, at, None, False)
    qk_own.append(after(crossed_next, values) + passed if planes == 4 else ring(after(qk_own[-1], values)))
    blocks, at = blocks_of(qk_own, [planes - 1])
    qk, sums = project(pieces, blocks, at, qk, True)
    partial_sums = [sums]
    partial_sums.append(along_x(sums))
    for py in range(1, lines):
        partial_sums.append(along_y(sums, py))
        partial_sums.append(send(sums, lambda z, x, y, c: (z, x ^ 1, (y - py) % lines, c)))

    bias = jnp.where(tile_mask.T, 0.0, mask_bias).astype(jnp.bfloat16)
    bias = jnp.pad(bias, ((0, 0), (0, dim - TILES_OWN)))
    bias = jnp.tile(jnp.repeat(bias, piece, axis=0), (n, 1))
    weights = [soft_weights(qk, partial_sums, gains, after(bias, values), features, 0, heads)]
    if planes == 4:
        v_own.append(after(v_crossed, weights[0]) + v_passed[0])
        v_own.append(after(v_crossed_next, weights[0]) + v_passed[1])
    else:
        v_own.append(ring(after(v_own[-1], sums)))
    blocks, at = blocks_of(v_own, range(split, planes))
    mixed = mix_values(weights, values, pieces, blocks, at, order, place, groups, capacity, piece)
    returned = lax.all_to_all(
        mixed.reshape(groups * n, capacity * piece, heads * dim), AXES, split_axis=0, concat_axis=0, tiled=True
    )
    return place_tiles(returned, tile_owner, groups, n, capacity)


def solution(mesh):
    return jax.shard_map(
        transposed,
        mesh=mesh,
        in_specs=(
            P("bal", "seq", None),
            P("bal", "seq", None),
            P("seq", None),
            P("seq", None),
            P("bal", None, None, None),
            P("bal"),
            P("bal", None, None),
        ),
        out_specs=P("bal", "seq", None),
        check_vma=False,
    )
```

```python
import jax
import jax.numpy as jnp
from jax import lax
from jax.experimental import pallas as pl
from jax.experimental.pallas import tpu as pltpu
from jax.sharding import PartitionSpec as P


TILES_OWN = 16
AXES = ("bal", "seq")

eps_norm = 1e-06
log2_e = 1.4426950408889634
mask_bias = -3e38


def tile_layout(clip_shape):
    frames_of = clip_shape[:, 0]
    rows_of = clip_shape[:, 1]
    cols_of = clip_shape[:, 2]
    clip_sizes = frames_of * rows_of * cols_of
    clip_ends = jnp.cumsum(clip_sizes)
    clip_starts = clip_ends - clip_sizes
    local_index = jnp.arange(TILES_OWN, dtype=jnp.int32)
    member = jnp.sum((local_index[:, None] >= clip_ends[None, :]).astype(jnp.int32), axis=1)
    onehot = member[:, None] == jnp.arange(clip_shape.shape[0], dtype=jnp.int32)[None, :]

    def select_clip(values):
        return jnp.sum(jnp.where(onehot, values[None, :], 0), axis=1)

    offset = local_index - select_clip(clip_starts)
    height = jnp.maximum(select_clip(rows_of), 1)
    width_tiles = jnp.maximum(select_clip(cols_of), 1)
    frame_index = offset // (height * width_tiles)
    row_index = offset // width_tiles % height
    column = offset % width_tiles

    def within_one(coords):
        return jnp.abs(coords[:, None] - coords[None, :]) <= 1

    tile_mask = (
        (member[:, None] == member[None, :])
        & within_one(frame_index)
        & within_one(row_index)
        & within_one(column)
    )
    return (member.astype(jnp.int32), tile_mask)


def smem():
    return pl.BlockSpec(memory_space=pltpu.SMEM)


def vmem():
    return pl.BlockSpec(memory_space=pltpu.VMEM)


def pick_tiles(tokens, tile_owner, ids, groups, capacity):
    count = tokens.shape[0]

    def body(own_ref, ids_ref, tok_ref, *rest):
        outs, seen, index = rest[:groups], rest[groups], rest[groups + 1]
        for k in range(groups):
            seen[k] = 0
        for k in range(groups * capacity):
            index[k] = 0
        for i in range(count):
            k = lax.rem(own_ref[i] - ids_ref[0] + groups, groups)
            r = seen[k]
            seen[k] = r + 1
            index[k * capacity + r] = i
        for k in range(groups):
            for j in range(capacity):
                outs[k][j] = tok_ref[index[k * capacity + j]]

    shape = jax.ShapeDtypeStruct((capacity,) + tokens.shape[1:], tokens.dtype)
    return pl.pallas_call(
        body,
        out_shape=[shape] * groups,
        in_specs=[smem(), smem(), vmem()],
        out_specs=[vmem()] * groups,
        scratch_shapes=[
            pltpu.SMEM((groups,), jnp.int32),
            pltpu.SMEM((groups * capacity,), jnp.int32),
        ],
        name="pick_tiles",
    )(tile_owner, ids, tokens)


def norm_tiles(pieces, table, member, place, ids, groups):
    capacity, piece, width = pieces[0].shape
    tiles = TILES_OWN
    depth = width // groups

    def body(member_ref, place_ref, ids_ref, table_ref, *rest):
        ins, out_ref, held = rest[:groups], rest[groups], rest[groups + 1]
        for k in range(groups):
            source = lax.rem(ids_ref[1] - k + groups, groups)
            for j in range(capacity):
                held[place_ref[source * capacity + j]] = ins[k][j]

        def one(r, carry):
            values = held[r].astype(jnp.float32)
            center = jnp.mean(values, axis=-1, keepdims=True)
            values = values - center
            spread = jnp.mean(jnp.square(values), axis=-1, keepdims=True)
            values = values * lax.rsqrt(spread + eps_norm)
            rows = table_ref[member_ref[r]]
            done = (values * (1.0 + rows[1:2]) + rows[0:1]).astype(out_ref.dtype)
            at = pl.multiple_of(r * piece, piece)
            for g in range(groups):
                out_ref[g, pl.ds(at, piece), :] = done[:, g * depth : (g + 1) * depth]
            return carry

        lax.fori_loop(0, tiles, one, 0)

    return pl.pallas_call(
        body,
        out_shape=jax.ShapeDtypeStruct((groups, tiles * piece, depth), pieces[0].dtype),
        in_specs=[smem(), smem(), smem(), vmem()] + [vmem()] * groups,
        out_specs=vmem(),
        scratch_shapes=[pltpu.VMEM((tiles + 1, piece, width), pieces[0].dtype)],
        cost_estimate=pl.CostEstimate(
            flops=12 * tiles * piece * width,
            bytes_accessed=4 * tiles * piece * width,
            transcendentals=0,
        ),
        name="norm_tiles",
    )(member, place, ids, table, *pieces)


def project(xs, blocks, at, acc, sums):
    heads, depth, cols = blocks[0].shape
    sizes = [x.shape[1] for x in xs]
    total, m, n = sum(sizes), len(xs), len(blocks)

    def body(at_ref, *refs):
        x_refs, w_refs, rest = refs[: m * n], refs[m * n : (m + 1) * n], list(refs[(m + 1) * n :])
        acc_ref = rest.pop(0) if acc is not None else None
        out_ref = rest.pop(0)
        left = [jnp.concatenate([x_refs[i * n + j][0] for j in range(n)], axis=1) for i in range(m)]
        right = jnp.concatenate([ref[0] for ref in w_refs], axis=0)
        part = jnp.dot(jnp.concatenate(left, axis=0), right, preferred_element_type=jnp.float32)
        if acc is not None:
            part += acc_ref[0]
        out_ref[0] = part
        if sums:
            sums_ref, squares = rest
            head = pl.program_id(0)

            @pl.when(head == 0)
            def _():
                squares[...] = jnp.square(part)

            @pl.when(head > 0)
            def _():
                squares[...] += jnp.square(part)

            @pl.when(head == heads - 1)
            def _():
                lane = lax.broadcasted_iota(jnp.int32, (8, cols), 1)
                row = lax.broadcasted_iota(jnp.int32, (8, cols), 0)
                sums_ref[...] = lax.dot_general(
                    (lane // (cols // 2) == row).astype(jnp.float32),
                    squares[...],
                    (((1,), (1,)), ((), ())),
                    precision=lax.Precision.HIGHEST,
                    preferred_element_type=jnp.float32,
                )

    specs = [pl.BlockSpec((1, size, depth), lambda h, a, j=j: (a[j], 0, 0)) for size in sizes for j in range(n)]
    specs += [pl.BlockSpec((1, depth, cols), lambda h, a: (h, 0, 0))] * n
    args = [x for x in xs for _ in range(n)] + list(blocks)
    acc_spec = pl.BlockSpec((1, total, cols), lambda h, a: (h, 0, 0))
    aliases = {}
    if acc is not None:
        aliases = {1 + len(args): 0}
        specs.append(acc_spec)
        args.append(acc)
    out_shape = [jax.ShapeDtypeStruct((heads, total, cols), jnp.float32)]
    out_specs = [acc_spec]
    scratch = []
    if sums:
        out_shape.append(jax.ShapeDtypeStruct((8, total), jnp.float32))
        out_specs.append(pl.BlockSpec((8, total), lambda h, a: (0, 0)))
        scratch.append(pltpu.VMEM((total, cols), jnp.float32))
    return pl.pallas_call(
        body,
        out_shape=out_shape,
        grid_spec=pltpu.PrefetchScalarGridSpec(
            num_scalar_prefetch=1, grid=(heads,), in_specs=specs, out_specs=out_specs, scratch_shapes=scratch
        ),
        input_output_aliases=aliases,
        cost_estimate=pl.CostEstimate(
            flops=2 * n * total * depth * cols * heads,
            bytes_accessed=2 * n * (total + cols * heads) * depth + 8 * total * cols * heads,
            transcendentals=0,
        ),
        name="project",
    )(at, *args)


def soft_weights(qk, partial_sums, gains, bias, features, first, count):
    heads, total, cols = qk.shape
    dim = cols // 2
    n = len(partial_sums)
    rows = total // n
    extra = bias.shape[1]

    def body(*refs):
        q_ref, k_ref = refs[0], refs[1]
        sum_refs = refs[2 : 2 + n]
        qg_ref, kg_ref, bias_ref, out_ref, scales, keys = refs[2 + n :]
        head = pl.program_id(0)

        @pl.when(head == 0)
        def _():
            keys[:, dim:] = bias_ref[...]
            for p in range(n):
                whole = None
                for q in range(n):
                    there = (p // 2 - q // 2) % (n // 2) * 2 + (p % 2 ^ q % 2)
                    part = sum_refs[q][:, there * rows : (there + 1) * rows]
                    whole = part if whole is None else whole + part
                scales[p * rows : (p + 1) * rows] = jnp.transpose(lax.rsqrt(whole / features + eps_norm))

        keys[:, :dim] = (k_ref[0] * scales[:, 1:2] * kg_ref[pl.ds(first + head, 1), :]).astype(keys.dtype)
        lane = lax.broadcasted_iota(jnp.int32, (rows, extra), 1)
        row = lax.broadcasted_iota(jnp.int32, (rows, extra), 0)
        tile = (row // (rows // TILES_OWN) == lane).astype(keys.dtype)
        for p in range(n):
            here = slice(p * rows, (p + 1) * rows)
            query = q_ref[0, here] * scales[here, 0:1] * qg_ref[pl.ds(first + head, 1), :]
            scores = lax.dot_general(
                jnp.concatenate([query.astype(keys.dtype), tile], axis=1),
                keys[...],
                (((1,), (1,)), ((), ())),
                preferred_element_type=jnp.float32,
            )
            largest = jnp.max(scores, axis=-1, keepdims=True)
            powers = jnp.exp2((scores - largest) * (dim ** (-0.5) * log2_e))
            share = 1.0 / jnp.sum(powers, axis=-1, keepdims=True)
            out_ref[0, here] = (powers * share).astype(out_ref.dtype)

    whole_sum = pl.BlockSpec((8, total), lambda h: (0, 0))
    gain = pl.BlockSpec((heads, dim), lambda h: (0, 0))
    return pl.pallas_call(
        body,
        out_shape=jax.ShapeDtypeStruct((count, total, total), jnp.bfloat16),
        grid=(count,),
        in_specs=[
            pl.BlockSpec((1, total, dim), lambda h: (first + h, 0, 0)),
            pl.BlockSpec((1, total, dim), lambda h: (first + h, 0, 1)),
        ]
        + [whole_sum] * n
        + [gain, gain, pl.BlockSpec(bias.shape, lambda h: (0, 0))],
        out_specs=pl.BlockSpec((1, total, total), lambda h: (h, 0, 0)),
        scratch_shapes=[pltpu.VMEM((total, 8), jnp.float32), pltpu.VMEM((total, dim + extra), jnp.bfloat16)],
        cost_estimate=pl.CostEstimate(
            flops=(2 * dim + 8) * count * total * total,
            bytes_accessed=count * total * (2 * total + 4 * cols),
            transcendentals=count * total * total,
        ),
        name="soft_weights",
    )(qk, qk, *partial_sums, *gains, bias)


def mix_values(weights, values, xs, blocks, extra, at, order, place, groups, capacity, piece):
    parts, (count, total, _) = len(weights), weights[0].shape
    heads = parts * count
    packed, _, cols = values.shape
    depth = blocks[0].shape[1]
    dim = packed * cols // heads
    share = heads // packed
    n = order.shape[0]
    rows = total // n
    sizes = [x.shape[1] for x in xs]
    m, k = len(xs), len(blocks)
    full = groups * capacity == TILES_OWN

    def body(order_ref, place_ref, at_ref, *refs):
        weight_refs, x_refs, refs = refs[:parts], refs[parts : parts + m * k], refs[parts + m * k :]
        w_refs, e_refs, refs = refs[:k], refs[k : k + len(extra)], refs[k + len(extra) :]
        acc_ref, out_ref, held, *staged = refs
        head = pl.program_id(0)

        @pl.when(head % share == 0)
        def _():
            left = [jnp.concatenate([x_refs[i * k + j][0] for j in range(k)], axis=1) for i in range(m)]
            sides = [ref[0] for ref in w_refs]
            if extra:
                sides = [side + ref[0] for side, ref in zip(sides, e_refs)]
            right = jnp.concatenate(sides, axis=0)
            done = acc_ref[0] + jnp.dot(jnp.concatenate(left, axis=0), right, preferred_element_type=jnp.float32)
            for i in range(share):
                held[i] = done[:, i * dim : (i + 1) * dim].astype(held.dtype)

        for i in range(parts):

            @pl.when(head // count == i)
            def _(weight_ref=weight_refs[i]):
                mixed = jnp.dot(weight_ref[0], held[head % share], preferred_element_type=jnp.float32)
                for p in range(n):
                    block = mixed[p * rows : (p + 1) * rows]
                    if full:
                        out_ref[:, order_ref[p]] = block.astype(out_ref.dtype).reshape(groups, capacity * piece, dim)
                        continue
                    staged[0][...] = block
                    for slot in range(groups * capacity):
                        tile = jnp.minimum(place_ref[slot], TILES_OWN - 1)
                        tile_rows = staged[0][pl.ds(pl.multiple_of(tile * piece, piece), piece), :]
                        to = slot % capacity * piece
                        out_ref[slot // capacity, order_ref[p], to : to + piece] = tile_rows.astype(out_ref.dtype)

    def weight_block(i):
        return pl.BlockSpec((1, total, total), lambda h, o, s, a: (jnp.clip(h - i * count, 0, count - 1), 0, 0))

    return pl.pallas_call(
        body,
        out_shape=jax.ShapeDtypeStruct((groups, n, capacity * piece, heads * dim), jnp.bfloat16),
        grid_spec=pltpu.PrefetchScalarGridSpec(
            num_scalar_prefetch=3,
            grid=(heads,),
            in_specs=[weight_block(i) for i in range(parts)]
            + [pl.BlockSpec((1, size, depth), lambda h, o, s, a, j=j: (a[j], 0, 0)) for size in sizes for j in range(k)]
            + [pl.BlockSpec((1, depth, cols), lambda h, o, s, a: (h // share, 0, 0))] * (k + len(extra))
            + [pl.BlockSpec((1, total, cols), lambda h, o, s, a: (h // share, 0, 0))],
            out_specs=pl.BlockSpec((groups, n, capacity * piece, dim), lambda h, o, s, a: (0, 0, 0, h)),
            scratch_shapes=[pltpu.VMEM((share, total, dim), jnp.bfloat16)]
            + [pltpu.VMEM((rows, dim), jnp.float32)] * (not full),
        ),
        cost_estimate=pl.CostEstimate(
            flops=2 * heads * total * (total + k * depth) * dim,
            bytes_accessed=heads * total * (2 * total + 6 * dim),
            transcendentals=0,
        ),
        name="mix_values",
    )(order, place, at, *weights, *[x for x in xs for _ in range(k)], *blocks, *extra, values)


def place_tiles(returned, tile_owner, groups, n, capacity):
    _, rows, width = returned.shape
    piece = rows // capacity
    count = tile_owner.shape[0]

    def body(own_ref, in_ref, out_ref, seen):
        for k in range(groups):
            seen[k] = 0
        for i in range(count):
            owner = own_ref[i]
            rank = seen[owner]
            seen[owner] = rank + 1
            at = pl.multiple_of(rank * piece, piece)
            for g in range(n):
                source = (owner // 2 * 2 + g % 2) * n + g // 2 * 2 + lax.rem(owner, 2)
                out_ref[i, :, g * width : (g + 1) * width] = in_ref[source, pl.ds(at, piece), :]

    return pl.pallas_call(
        body,
        out_shape=jax.ShapeDtypeStruct((count, piece, n * width), returned.dtype),
        in_specs=[smem(), vmem()],
        out_specs=vmem(),
        scratch_shapes=[pltpu.SMEM((groups,), jnp.int32)],
        name="place_tiles",
    )(tile_owner, returned)


def transposed(tokens, w_qkv, q_gain, k_gain, modulation, tile_owner, clip_dims):
    groups, n = lax.axis_size("bal"), lax.axis_size("seq")
    planes, lines = groups // 2, n // 2
    owned_tiles, piece, _ = tokens.shape
    capacity = owned_tiles // min(groups, owned_tiles)
    heads, dim = q_gain.shape
    features = heads * n * dim

    def send(value, to):
        pairs = []
        for b in range(groups):
            for s in range(n):
                z, x, y, c = to(b // 2, b % 2, s // 2, s % 2)
                pairs.append((b * n + s, (z * 2 + x) * n + y * 2 + c))
        return lax.ppermute(value, AXES, pairs)

    def swap(value):
        return send(value, lambda z, x, y, c: (z, c, y, x))

    def ring(value):
        return send(value, lambda z, x, y, c: ((z + 1) % planes, x, y, c))

    def other_core(value):
        return send(value, lambda z, x, y, c: (z, x, y, 1 - c))

    def after(value, *others):
        return lax.optimization_barrier((value, *others))[0]

    bal, seq = lax.axis_index("bal"), lax.axis_index("seq")
    z, x, y, c = bal // 2, bal % 2, seq // 2, seq % 2
    ids = jnp.stack([bal, z * 2 + c]).astype(jnp.int32)

    outgoing = pick_tiles(tokens, tile_owner, ids, groups, capacity)

    by_head = after(jnp.transpose(w_qkv, (1, 0, 2)), outgoing[0])
    pair = 2 if heads % 2 == 0 else 1
    v_columns = by_head[:, :, 2 * dim :]
    v_columns = jnp.concatenate([v_columns[i::pair] for i in range(pair)], axis=2)
    qk_own = [swap(by_head[:, :, : 2 * dim])]

    def to_owner(k):
        def to(z, x, y, c):
            owner = (z * 2 + x + k) % groups
            return owner // 2, c, y, owner % 2

        return to

    arrived = []
    for k in range(groups):
        arrived.append(send(outgoing[k], to_owner(k)))
    table = swap(after(modulation[0], outgoing[0]))
    clips = swap(after(clip_dims[0], outgoing[0]))
    gains = (swap(q_gain), swap(k_gain))
    member, tile_mask = tile_layout(clips)
    if groups * capacity == TILES_OWN:
        place = jnp.arange(TILES_OWN, dtype=jnp.int32)
    else:
        named = lax.all_gather(tile_owner, "bal", axis=0) == ids[1]
        live = jnp.arange(capacity)[None, :] < jnp.sum(named, axis=1, dtype=jnp.int32)[:, None]
        live = live.reshape(-1)
        place = jnp.where(live, jnp.cumsum(live.astype(jnp.int32)) - 1, TILES_OWN).astype(jnp.int32)
    gated = jnp.maximum(lax.optimization_barrier(member), 0)
    normed = norm_tiles(arrived, table, gated, place, ids, groups)

    def along_x(value):
        return send(value, lambda z, x, y, c: (z, x ^ 1, y, c))

    def along_y(value, py):
        return send(value, lambda z, x, y, c: (z, x, (y - py) % lines, c))

    across = along_x(normed)
    pieces = [normed, across]
    order = [y * 2 + x, y * 2 + (x ^ 1)]
    half = normed.shape[1] // 2
    for py in range(1, lines):
        beside = along_y(normed, py)
        corner = [along_x(beside[:, :half]), along_y(across[:, half:], py)]
        pieces += [beside, *corner]
        order += [(y + py) % lines * 2 + x, (y + py) % lines * 2 + (x ^ 1)]
    order = jnp.stack(order).astype(jnp.int32)

    def near_planes(own):
        if planes == 4:
            return [own, send(own, lambda z, x, y, c: (z ^ 1, x, y, c))]
        got = [own]
        for _ in range(planes - 2):
            got.append(ring(got[-1]))
        return got

    def send_some(value, hops):
        pairs = []
        for b in range(groups):
            for s in range(n):
                if b // 2 in hops:
                    pairs.append((b * n + s, (hops[b // 2] * 2 + b % 2) * n + s))
        return lax.ppermute(value, AXES, pairs)

    def cross(value):
        return send_some(value, {1: 2, 2: 1})

    def outward(value):
        return send_some(value, {1: 0, 2: 3})

    def plane_at(step):
        if planes != 4:
            return (z - step) % planes
        low = z < 2
        return [z, z ^ 1, jnp.where(low, 2, 1), jnp.where(low, 3, 0)][step]

    def blocks_of(own, steps):
        blocks, at = [], []
        for step in steps:
            blocks += [own[step], other_core(own[step])]
            at += [plane_at(step) * 2 + c, plane_at(step) * 2 + 1 - c]
        return blocks, jnp.stack(at).astype(jnp.int32)

    qk_own = near_planes(qk_own[0])
    v_first = swap(v_columns)
    v_own = near_planes(after(v_first, *arrived))
    if planes == 4:
        crossed = cross(after(qk_own[0], *arrived))
        crossed_next = cross(after(qk_own[1], crossed))
        qk_own.append(crossed + outward(crossed))
        passed = outward(crossed_next)
        v_crossed = cross(after(v_own[0], crossed_next))
        v_crossed_next = cross(after(v_own[1], crossed_next))
        v_passed = [outward(after(v_crossed, passed)), outward(after(v_crossed_next, passed))]

    blocks, at = blocks_of(qk_own, range(planes - 1))
    qk, *_ = project(pieces, blocks, at, None, False)
    split = max(planes - 2, 1)
    blocks, at = blocks_of(v_own, range(split))
    blocks[0] = after(blocks[0], qk)
    values, *_ = project(pieces, blocks, at, None, False)
    qk_own.append(after(crossed_next, values) + passed if planes == 4 else ring(after(qk_own[-1], values)))
    blocks, at = blocks_of(qk_own, [planes - 1])
    qk, sums = project(pieces, blocks, at, qk, True)
    partial_sums = [sums]
    partial_sums.append(along_x(sums))
    for py in range(1, lines):
        partial_sums.append(along_y(sums, py))
        partial_sums.append(send(sums, lambda z, x, y, c: (z, x ^ 1, (y - py) % lines, c)))

    bias = jnp.where(tile_mask.T, 0.0, mask_bias).astype(jnp.bfloat16)
    bias = jnp.pad(bias, ((0, 0), (0, dim - TILES_OWN)))
    bias = jnp.tile(jnp.repeat(bias, piece, axis=0), (n, 1))
    weights = [soft_weights(qk, partial_sums, gains, after(bias, values), features, 0, heads)]
    extra = []
    if planes == 4:
        v_own += [v_crossed, v_crossed_next]
        for passed in v_passed:
            passed = after(passed, weights[0])
            extra += [passed, other_core(passed)]
    else:
        v_own.append(ring(after(v_own[-1], sums)))
    blocks, at = blocks_of(v_own, range(split, planes))
    mixed = mix_values(weights, values, pieces, blocks, extra, at, order, place, groups, capacity, piece)
    returned = lax.all_to_all(
        mixed.reshape(groups * n, capacity * piece, heads * dim), AXES, split_axis=0, concat_axis=0, tiled=True
    )
    return place_tiles(returned, tile_owner, groups, n, capacity)


def solution(mesh):
    return jax.shard_map(
        transposed,
        mesh=mesh,
        in_specs=(
            P("bal", "seq", None),
            P("bal", "seq", None),
            P("seq", None),
            P("seq", None),
            P("bal", None, None, None),
            P("bal"),
            P("bal", None, None),
        ),
        out_specs=P("bal", "seq", None),
        check_vma=False,
    )
```
